32 devices in a mesh: dp: 8 (over z, y), tensor: 4 (over x, core).
Axes of the slice: x: 2, y: 2, z: 4, core: 2. Of those that a mesh axis runs over, the one named last changes fastest.
Arguments:
- tokens: bfloat16 [16384, 1536], P(('dp', 'tensor')), may hold values from -6 to 6
- segments: int32 [16384], P('dp'), may hold values from 0 to 3, as said below
- positions: int32 [16384], P('dp'), may hold values from 0 to 2044, as said below
- norm_attn: float32 [1536], replicated, may hold values from 0.1 to 1.9
- w_query: bfloat16 [1536, 1536], P(None, 'tensor'), may hold values from -0.15625 to 0.15625
- key_weight: bfloat16 [1536, 768], P(None, 'tensor'), may hold values from -0.15625 to 0.15625
- value_weight: bfloat16 [1536, 768], P(None, 'tensor'), may hold values from -0.15625 to 0.15625
- w_out: bfloat16 [1536, 1536], P('tensor'), may hold values from -1.5 to 1.5
- norm_mlp: float32 [1536], replicated, may hold values from 0.1 to 1.9
- w_gate: bfloat16 [1536, 4096], P(None, 'tensor'), may hold values from -0.15625 to 0.15625
- w_up: bfloat16 [1536, 4096], P(None, 'tensor'), may hold values from -0.15625 to 0.15625
- w_down: bfloat16 [4096, 1536], P('tensor'), may hold values from -0.09375 to 0.09375
- cotangent: bfloat16 [16384, 1536], P(('dp', 'tensor')), may hold values from -6 to 6
Outputs:
- output: bfloat16 [16384, 1536], P(('dp', 'tensor'))
- grad_tokens: float32 [16384, 1536], P(('dp', 'tensor'))
- grad_norm_attn: float32 [1536], replicated
- grad_w_query: float32 [1536, 1536], P(None, 'tensor')
- grad_w_key: float32 [1536, 768], P(None, 'tensor')
- grad_w_value: float32 [1536, 768], P(None, 'tensor')
- grad_w_out: float32 [1536, 1536], P('tensor')
- grad_norm_mlp: float32 [1536], replicated
- grad_w_gate: float32 [1536, 4096], P(None, 'tensor')
- grad_w_up: float32 [1536, 4096], P(None, 'tensor')
- grad_w_down: float32 [4096, 1536], P('tensor')
The draws below stay inside these ranges and needn't reach their ends.
Inputs may be any that keep to these rules, and one draw needn't show every extreme that they name: `segments`: within each sequence of 2048 tokens the document numbers never fall, start at 0 and end at 3, each document one token or more. `positions`: each token's position within its document, 0 at the document's first token; the first sequence holds a document of 2045 tokens.
All inputs are finite; a program needn't handle non-finite values.
Results may differ from the reference program's by a relative error of at most 0.018.
Values may be sent and summed in bfloat16 or wider, within the bound.
A program may use at most 256 MiB of HBM per device.

```python
import math
import jax
import jax.numpy as jnp
from jax import lax

MODEL_WIDTH = 1536
QUERY_HEADS = 16
VALUE_HEADS = 8
HEAD_SIZE = 96
FF = 4096
SEQ_LEN = 2048
DOCS = 4
TOKENS = 16384


def doc_layout(key):
    row_total = TOKENS // SEQ_LEN
    base_key = jax.random.fold_in(key, 7)

    def one_row(row_key, row_number):
        order = jax.random.permutation(row_key, SEQ_LEN - 1) + 1
        random_cuts = jnp.sort(order[:DOCS - 1])
        tail_cuts = (SEQ_LEN - DOCS + 1 + jnp.arange(DOCS - 1)).astype(random_cuts.dtype)
        cut_points = jnp.where(row_number == 0, tail_cuts, random_cuts)
        indices = jnp.arange(SEQ_LEN, dtype=jnp.int32)
        after_cut = indices[:, None] >= cut_points[None, :]
        segment_ids = jnp.sum(after_cut.astype(jnp.int32), axis=1)
        doc_start = jnp.max(jnp.where(after_cut, cut_points[None, :], 0), axis=1, initial=0)
        return (segment_ids, indices - doc_start)
    row_keys = jax.random.split(base_key, row_total)
    row_numbers = jnp.arange(row_total, dtype=jnp.int32)
    segment_ids, places = jax.vmap(one_row)(row_keys, row_numbers)
    return (segment_ids.reshape(-1).astype(jnp.int32), places.reshape(-1).astype(jnp.int32))


def draw_segments(key, part):
    return doc_layout(key)[0]


def draw_positions(key, part):
    return doc_layout(key)[1]


def steps_of(own_key, dims, cuts, low, top_value):
    level = 1.0
    for position, parts in cuts:
        draws = jax.random.uniform(jax.random.fold_in(jax.random.fold_in(own_key, 6), position), (parts,), jnp.float32, low / len(cuts), top_value / len(cuts))
        level = level * jnp.repeat(jnp.exp(draws), dims[position] // parts).reshape((-1,) + (1,) * (len(dims) - 1 - position))
    return level


def centred(key, dims, spread, limit, pieces=(), held_as=jnp.bfloat16):
    entries = spread * jax.random.normal(key, dims, jnp.float32)
    if pieces:
        entries = entries * steps_of(key, dims, pieces, -0.22, 0.18)
    return jnp.clip(entries, -limit, limit).astype(held_as)


def setup_inputs(seed: int = 0) -> dict:
    splits = jax.random.split(jax.random.key(seed), 14)
    tokens = centred(splits[0], (TOKENS, MODEL_WIDTH), 1.0, 6.0, ((0, 32),))
    segments = draw_segments(jax.random.fold_in(splits[13], 71), 0)
    positions = draw_positions(jax.random.fold_in(splits[13], 71), 0)
    norm_attn = jnp.clip(1.0 + 0.18 * jax.random.normal(splits[3], (MODEL_WIDTH,), jnp.float32), 0.1, 1.9)
    w_query = centred(splits[4], (MODEL_WIDTH, QUERY_HEADS * HEAD_SIZE), MODEL_WIDTH ** -0.5, 0.15625, ((1, 4),))
    key_weight = centred(splits[5], (MODEL_WIDTH, VALUE_HEADS * HEAD_SIZE), MODEL_WIDTH ** -0.5, 0.15625, ((1, 4),))
    value_weight = centred(splits[6], (MODEL_WIDTH, VALUE_HEADS * HEAD_SIZE), MODEL_WIDTH ** -0.5, 0.15625, ((1, 4),))
    w_out = centred(splits[7], (QUERY_HEADS * HEAD_SIZE, MODEL_WIDTH), QUERY_HEADS ** -0.5, 1.5, ((0, 4),))
    norm_mlp = jnp.clip(1.0 + 0.18 * jax.random.normal(splits[8], (MODEL_WIDTH,), jnp.float32), 0.1, 1.9)
    w_gate = centred(splits[9], (MODEL_WIDTH, FF), MODEL_WIDTH ** -0.5, 0.15625, ((1, 4),))
    w_up = centred(splits[10], (MODEL_WIDTH, FF), MODEL_WIDTH ** -0.5, 0.15625, ((1, 4),))
    w_down = centred(splits[11], (FF, MODEL_WIDTH), FF ** -0.5, 0.09375, ((0, 4),))
    cotangent = centred(splits[12], (TOKENS, MODEL_WIDTH), 1.0, 6.0, ((0, 32),))
    return dict(tokens=tokens, segments=segments, positions=positions, norm_attn=norm_attn, w_query=w_query, key_weight=key_weight, value_weight=value_weight, w_out=w_out, norm_mlp=norm_mlp, w_gate=w_gate, w_up=w_up, w_down=w_down, cotangent=cotangent)


epsilon = 1e-05
rope_base = 100000.0
masked_value = -1e+30

@jax.custom_vjp
def lowered_precision(v):
    return lax.optimization_barrier(v.astype(jnp.bfloat16)).astype(jnp.float32)

@jax.custom_vjp
def lowered_backward(v):
    return v

def low_keep(v):
    return (lowered_precision(v), None)

def low_pass(kept, grad):
    return (grad,)

def back_keep(v):
    return (v, None)

def back_low(kept, grad):
    return (lowered_precision(grad),)
lowered_precision.defvjp(low_keep, low_pass)
lowered_backward.defvjp(back_keep, back_low)

def product_accurate(left, right):
    return jnp.dot(left, right, precision=lax.Precision.HIGHEST)

def angle_tables(positions, width):
    middle = width // 2
    freq_steps = jnp.arange(middle, dtype=jnp.float32)
    inverse = jnp.exp(freq_steps * (-2.0 * math.log(rope_base) / width))
    angles = positions.astype(jnp.float32)[:, None] * inverse[None, :]
    return (jnp.cos(angles)[:, None, :], jnp.sin(angles)[:, None, :])

def apply_rotary(values, cosine_lookup, sine_lookup):
    middle = values.shape[-1] // 2
    front, second = (values[..., :middle], values[..., middle:])
    return jnp.concatenate([front * cosine_lookup - second * sine_lookup, second * cosine_lookup + front * sine_lookup], axis=-1)

def attend_block(query_block, rows_seg, rows_idx, heads_of_key, heads_of_value, segments, indices):
    allowed = (rows_seg[:, None] == segments[None, :]) & (indices[None, :] <= rows_idx[:, None])
    scores = jnp.einsum('qgrd,kgd->grqk', query_block, heads_of_key, precision=lax.Precision.HIGHEST) * (1.0 / math.sqrt(HEAD_SIZE))
    scores = lowered_backward(scores)
    scores = jnp.where(allowed[None, None], scores, masked_value)
    row_peak = lax.optimization_barrier(jnp.max(scores, axis=-1, keepdims=True))
    weights = jnp.exp(scores - row_peak)
    weights_low = lowered_precision(weights / lax.optimization_barrier(jnp.sum(weights, axis=-1, keepdims=True)))
    return jnp.einsum('grqk,kgd->qgrd', weights_low, heads_of_value, precision=lax.Precision.HIGHEST)
checked_block = jax.checkpoint(attend_block)

def layer(inputs, norm_attn, w_query, key_weight, value_weight, w_out, norm_mlp, w_gate, w_up, w_down, segments, cosine_lookup, sine_lookup):
    sequence_length = inputs.shape[0]
    rows_per_block = min(512, sequence_length)
    block_total = sequence_length // rows_per_block
    head_repetitions = QUERY_HEADS // VALUE_HEADS
    indices = jnp.arange(sequence_length, dtype=jnp.int32)
    unit_one = inputs * lax.rsqrt(lax.optimization_barrier(jnp.mean(inputs * inputs, axis=-1, keepdims=True)) + epsilon)
    first_normalized = lowered_precision(unit_one * norm_attn)
    query_rows = lowered_precision(apply_rotary(lowered_backward(product_accurate(first_normalized, w_query)).reshape(sequence_length, QUERY_HEADS, HEAD_SIZE), cosine_lookup, sine_lookup))
    heads_of_key = lowered_precision(apply_rotary(lowered_backward(product_accurate(first_normalized, key_weight)).reshape(sequence_length, VALUE_HEADS, HEAD_SIZE), cosine_lookup, sine_lookup))
    heads_of_value = lowered_precision(lowered_backward(product_accurate(first_normalized, value_weight))).reshape(sequence_length, VALUE_HEADS, HEAD_SIZE)
    blocks_of_query = query_rows.reshape(block_total, rows_per_block, VALUE_HEADS, head_repetitions, HEAD_SIZE)
    seg_blocks = segments.reshape(block_total, rows_per_block)
    index_blocks = indices.reshape(block_total, rows_per_block)

    def one_block(member):
        return checked_block(member[0], member[1], member[2], heads_of_key, heads_of_value, segments, indices)
    mixed_heads = lax.map(one_block, (blocks_of_query, seg_blocks, index_blocks))
    attended = lowered_precision(lowered_backward(mixed_heads.reshape(sequence_length, QUERY_HEADS * HEAD_SIZE)))
    hidden_one = inputs + lowered_backward(product_accurate(attended, w_out))
    unit_two = hidden_one * lax.rsqrt(lax.optimization_barrier(jnp.mean(hidden_one * hidden_one, axis=-1, keepdims=True)) + epsilon)
    normed_two = lowered_precision(unit_two * norm_mlp)
    gate_proj = lowered_backward(product_accurate(normed_two, w_gate))
    up_proj = lowered_backward(product_accurate(normed_two, w_up))
    hidden = lowered_precision(jax.nn.silu(gate_proj) * up_proj)
    return hidden_one + product_accurate(hidden, w_down)

def reference(tokens, segments, positions, norm_attn, w_query, key_weight, value_weight, w_out, norm_mlp, w_gate, w_up, w_down, cotangent):
    seq_total = TOKENS // SEQ_LEN
    params = (norm_attn.astype(jnp.float32), w_query.astype(jnp.float32), key_weight.astype(jnp.float32), value_weight.astype(jnp.float32), w_out.astype(jnp.float32), norm_mlp.astype(jnp.float32), w_gate.astype(jnp.float32), w_up.astype(jnp.float32), w_down.astype(jnp.float32))
    seq_tokens = tokens.astype(jnp.float32).reshape(seq_total, SEQ_LEN, MODEL_WIDTH)
    seq_grads = cotangent.astype(jnp.float32).reshape(seq_total, SEQ_LEN, MODEL_WIDTH)
    seq_segments = segments.reshape(seq_total, SEQ_LEN)
    seq_places = positions.reshape(seq_total, SEQ_LEN)

    def one_sequence(running, member):
        inputs, grads_in, segs_here, places_here = member
        cosine_lookup, sine_lookup = angle_tables(places_here, HEAD_SIZE)

        def forward(inputs_now, *weights):
            return layer(inputs_now, *weights, segs_here, cosine_lookup, sine_lookup)
        result, pullback = jax.vjp(forward, inputs, *params)
        pulled = pullback(grads_in)
        running = tuple((before + gradient for before, gradient in zip(running, pulled[1:])))
        return (running, (result.astype(jnp.bfloat16), pulled[0]))
    starts = tuple((jnp.zeros_like(weight) for weight in params))
    running, (outputs, grad_rows) = lax.scan(one_sequence, starts, (seq_tokens, seq_grads, seq_segments, seq_places))
    return (outputs.reshape(TOKENS, MODEL_WIDTH), grad_rows.reshape(TOKENS, MODEL_WIDTH), running[0], running[1], running[2], running[3], running[4], running[5], running[6], running[7], running[8])
```

```python
import functools
import math

import jax
import jax.numpy as jnp
from jax import lax
from jax.experimental import pallas as pl
from jax.experimental.pallas import tpu as pltpu
from jax.sharding import PartitionSpec as P

HEAD_SIZE = 96
HALF = HEAD_SIZE // 2
LANES = 128
epsilon = 1e-05
rope_base = 100000.0
masked_value = -1e30
score_scale = 1.0 / math.sqrt(HEAD_SIZE)
log2_e = math.log2(math.e)
bf16, f32 = jnp.bfloat16, jnp.float32
NN = (((1,), (0,)), ((), ()))
NT = (((1,), (1,)), ((), ()))
TN = (((0,), (0,)), ((), ()))
VMEM_LIMIT = 62 * 1024 * 1024
CHUNKS = 2


def dot(left, right, dims=NN):
    return lax.dot_general(left, right, dims, preferred_element_type=f32)


def params():
    return pltpu.CompilerParams(vmem_limit_bytes=VMEM_LIMIT)


def cost(flops, nbytes):
    return pl.CostEstimate(flops=int(flops), bytes_accessed=int(nbytes), transcendentals=0)


def whole(shape):
    return pl.BlockSpec(shape, lambda *_: (0,) * len(shape), pipeline_mode=pl.Buffered(1))


def swap(values, bits):
    size = lax.axis_size("tensor")
    return lax.ppermute(values, "tensor", [(i, i ^ bits) for i in range(size)])


def gather_four(own):
    side = swap(own, 1)
    across = swap(own, 2)
    return own, side, across, swap(across, 1)


def scatter_sum(part):
    from_side_2 = swap(part[3], 1)
    travelling = (part[2].astype(f32) + from_side_2.astype(f32)).astype(bf16)
    from_across = swap(travelling, 2)
    from_side_0 = swap(part[1], 1)
    return part[0], from_side_0, from_across


def dp_swap(values, bits):
    size = lax.axis_size("dp")
    return lax.ppermute(values, "dp", [(i, i ^ bits) for i in range(size)])


def dp_sum(values):
    size, index = lax.axis_size("dp"), lax.axis_index("dp")
    rows = values.shape[0]
    piece = values
    bit = 1
    while bit < size:
        half = piece.shape[0] // 2
        mine = (index // bit) % 2
        send = lax.dynamic_slice_in_dim(piece, (1 - mine) * half, half, 0)
        keep = lax.dynamic_slice_in_dim(piece, mine * half, half, 0)
        got = dp_swap(send, bit)
        piece = (keep.astype(f32) + got.astype(f32)).astype(bf16)
        bit *= 2
    while bit > 1:
        bit //= 2
        mine = (index // bit) % 2
        got = dp_swap(piece, bit)
        piece = jnp.where(mine == 0, jnp.concatenate([piece, got], 0), jnp.concatenate([got, piece], 0))
    return piece.astype(f32)


def all_sum(values):
    bit = 1
    while bit < lax.axis_size("tensor"):
        values = values + swap(values, bit)
        bit *= 2
    bit = 1
    while bit < lax.axis_size("dp"):
        values = values + dp_swap(values, bit)
        bit *= 2
    return values


def qkv_kernel(count, *refs):
    xs, (wq, wk, wv, cos_ref, sin_ref), rest = refs[:count], refs[count : count + 5], refs[count + 5 :]
    qkv_ref, stack_ref = rest[-2:]
    for k in range(count):

        @pl.when(pl.program_id(0) == k)
        def _():
            x = xs[k][...]
            cos, sin = cos_ref[0, 0], sin_ref[0, 0]
            stack_ref[0, 0] = x
            rows = x.shape[0]
            lane = lax.broadcasted_iota(jnp.int32, (rows, LANES), 1)
            for w, base, turn in ((wq, 0, True), (wk, 4, True), (wv, 6, False)):
                y = dot(x, w[...])
                for h in range(w.shape[1] // LANES):
                    v = y[:, h * LANES : (h + 1) * LANES]
                    if turn:
                        v = v * cos + pltpu.roll(v, LANES // 2, 1) * sin
                    else:
                        v = jnp.where(lane == HALF, 1.0, v)
                    at = (base + h) * LANES
                    qkv_ref[0, 0, :, at : at + LANES] = v.astype(bf16)


def qkv_call(first, piece, pieces, xs, wq, wk, wv, cos, sin, before):
    count = len(xs)
    rows, width = xs[0].shape
    spec = lambda cols: pl.BlockSpec((1, 1, rows, cols), lambda k: (first + k, piece, 0, 0))
    aliased = before is not None
    inputs = [*xs, wq, wk, wv, cos, sin]
    specs = [whole((rows, width))] * count + [whole(w.shape) for w in (wq, wk, wv)] + [spec(LANES)] * 2
    aliases = {}
    if aliased:
        aliases = {len(inputs): 0, len(inputs) + 1: 1}
        inputs += list(before)
        specs += [pl.BlockSpec(memory_space=pl.ANY)] * 2
    return pl.pallas_call(
        functools.partial(qkv_kernel, count),
        grid=(count,),
        in_specs=specs,
        out_specs=[spec(8 * LANES), spec(width)],
        out_shape=[
            jax.ShapeDtypeStruct((4, pieces, rows, 8 * LANES), bf16),
            jax.ShapeDtypeStruct((4, pieces, rows, width), bf16),
        ],
        input_output_aliases=aliases,
        compiler_params=params(),
        cost_estimate=cost(2 * count * rows * width * 8 * LANES, 2 * width * 8 * LANES + count * rows * width * 6),
        name="project_qkv",
    )(*inputs)


def attend_kernel(me_ref, q_ref, k_ref, v_ref, start_ref, o_ref, lse_ref, *, blocks, size):
    me = me_ref[0]
    for i in range(blocks):
        at = pl.multiple_of((i ^ me) * size, size)
        queries = [q_ref[pl.ds(at, size), r * LANES : (r + 1) * LANES] for r in range(2)]
        start = start_ref[:, pl.ds(at, size)]
        state = [None, None]
        for j in [i, *range(i)]:
            key_at = pl.multiple_of((j ^ me) * size, size)
            keys = k_ref[pl.ds(key_at, size), :]
            values = v_ref[pl.ds(key_at, size), :]
            key_rows = lax.broadcasted_iota(jnp.int32, (size, size), 0)
            allowed = key_rows >= start - j * size
            if j == i:
                allowed &= key_rows <= lax.broadcasted_iota(jnp.int32, (size, size), 1)
            for r in range(2):
                scores = jnp.where(allowed, dot(keys, queries[r], NT) * (score_scale * log2_e), masked_value)
                peak = jnp.max(scores, axis=0, keepdims=True)
                if state[r] is not None:
                    peak = jnp.maximum(state[r][0], peak)
                weights = jnp.exp2(scores - peak)
                mixed = dot(values, weights.astype(bf16), TN)
                if state[r] is not None:
                    mixed += state[r][1] * jnp.exp2(state[r][0] - peak)
                state[r] = (peak, mixed)
        for r, (peak, mixed) in enumerate(state):
            total = mixed[HALF : HALF + 1, :]
            o_ref[pl.ds(at, size), r * LANES : (r + 1) * LANES] = (mixed / total).T.astype(bf16)
            lse_ref[0, r : r + 1, pl.ds(at, size)] = peak + jnp.log2(total)


def attend(me, qkv, start, blocks):
    seq = qkv.shape[0]
    flops = 2 * 2 * 4 * LANES * seq * seq
    return pl.pallas_call(
        functools.partial(attend_kernel, blocks=blocks, size=seq // blocks),
        grid_spec=pltpu.PrefetchScalarGridSpec(
            num_scalar_prefetch=1,
            grid=(2,),
            in_specs=[
                pl.BlockSpec((seq, 2 * LANES), lambda g, _: (0, g)),
                pl.BlockSpec((seq, LANES), lambda g, _: (0, 4 + g)),
                pl.BlockSpec((seq, LANES), lambda g, _: (0, 6 + g)),
                pl.BlockSpec((1, seq), lambda g, _: (0, 0)),
            ],
            out_specs=[
                pl.BlockSpec((seq, 2 * LANES), lambda g, _: (0, g)),
                pl.BlockSpec((1, 2, seq), lambda g, _: (g, 0, 0)),
            ],
        ),
        out_shape=[jax.ShapeDtypeStruct((seq, 4 * LANES), bf16), jax.ShapeDtypeStruct((2, 2, seq), f32)],
        compiler_params=params(),
        cost_estimate=cost(flops, 6 * seq * 8 * LANES),
        name="attention",
    )(me, qkv, qkv, qkv, start)


def attend_back_kernel(
    me_ref, q_ref, k_ref, v_ref, o_ref, do_ref, lse_ref, start_ref, cos_ref, sin_ref,
    dq_ref, dk_ref, dv_ref, dq_sum, dk_sum, dv_sum, inner, *, blocks, size,
):
    me = me_ref[0]
    for c in range(blocks):
        rows = slice(c * size, (c + 1) * size)
        for r in range(2):
            cols = slice(r * LANES, (r + 1) * LANES)
            product = do_ref[rows, cols].astype(f32) * o_ref[rows, cols].astype(f32)
            inner[r : r + 1, rows] = jnp.sum(product.T, axis=0, keepdims=True)
    for i in reversed(range(blocks)):
        for j in [i, *range(i)]:
            at = pl.multiple_of((i ^ me) * size, size)
            key_at = pl.multiple_of((j ^ me) * size, size)
            keys = k_ref[pl.ds(key_at, size), :]
            values = v_ref[pl.ds(key_at, size), :]
            start = start_ref[:, pl.ds(at, size)]
            key_rows = lax.broadcasted_iota(jnp.int32, (size, size), 0)
            allowed = key_rows >= start - j * size
            if j == i:
                allowed &= key_rows <= lax.broadcasted_iota(jnp.int32, (size, size), 1)
            dk = dv = None
            for r in range(2):
                cols = slice(r * LANES, (r + 1) * LANES)
                queries = q_ref[pl.ds(at, size), cols]
                grads = do_ref[pl.ds(at, size), cols]
                scores = jnp.where(allowed, dot(keys, queries, NT) * (score_scale * log2_e), masked_value)
                weights = jnp.exp2(scores - lse_ref[0, r : r + 1, pl.ds(at, size)])
                grad_weights = dot(values, grads, NT)
                grad_scores = (weights * (grad_weights - inner[r : r + 1, pl.ds(at, size)])).astype(bf16)
                dv_term = dot(weights.astype(bf16), grads)
                dk_term = dot(grad_scores, queries)
                dv = dv_term if dv is None else dv + dv_term
                dk = dk_term if dk is None else dk + dk_term
                dq = dot(grad_scores, keys, TN)
                if j == i:
                    dq_sum[pl.ds(at, size), cols] = dq
                else:
                    dq_sum[pl.ds(at, size), cols] += dq
            if i == blocks - 1:
                dk_sum[pl.ds(key_at, size), :] = dk
                dv_sum[pl.ds(key_at, size), :] = dv
            else:
                dk_sum[pl.ds(key_at, size), :] += dk
                dv_sum[pl.ds(key_at, size), :] += dv
    for c in range(blocks):
        rows = slice(c * size, (c + 1) * size)
        cos, sin = cos_ref[rows, :], sin_ref[rows, :]

        def back(grads):
            return ((grads * cos - pltpu.roll(grads, LANES // 2, 1) * sin) * score_scale).astype(bf16)

        for r in range(2):
            cols = slice(r * LANES, (r + 1) * LANES)
            dq_ref[rows, cols] = back(dq_sum[rows, cols])
        dk_ref[rows, :] = back(dk_sum[rows, :])
        dv_ref[rows, :] = dv_sum[rows, :].astype(bf16)


def attend_back(me, qkv, attended, grads, lse, start, cos, sin, blocks):
    seq = qkv.shape[0]
    pair = pl.BlockSpec((seq, 2 * LANES), lambda g, _: (0, g))
    single = pl.BlockSpec((seq, LANES), lambda g, _: (0, g))
    table = pl.BlockSpec((seq, LANES), lambda g, _: (0, 0))
    return pl.pallas_call(
        functools.partial(attend_back_kernel, blocks=blocks, size=seq // blocks),
        grid_spec=pltpu.PrefetchScalarGridSpec(
            num_scalar_prefetch=1,
            grid=(2,),
            in_specs=[
                pair,
                pl.BlockSpec((seq, LANES), lambda g, _: (0, 4 + g)),
                pl.BlockSpec((seq, LANES), lambda g, _: (0, 6 + g)),
                pair,
                pair,
                pl.BlockSpec((1, 2, seq), lambda g, _: (g, 0, 0)),
                pl.BlockSpec((1, seq), lambda g, _: (0, 0)),
                table,
                table,
            ],
            out_specs=[pair, single, single],
            scratch_shapes=[
                pltpu.VMEM((seq, 2 * LANES), f32),
                pltpu.VMEM((seq, LANES), f32),
                pltpu.VMEM((seq, LANES), f32),
                pltpu.VMEM((2, seq), f32),
            ],
        ),
        out_shape=[
            jax.ShapeDtypeStruct((seq, 4 * LANES), bf16),
            jax.ShapeDtypeStruct((seq, 2 * LANES), bf16),
            jax.ShapeDtypeStruct((seq, 2 * LANES), bf16),
        ],
        compiler_params=params(),
        cost_estimate=cost(5 * 2 * 4 * LANES * seq * seq, 10 * seq * 8 * LANES),
        name="attention_back",
    )(me, qkv, qkv, qkv, attended, grads, lse, start, cos, sin)


def out_kernel(att_ref, w_ref, *outs):
    p = pl.program_id(0)
    for k in range(4):

        @pl.when(p == k)
        def _():
            outs[3 - k][...] = dot(att_ref[0, 0], w_ref[...]).astype(bf16)


def out_projection(attended, w_out, piece):
    _, pieces, rows, depth = attended.shape
    width = w_out.shape[1]
    out = jax.ShapeDtypeStruct((rows, width), bf16)
    terms = pl.pallas_call(
        out_kernel,
        grid=(4,),
        in_specs=[pl.BlockSpec((1, 1, rows, depth), lambda k: (k, piece, 0, 0)), whole(w_out.shape)],
        out_specs=[whole((rows, width))] * 4,
        out_shape=[out] * 4,
        compiler_params=params(),
        cost_estimate=cost(8 * rows * depth * width, 2 * (depth * width + 4 * rows * (depth + width))),
        name="out_projection",
    )(attended, w_out)
    return terms[::-1]


def norm_kernel(x_ref, a_ref, b_ref, c_ref, gain_ref, hidden_ref, normed_ref):
    hidden = x_ref[...].astype(f32) + (a_ref[...].astype(f32) + b_ref[...].astype(f32) + c_ref[...].astype(f32))
    hidden_ref[...] = hidden
    inverse = lax.rsqrt(jnp.mean(hidden * hidden, axis=-1, keepdims=True) + epsilon)
    normed_ref[...] = (hidden * inverse * gain_ref[...]).astype(bf16)


def add_norm(tokens, piece, terms, gain):
    rows, width = terms[0].shape
    step = min(rows, 128)
    block = pl.BlockSpec((step, width), lambda k: (k, 0))
    return pl.pallas_call(
        norm_kernel,
        grid=(rows // step,),
        in_specs=[pl.BlockSpec((step, width), lambda k: (piece * (rows // step) + k, 0)), block, block, block, whole((1, width))],
        out_specs=[block, block],
        out_shape=[jax.ShapeDtypeStruct((rows, width), f32), jax.ShapeDtypeStruct((rows, width), bf16)],
        compiler_params=params(),
        cost_estimate=cost(10 * rows * width, 14 * rows * width),
        name="add_norm",
    )(tokens, *terms, gain)


def mlp_kernel(count, *refs):
    xs, cots = refs[:count], refs[count : 2 * count]
    wg, wu, wd = refs[2 * count : 2 * count + 3]
    stack_x, stack_cot, hidden_ref, gate_ref, up_ref, *parts = refs[-(5 + 2 * count) :]
    for k in range(count):

        @pl.when(pl.program_id(0) == k)
        def _():
            x, cot = xs[k][...], cots[k][...]
            stack_x[0, 0], stack_cot[0, 0] = x, cot
            gate = dot(x, wg[...])
            up = dot(x, wu[...])
            grad_hidden = dot(cot, wd[...], NT)
            sig = jax.nn.sigmoid(gate)
            act = gate * sig
            hidden = (act * up).astype(bf16)
            grad_gate = (grad_hidden * up * sig * (1.0 + gate * (1.0 - sig))).astype(bf16)
            grad_up = (grad_hidden * act).astype(bf16)
            hidden_ref[0, 0], gate_ref[0, 0], up_ref[0, 0] = hidden, grad_gate, grad_up
            parts[k][...] = (dot(grad_gate, wg[...], NT) + dot(grad_up, wu[...], NT)).astype(bf16)
            parts[count + k][...] = dot(hidden, wd[...]).astype(bf16)


def mlp_call(first, piece, pieces, xs, cots, wg, wu, wd, before):
    count = len(xs)
    rows, width = xs[0].shape
    units = wg.shape[1]
    spec = lambda cols: pl.BlockSpec((1, 1, rows, cols), lambda k: (first + k, piece, 0, 0))
    inputs = [*xs, *cots, wg, wu, wd]
    specs = [whole((rows, width))] * (2 * count) + [whole(w.shape) for w in (wg, wu, wd)]
    aliases = {}
    if before is not None:
        aliases = {len(inputs) + k: k for k in range(5)}
        inputs += list(before)
        specs += [pl.BlockSpec(memory_space=pl.ANY)] * 5
    cols = (width, width, units, units, units)
    outs = pl.pallas_call(
        functools.partial(mlp_kernel, count),
        grid=(count,),
        in_specs=specs,
        out_specs=[spec(c) for c in cols] + [whole((rows, width))] * (2 * count),
        out_shape=[jax.ShapeDtypeStruct((4, pieces, rows, c), bf16) for c in cols]
        + [jax.ShapeDtypeStruct((rows, width), bf16)] * (2 * count),
        input_output_aliases=aliases,
        compiler_params=params(),
        cost_estimate=cost(12 * count * rows * width * units, 6 * width * units + 2 * count * rows * (6 * width + 3 * units)),
        name="mlp",
    )(*inputs)
    return outs[:5], outs[5 : 5 + count], outs[5 + count :]


def norm_back_kernel(hidden_ref, cot_ref, a_ref, b_ref, c_ref, gain_ref, grad_ref, low_ref, gain_grad_ref):
    hidden = hidden_ref[...]
    grad = a_ref[...].astype(f32) + b_ref[...].astype(f32) + c_ref[...].astype(f32)
    inverse = lax.rsqrt(jnp.mean(hidden * hidden, axis=-1, keepdims=True) + epsilon)
    unit = hidden * inverse
    scaled = grad * gain_ref[...]
    result = cot_ref[...].astype(f32) + inverse * (scaled - unit * jnp.mean(scaled * unit, axis=-1, keepdims=True))
    grad_ref[...] = result
    if low_ref is not None:
        low_ref[...] = result.astype(bf16)
    product = grad * unit
    sums = jnp.sum(product.reshape(-1, 8, product.shape[-1]), axis=0)

    @pl.when(pl.program_id(0) == 0)
    def _():
        gain_grad_ref[...] = sums

    @pl.when(pl.program_id(0) > 0)
    def _():
        gain_grad_ref[...] += sums


def norm_back(hidden, cot, piece, cot_piece, terms, gain, low):
    rows, width = terms[0].shape
    step = min(rows, 128)
    steps = rows // step
    block = pl.BlockSpec((step, width), lambda k: (k, 0))
    at = lambda base: pl.BlockSpec((step, width), lambda k: (base * steps + k, 0))
    outs = [block] + [block] * low + [whole((8, width))]
    shapes = [jax.ShapeDtypeStruct((rows, width), f32)] + [jax.ShapeDtypeStruct((rows, width), bf16)] * low
    shapes += [jax.ShapeDtypeStruct((8, width), f32)]

    def kernel(h, c, t0, t1, t2, gain_ref, *out_refs):
        grad_ref, *rest = out_refs
        if not low:
            rest = [None, *rest]
        cast = h
        norm_back_kernel(_Widened(cast), c, t0, t1, t2, gain_ref, grad_ref, *rest)

    return pl.pallas_call(
        kernel,
        grid=(steps,),
        in_specs=[at(piece), at(cot_piece), block, block, block, whole((1, width))],
        out_specs=outs,
        out_shape=shapes,
        compiler_params=params(),
        cost_estimate=cost(20 * rows * width, 20 * rows * width),
        name="norm_back",
    )(hidden, cot, *terms, gain)


class _Widened:
    def __init__(self, ref):
        self.ref = ref

    def __getitem__(self, index):
        return self.ref[index].astype(f32)


def grad_attended_kernel(*refs):
    xs, w, rest = refs[:4], refs[4], refs[5:]
    out_ref, stack_ref = rest[-2:]
    for k in range(4):

        @pl.when(pl.program_id(0) == k)
        def _():
            g = xs[k][...]
            stack_ref[0, 0] = g
            out_ref[0, 0] = dot(g, w[...], NT).astype(bf16)


def grad_attended_call(piece, pieces, xs, w_out, before):
    rows, width = xs[0].shape
    depth = w_out.shape[0]
    spec = lambda cols: pl.BlockSpec((1, 1, rows, cols), lambda k: (k, piece, 0, 0))
    inputs = [*xs, w_out]
    specs = [whole((rows, width))] * 4 + [whole(w_out.shape)]
    aliases = {}
    if before is not None:
        aliases = {5: 0, 6: 1}
        inputs += list(before)
        specs += [pl.BlockSpec(memory_space=pl.ANY)] * 2
    return pl.pallas_call(
        grad_attended_kernel,
        grid=(4,),
        in_specs=specs,
        out_specs=[spec(depth), spec(width)],
        out_shape=[jax.ShapeDtypeStruct((4, pieces, rows, c), bf16) for c in (depth, width)],
        input_output_aliases=aliases,
        compiler_params=params(),
        cost_estimate=cost(8 * rows * width * depth, 2 * (width * depth + 4 * rows * (2 * width + depth))),
        name="grad_attended",
    )(*inputs)


def grad_normed_kernel(dq_ref, dk_ref, dv_ref, wq, wk, wv, *outs):
    for k in range(4):

        @pl.when(pl.program_id(0) == k)
        def _():
            total = dot(dq_ref[...], wq[...], NT) + dot(dk_ref[...], wk[...], NT) + dot(dv_ref[...], wv[...], NT)
            outs[3 - k][...] = total.astype(bf16)


def grad_normed(dq, dk, dv, wq, wk, wv):
    rows, width = dq.shape[0] // 4, wq.shape[0]
    block = lambda cols: pl.BlockSpec((rows, cols), lambda k: (k, 0))
    terms = pl.pallas_call(
        grad_normed_kernel,
        grid=(4,),
        in_specs=[block(dq.shape[1]), block(dk.shape[1]), block(dv.shape[1])] + [whole(w.shape) for w in (wq, wk, wv)],
        out_specs=[whole((rows, width))] * 4,
        out_shape=[jax.ShapeDtypeStruct((rows, width), bf16)] * 4,
        compiler_params=params(),
        cost_estimate=cost(8 * rows * width * 8 * LANES, 2 * width * 8 * LANES + 8 * rows * (width + 8 * LANES)),
        name="grad_normed",
    )(dq, dk, dv, wq, wk, wv)
    return terms[::-1]


def spread(heads):
    col = lax.broadcasted_iota(jnp.int32, (heads * HEAD_SIZE, heads * LANES), 1)
    row = lax.broadcasted_iota(jnp.int32, (heads * HEAD_SIZE, heads * LANES), 0)
    half, feature = row // HALF, row % HALF
    return (col == half * (LANES // 2) + feature).astype(bf16)


def body(
    tokens, segments, positions, norm_attn, w_query, key_weight, value_weight, w_out,
    norm_mlp, w_gate, w_up, w_down, cotangent,
):
    seq = segments.shape[0]
    own, width = tokens.shape
    me = lax.axis_index("tensor")
    order = me ^ jnp.arange(4, dtype=jnp.int32)
    blocks = 4

    starts = jnp.zeros_like(segments)
    for document in (1, 2, 3):
        first = jnp.sum((segments < document).astype(jnp.int32))
        starts = jnp.where(segments >= document, first, starts)
    start = jnp.take(starts.reshape(4, own), order, axis=0).reshape(1, seq)
    places = jnp.take(positions.reshape(4, own), order, axis=0).reshape(seq)
    lane = jnp.arange(LANES // 2)
    inverse = jnp.exp(lane.astype(f32) * (-2.0 * math.log(rope_base) / HEAD_SIZE))
    angles = places.astype(f32)[:, None] * jnp.where(lane < HALF, inverse, 0.0)[None, :]
    cos, sin = jnp.cos(angles), jnp.sin(angles)
    cos = jnp.concatenate([cos, cos], 1)
    sin = jnp.concatenate([-sin, sin], 1)
    me_ref = me.astype(jnp.int32).reshape(1)

    spread_q, spread_k = spread(w_query.shape[1] // HEAD_SIZE), spread(key_weight.shape[1] // HEAD_SIZE)
    wq = dot(w_query, spread_q).astype(bf16)
    wk = dot(key_weight, spread_k).astype(bf16)
    wv = dot(value_weight, spread_k).astype(bf16)
    wo = dot(spread_q, w_out, TN).astype(bf16)
    gain_attn, gain_mlp = norm_attn.reshape(1, width), norm_mlp.reshape(1, width)

    inputs = tokens.astype(f32)
    inverse_one = lax.rsqrt(jnp.mean(inputs * inputs, axis=-1, keepdims=True) + epsilon)
    normed_one = (inputs * inverse_one * norm_attn).astype(bf16)

    pieces, rows = CHUNKS, own // CHUNKS
    table = lambda t: t.reshape(4, pieces, rows, LANES)
    split = lambda t: [t[k * rows : (k + 1) * rows] for k in range(pieces)]
    stacks = None
    gathered = [gather_four(x) for x in split(normed_one)]
    for first in (0, 2):
        for piece in range(pieces):
            stacks = qkv_call(first, piece, pieces, gathered[piece][first : first + 2], wq, wk, wv, table(cos), table(sin), stacks)
    qkv, attn_in = stacks[0].reshape(seq, 8 * LANES), stacks[1].reshape(seq, width)

    attended, lse = attend(me_ref, qkv, start, blocks)
    cots = [gather_four(x) for x in split(cotangent)]

    attended_pieces = attended.reshape(4, pieces, rows, 4 * LANES)
    hidden_one, grad_one, gain_two_grads = [], [], []
    stacks = grads = None
    outs = []
    for piece in range(pieces):
        terms = scatter_sum(out_projection(attended_pieces, wo, piece))
        hidden, normed = add_norm(tokens, piece, terms, gain_mlp)
        xs = gather_four(normed)
        stacks, grad_low, out_low = mlp_call(0, piece, pieces, xs[:2], cots[piece][:2], w_gate, w_up, w_down, stacks)
        stacks, grad_high, out_high = mlp_call(2, piece, pieces, xs[2:], cots[piece][2:], w_gate, w_up, w_down, stacks)
        terms = scatter_sum([*grad_low, *grad_high])
        grad, low, gain_grad = norm_back(hidden, cotangent, 0, piece, terms, gain_mlp, 1)
        grads = grad_attended_call(piece, pieces, gather_four(low), wo, grads)
        hidden_one.append(hidden)
        grad_one.append(grad)
        gain_two_grads.append(gain_grad)
        outs.append([*out_low, *out_high])
    mlp_in, grad_out, hidden, grad_gate, grad_up = [t.reshape(seq, -1) for t in stacks]
    grad_attended, grad_rows = [t.reshape(seq, -1) for t in grads]

    grad_w_down = dp_sum(dot(hidden, grad_out, TN).astype(bf16))
    grad_w_gate = dp_sum(dot(mlp_in, grad_gate, TN).astype(bf16))
    grad_w_up = dp_sum(dot(mlp_in, grad_up, TN).astype(bf16))
    grad_w_out = dp_sum(dot(dot(attended, spread_q, NT).astype(bf16), grad_rows, TN).astype(bf16))

    output = []
    for piece in range(pieces):
        a, b, c = scatter_sum(outs[piece])
        output.append((hidden_one[piece] + (a.astype(f32) + b.astype(f32) + c.astype(f32))).astype(bf16))
    output = jnp.concatenate(output, 0)

    dq, dk, dv = attend_back(me_ref, qkv, attended, grad_attended, lse, start, cos, sin, blocks)
    grad_w_query = dp_sum(dot(attn_in, dot(dq, spread_q, NT).astype(bf16), TN).astype(bf16))
    grad_w_key = dp_sum(dot(attn_in, dot(dk, spread_k, NT).astype(bf16), TN).astype(bf16))
    grad_w_value = dp_sum(dot(attn_in, dot(dv, spread_k, NT).astype(bf16), TN).astype(bf16))
    terms = scatter_sum(grad_normed(dq, dk, dv, wq, wk, wv))
    grad_tokens, gain_one_grad = norm_back(tokens, jnp.concatenate(grad_one, 0), 0, 0, terms, gain_attn, 0)

    gains = jnp.stack([jnp.sum(gain_one_grad, 0), jnp.sum(sum(gain_two_grads), 0)])
    gains = all_sum(gains)
    return (
        output, grad_tokens, gains[0], grad_w_query, grad_w_key, grad_w_value, grad_w_out,
        gains[1], grad_w_gate, grad_w_up, grad_w_down,
    )


def solution(mesh):
    rows, cols, both = P("tensor", None), P(None, "tensor"), P(("dp", "tensor"), None)
    in_specs = (both, P("dp"), P("dp"), P(), cols, cols, cols, rows, P(), cols, cols, rows, both)
    out_specs = (both, both, P(), cols, cols, cols, rows, P(), cols, cols, rows)
    return jax.shard_map(body, mesh=mesh, in_specs=in_specs, out_specs=out_specs, check_vma=False)
```

```python
import functools
import math

import jax
import jax.numpy as jnp
from jax import lax
from jax.experimental import pallas as pl
from jax.experimental.pallas import tpu as pltpu
from jax.sharding import PartitionSpec as P

HEAD_SIZE = 96
HALF = HEAD_SIZE // 2
LANES = 128
epsilon = 1e-05
rope_base = 100000.0
masked_value = -1e30
score_scale = 1.0 / math.sqrt(HEAD_SIZE)
log2_e = math.log2(math.e)
bf16, f32 = jnp.bfloat16, jnp.float32
NN = (((1,), (0,)), ((), ()))
NT = (((1,), (1,)), ((), ()))
TN = (((0,), (0,)), ((), ()))
VMEM_LIMIT = 67043328
CHUNKS = 4


def dot(left, right, dims=NN):
    return lax.dot_general(left, right, dims, preferred_element_type=f32)


def params():
    return pltpu.CompilerParams(vmem_limit_bytes=VMEM_LIMIT)


def cost(flops, nbytes):
    return pl.CostEstimate(flops=int(flops), bytes_accessed=int(nbytes), transcendentals=0)


def whole(shape):
    return pl.BlockSpec(shape, lambda *_: (0,) * len(shape), pipeline_mode=pl.Buffered(1))


def swap(values, bits):
    size = lax.axis_size("tensor")
    return lax.ppermute(values, "tensor", [(i, i ^ bits) for i in range(size)])


def dp_swap(values, bits):
    size = lax.axis_size("dp")
    return lax.ppermute(values, "dp", [(i, i ^ bits) for i in range(size)])


def dp_sum(values):
    size, index = lax.axis_size("dp"), lax.axis_index("dp")
    rows = values.shape[0]
    piece = values
    bit = 1
    while bit < size:
        half = piece.shape[0] // 2
        mine = (index // bit) % 2
        send = lax.dynamic_slice_in_dim(piece, (1 - mine) * half, half, 0)
        keep = lax.dynamic_slice_in_dim(piece, mine * half, half, 0)
        got = dp_swap(send, bit)
        piece = (keep.astype(f32) + got.astype(f32)).astype(bf16)
        bit *= 2
    while bit > 1:
        bit //= 2
        mine = (index // bit) % 2
        got = dp_swap(piece, bit)
        piece = jnp.where(mine == 0, jnp.concatenate([piece, got], 0), jnp.concatenate([got, piece], 0))
    return piece.astype(f32)


def all_sum(values):
    bit = 1
    while bit < lax.axis_size("tensor"):
        values = values + swap(values, bit)
        bit *= 2
    bit = 1
    while bit < lax.axis_size("dp"):
        values = values + dp_swap(values, bit)
        bit *= 2
    return values


ANY = pl.BlockSpec(memory_space=pl.ANY)
VMEM = pl.BlockSpec(memory_space=pltpu.VMEM)


def peer(bits):
    me = lax.axis_index("tensor")
    low, high = lax.rem(me, 2), lax.div(me, 2)
    if bits % 2:
        low = 1 - low
    if bits // 2:
        high = 1 - high
    return 2 * high + low


def partner(bits):
    return {"tensor": peer(bits)}


def send(source, target, sems, at, bits):
    return pltpu.make_async_remote_copy(
        src_ref=source,
        dst_ref=target,
        send_sem=sems[0].at[at],
        recv_sem=sems[1].at[at],
        device_id=partner(bits),
        device_id_type=pl.DeviceIdType.MESH,
    )


def meet():
    barrier = pltpu.get_barrier_semaphore()
    for bits in (1, 2):
        pl.semaphore_signal(barrier, inc=1, device_id=partner(bits), device_id_type=pl.DeviceIdType.MESH)
    pl.semaphore_wait(barrier, 2)


def comm_params(number):
    return pltpu.CompilerParams(vmem_limit_bytes=VMEM_LIMIT, collective_id=number, has_side_effects=True)


def dma_sems(*shape):
    return [pltpu.SemaphoreType.DMA(shape)] * 2


def qkv_kernel(x_ref, wq, wk, wv, cos_ref, sin_ref, qkv_ref, stack_ref, land, send_sem, recv_sem, out_sem):
    sems = (send_sem, recv_sem)
    own = x_ref.shape[0]
    rows = own // CHUNKS
    lane = lax.broadcasted_iota(jnp.int32, (rows, LANES), 1)

    def project(ref, base):
        x = ref[...]
        cos, sin = cos_ref[pl.ds(base, rows), :], sin_ref[pl.ds(base, rows), :]
        for w, first, turn in ((wq, 0, True), (wk, 4, True), (wv, 6, False)):
            y = dot(x, w[...])
            for h in range(w.shape[1] // LANES):
                v = y[:, h * LANES : (h + 1) * LANES]
                if turn:
                    v = v * cos + pltpu.roll(v, LANES // 2, 1) * sin
                else:
                    v = jnp.where(lane == HALF, 1.0, v)
                at = (first + h) * LANES
                qkv_ref[pl.ds(base, rows), at : at + LANES] = v.astype(bf16)

    def piece(k):
        return pl.ds(pl.multiple_of(k * rows, rows), rows)

    side = send(x_ref, land.at[0], sems, 2 * CHUNKS, 1)
    across = lambda k: send(x_ref.at[piece(k)], land.at[1, piece(k)], sems, k, 2)
    onward = lambda k: send(land.at[1, piece(k)], land.at[2, piece(k)], sems, CHUNKS + k, 1)
    store = lambda p: pltpu.make_async_copy(x_ref if p == 0 else land.at[p - 1], stack_ref.at[p], out_sem.at[p])

    meet()
    side.start()
    for k in range(CHUNKS):
        across(k).start()
    store(0).start()

    @pl.loop(0, CHUNKS)
    def _(k):
        project(x_ref.at[piece(k)], pl.multiple_of(k * rows, rows))

    side.wait_recv()
    store(1).start()

    @pl.loop(0, CHUNKS)
    def _(k):
        project(land.at[0, piece(k)], pl.multiple_of(own + k * rows, rows))

    @pl.loop(0, CHUNKS)
    def _(k):
        across(k).wait_recv()
        onward(k).start()
        project(land.at[1, piece(k)], pl.multiple_of(2 * own + k * rows, rows))
        onward(k).wait_recv()
        project(land.at[2, piece(k)], pl.multiple_of(3 * own + k * rows, rows))

    store(2).start()
    store(3).start()
    side.wait_send()
    for k in range(CHUNKS):
        across(k).wait_send()
        onward(k).wait_send()
    for p in range(4):
        store(p).wait()


def project_qkv(x, wq, wk, wv, cos, sin):
    own, width = x.shape
    return pl.pallas_call(
        qkv_kernel,
        in_specs=[VMEM] * 6,
        out_specs=[VMEM, ANY],
        out_shape=[jax.ShapeDtypeStruct((4 * own, 8 * LANES), bf16), jax.ShapeDtypeStruct((4, own, width), bf16)],
        scratch_shapes=[pltpu.VMEM((3, own, width), bf16), *dma_sems(2 * CHUNKS + 1), pltpu.SemaphoreType.DMA((4,))],
        compiler_params=comm_params(1),
        cost_estimate=cost(40e-6 * 1e15, 20e6),
        name="gather_project_qkv",
    )(x, wq, wk, wv, cos, sin)


def attend_kernel(
    q_ref, k_ref, v_ref, start_ref, cot_ref, o_ref, lse_ref, cots_ref, send_sem, recv_sem, *, blocks, size
):
    sems = (send_sem, recv_sem)
    side = send(cot_ref, cots_ref.at[0], sems, 2 * CHUNKS, 1)
    across = lambda k: send(cot_ref.at[k], cots_ref.at[1, k], sems, k, 2)
    onward = lambda k: send(cots_ref.at[1, k], cots_ref.at[2, k], sems, CHUNKS + k, 1)

    @pl.when(pl.program_id(0) == 0)
    def _():
        meet()
        side.start()
        for k in range(CHUNKS):
            across(k).start()

    for i in range(blocks):
        at = pl.multiple_of(peer(i) * size, size)
        queries = [q_ref[pl.ds(at, size), r * LANES : (r + 1) * LANES] for r in range(2)]
        start = start_ref[:, pl.ds(at, size)]
        state = [None, None]
        for j in [i, *range(i)]:
            key_at = pl.multiple_of(peer(j) * size, size)
            keys = k_ref[pl.ds(key_at, size), :]
            values = v_ref[pl.ds(key_at, size), :]
            key_rows = lax.broadcasted_iota(jnp.int32, (size, size), 0)
            allowed = key_rows >= start - j * size
            if j == i:
                allowed &= key_rows <= lax.broadcasted_iota(jnp.int32, (size, size), 1)
            for r in range(2):
                scores = jnp.where(allowed, dot(keys, queries[r], NT) * (score_scale * log2_e), masked_value)
                peak = jnp.max(scores, axis=0, keepdims=True)
                if state[r] is not None:
                    peak = jnp.maximum(state[r][0], peak)
                weights = jnp.exp2(scores - peak)
                mixed = dot(values, weights.astype(bf16), TN)
                if state[r] is not None:
                    mixed += state[r][1] * jnp.exp2(state[r][0] - peak)
                state[r] = (peak, mixed)
        for r, (peak, mixed) in enumerate(state):
            total = mixed[HALF : HALF + 1, :]
            o_ref[pl.ds(at, size), r * LANES : (r + 1) * LANES] = (mixed / total).T.astype(bf16)
            lse_ref[0, r : r + 1, pl.ds(at, size)] = peak + jnp.log2(total)

    @pl.when(pl.program_id(0) == 1)
    def _():
        for k in range(CHUNKS):
            across(k).wait_recv()
            onward(k).start()
        side.wait()
        for k in range(CHUNKS):
            across(k).wait_send()
            onward(k).wait()


def attend(qkv, start, cot, blocks):
    seq = qkv.shape[0]
    own, width = cot.shape
    pieces = (CHUNKS, own // CHUNKS, width)
    flops = 2 * 2 * 4 * LANES * seq * seq
    return pl.pallas_call(
        functools.partial(attend_kernel, blocks=blocks, size=seq // blocks),
        grid=(2,),
        in_specs=[
            pl.BlockSpec((seq, 2 * LANES), lambda g: (0, g)),
            pl.BlockSpec((seq, LANES), lambda g: (0, 4 + g)),
            pl.BlockSpec((seq, LANES), lambda g: (0, 6 + g)),
            pl.BlockSpec((1, seq), lambda g: (0, 0)),
            ANY,
        ],
        out_specs=[
            pl.BlockSpec((seq, 2 * LANES), lambda g: (0, g)),
            pl.BlockSpec((1, 2, seq), lambda g: (g, 0, 0)),
            ANY,
        ],
        scratch_shapes=dma_sems(2 * CHUNKS + 1),
        out_shape=[
            jax.ShapeDtypeStruct((seq, 4 * LANES), bf16),
            jax.ShapeDtypeStruct((2, 2, seq), f32),
            jax.ShapeDtypeStruct((3, *pieces), bf16),
        ],
        compiler_params=comm_params(4),
        cost_estimate=cost(flops, 6 * seq * 8 * LANES),
        name="attention",
    )(qkv, qkv, qkv, start, cot.reshape(pieces))


def attend_back_kernel(
    q_ref, k_ref, v_ref, o_ref, do_ref, lse_ref, start_ref, cos_ref, sin_ref, parts, hid1,
    dq_ref, dk_ref, dv_ref, out_ref, dq_sum, dk_sum, dv_sum, inner, mine, side, across, send_sem, recv_sem, load_sem,
    *, blocks, size,
):
    pieces = parts.shape[0]
    sems = (send_sem, recv_sem)
    from_side = [send(parts.at[:, 3 - 2 * k], side.at[k], sems, k, 1) for k in range(2)]
    from_across = send(mine.at[0], across, sems, 2, 2)
    load = [pltpu.make_async_copy(parts.at[:, 2 - 2 * k], mine.at[k], load_sem.at[k]) for k in range(2)]

    @pl.when(pl.program_id(0) == 0)
    def _():
        load[0].start()
        load[1].start()
        meet()
        from_side[0].start()
        from_side[1].start()

    for c in range(blocks):
        rows = slice(c * size, (c + 1) * size)
        for r in range(2):
            cols = slice(r * LANES, (r + 1) * LANES)
            product = do_ref[rows, cols].astype(f32) * o_ref[rows, cols].astype(f32)
            inner[r : r + 1, rows] = jnp.sum(product.T, axis=0, keepdims=True)
    for i in reversed(range(blocks)):
        if i == blocks - 2:

            @pl.when(pl.program_id(0) == 0)
            def _():
                load[0].wait()
                from_side[0].wait_recv()
                for k in range(pieces):
                    mine[0, k] = (mine[0, k].astype(f32) + side[0, k].astype(f32)).astype(bf16)
                from_across.start()

        for j in [i, *range(i)]:
            at = pl.multiple_of(peer(i) * size, size)
            key_at = pl.multiple_of(peer(j) * size, size)
            keys = k_ref[pl.ds(key_at, size), :]
            values = v_ref[pl.ds(key_at, size), :]
            start = start_ref[:, pl.ds(at, size)]
            key_rows = lax.broadcasted_iota(jnp.int32, (size, size), 0)
            allowed = key_rows >= start - j * size
            if j == i:
                allowed &= key_rows <= lax.broadcasted_iota(jnp.int32, (size, size), 1)
            dk = dv = None
            for r in range(2):
                cols = slice(r * LANES, (r + 1) * LANES)
                queries = q_ref[pl.ds(at, size), cols]
                grads = do_ref[pl.ds(at, size), cols]
                scores = jnp.where(allowed, dot(keys, queries, NT) * (score_scale * log2_e), masked_value)
                weights = jnp.exp2(scores - lse_ref[0, r : r + 1, pl.ds(at, size)])
                grad_weights = dot(values, grads, NT)
                grad_scores = (weights * (grad_weights - inner[r : r + 1, pl.ds(at, size)])).astype(bf16)
                dv_term = dot(weights.astype(bf16), grads)
                dk_term = dot(grad_scores, queries)
                dv = dv_term if dv is None else dv + dv_term
                dk = dk_term if dk is None else dk + dk_term
                dq = dot(grad_scores, keys, TN)
                if j == i:
                    dq_sum[pl.ds(at, size), cols] = dq
                else:
                    dq_sum[pl.ds(at, size), cols] += dq
            if i == blocks - 1:
                dk_sum[pl.ds(key_at, size), :] = dk
                dv_sum[pl.ds(key_at, size), :] = dv
            else:
                dk_sum[pl.ds(key_at, size), :] += dk
                dv_sum[pl.ds(key_at, size), :] += dv
    for c in range(blocks):
        rows = slice(c * size, (c + 1) * size)
        cos, sin = cos_ref[rows, :], sin_ref[rows, :]

        def back(grads):
            return ((grads * cos - pltpu.roll(grads, LANES // 2, 1) * sin) * score_scale).astype(bf16)

        for r in range(2):
            cols = slice(r * LANES, (r + 1) * LANES)
            dq_ref[rows, cols] = back(dq_sum[rows, cols])
        dk_ref[rows, :] = back(dk_sum[rows, :])
        dv_ref[rows, :] = dv_sum[rows, :].astype(bf16)

    @pl.when(pl.program_id(0) == 1)
    def _():
        load[1].wait()
        from_side[1].wait_recv()
        from_across.wait()
        from_side[0].wait_send()
        from_side[1].wait_send()
        for k in range(pieces):
            term = mine[1, k].astype(f32) + side[1, k].astype(f32) + across[k].astype(f32)
            out_ref[k] = (hid1[k] + term).astype(bf16)


def attend_back(qkv, attended, grads, lse, start, cos, sin, parts, hid1, blocks):
    seq = qkv.shape[0]
    own = hid1.shape
    pair = pl.BlockSpec((seq, 2 * LANES), lambda g: (0, g))
    single = pl.BlockSpec((seq, LANES), lambda g: (0, g))
    table = pl.BlockSpec((seq, LANES), lambda g: (0, 0))
    return pl.pallas_call(
        functools.partial(attend_back_kernel, blocks=blocks, size=seq // blocks),
        grid=(2,),
        in_specs=[
            pair,
            pl.BlockSpec((seq, LANES), lambda g: (0, 4 + g)),
            pl.BlockSpec((seq, LANES), lambda g: (0, 6 + g)),
            pair,
            pair,
            pl.BlockSpec((1, 2, seq), lambda g: (g, 0, 0)),
            pl.BlockSpec((1, seq), lambda g: (0, 0)),
            table,
            table,
            ANY,
            whole(own),
        ],
        out_specs=[pair, single, single, whole(own)],
        scratch_shapes=[
            pltpu.VMEM((seq, 2 * LANES), f32),
            pltpu.VMEM((seq, LANES), f32),
            pltpu.VMEM((seq, LANES), f32),
            pltpu.VMEM((2, seq), f32),
            pltpu.VMEM((2, *own), bf16),
            pltpu.VMEM((2, *own), bf16),
            pltpu.VMEM(own, bf16),
            *dma_sems(3),
            pltpu.SemaphoreType.DMA((2,)),
        ],
        out_shape=[
            jax.ShapeDtypeStruct((seq, 4 * LANES), bf16),
            jax.ShapeDtypeStruct((seq, 2 * LANES), bf16),
            jax.ShapeDtypeStruct((seq, 2 * LANES), bf16),
            jax.ShapeDtypeStruct(own, bf16),
        ],
        compiler_params=comm_params(5),
        cost_estimate=cost(5 * 2 * 4 * LANES * seq * seq, 10 * seq * 8 * LANES),
        name="attention_back",
    )(qkv, qkv, qkv, attended, grads, lse, start, cos, sin, parts, hid1)


RS1_C0, RS1_C1, RS1_X, AG2_X, AG2_C, AG2_F, RS3_C0, RS3_C1, RS3_X, AG3_X, AG3_C, AG3_F = range(12)


def middle_kernel(
    att, wo, tokens, gain, cot_own, cots, wg, wu, wd,
    hid1, datt_out, parts_out, grad_one_out, dwd_out, dwg_out, dwu_out, dwo_out, gain_grad,
    xs, cot, hid, gg, gu, g, cr, xr, part_stage, grad_stage, datt_stage, tile_stage,
    send_sem, recv_sem, cot_sem, part_sem, grad_sem, datt_sem, tile_sem, free_sem,
):
    pieces, _, n, width = xs.shape
    units = wg.shape[1]
    heads = wo.shape[0]
    sems = (send_sem, recv_sem)
    two = (2 * n, width)

    def copy(kind, k):
        source, target, bits = {
            RS1_C0: (g.at[k, 3], cr.at[k, 0], 1),
            RS1_C1: (g.at[k, 1], cr.at[k, 1], 1),
            RS1_X: (g.at[k, 2], xr.at[k], 2),
            AG2_X: (xs.at[k, 0], xs.at[k, 2], 2),
            AG2_C: (xs.at[k, 0], xs.at[k, 1], 1),
            AG2_F: (xs.at[k, 2], xs.at[k, 3], 1),
            RS3_C0: (g.at[k, 3], cr.at[k, 0], 1),
            RS3_C1: (g.at[k, 1], cr.at[k, 1], 1),
            RS3_X: (g.at[k, 2], xr.at[k], 2),
            AG3_X: (g.at[k, 0], g.at[k, 2], 2),
            AG3_C: (g.at[k, 0], g.at[k, 1], 1),
            AG3_F: (g.at[k, 2], g.at[k, 3], 1),
        }[kind]
        return send(source, target, sems, (kind, k), bits)

    def credit(k, bits):
        pl.semaphore_signal(
            free_sem.at[bits - 1, k], inc=1, device_id=partner(bits), device_id_type=pl.DeviceIdType.MESH
        )

    def cot_copy(p):
        source = cot_own if p == 0 else cots.at[p - 1]
        return pltpu.make_async_copy(source, cot.at[:, p], cot_sem.at[p])

    def part_copy(k, low):
        return pltpu.make_async_copy(part_stage.at[k], parts_out.at[k, pl.ds(low, 2)], part_sem.at[k])

    for p in range(4):
        cot_copy(p).start()
    meet()

    @pl.loop(0, pieces)
    def _(k):
        for p, kind in ((3, RS1_C0), (1, RS1_C1)):
            g[k, p] = dot(att[p, k], wo[...]).astype(bf16)
            copy(kind, k).start()

    @pl.loop(0, pieces)
    def _(k):
        term = dot(att[2, k], wo[...])
        copy(RS1_C0, k).wait_recv()
        g[k, 2] = (term + cr[k, 0].astype(f32)).astype(bf16)
        copy(RS1_X, k).start()

    def feed_forward(k, low):
        x = xs[k, pl.ds(low, 2)].reshape(two)
        gate = dot(x, wg[...])
        up = dot(x, wu[...])
        grad_hidden = dot(cot[k, pl.ds(low, 2)].reshape(two), wd[...], NT)
        sig = jax.nn.sigmoid(gate)
        act = gate * sig
        hidden = (act * up).astype(bf16)
        grad_gate = (grad_hidden * up * sig * (1.0 + gate * (1.0 - sig))).astype(bf16)
        grad_up = (grad_hidden * act).astype(bf16)
        hid[k, pl.ds(low, 2)] = hidden.reshape(2, n, units)
        gg[k, pl.ds(low, 2)] = grad_gate.reshape(2, n, units)
        gu[k, pl.ds(low, 2)] = grad_up.reshape(2, n, units)
        back = dot(grad_gate, wg[...], NT) + dot(grad_up, wu[...], NT)
        g[k, pl.ds(low, 2)] = back.astype(bf16).reshape(2, n, width)
        return hidden

    def out_part(k, low, hidden):
        part_stage[k] = dot(hidden, wd[...]).astype(bf16).reshape(2, n, width)
        part_copy(k, low).start()

    for p in range(4):
        cot_copy(p).wait()

    @pl.loop(0, pieces)
    def _(k):
        term = dot(att[0, k], wo[...])
        copy(RS1_C1, k).wait_recv()
        copy(RS1_X, k).wait_recv()
        hidden = tokens[k].astype(f32) + (term + cr[k, 1].astype(f32) + xr[k].astype(f32))
        hid1[k] = hidden
        inverse = lax.rsqrt(jnp.mean(hidden * hidden, axis=-1, keepdims=True) + epsilon)
        xs[k, 0] = (hidden * inverse * gain[...]).astype(bf16)
        copy(AG2_X, k).start()
        copy(AG2_C, k).start()
        copy(AG2_C, k).wait_recv()
        copy(RS1_C1, k).wait_send()
        out_part(k, 0, feed_forward(k, 0))

    @pl.loop(0, pieces)
    def _(k):
        copy(AG2_X, k).wait_recv()
        copy(AG2_F, k).start()
        part_copy(k, 0).wait()
        copy(AG2_F, k).wait_recv()
        copy(RS1_C0, k).wait_send()
        copy(RS1_X, k).wait_send()
        hidden = feed_forward(k, 2)
        copy(RS3_C0, k).start()
        copy(RS3_C1, k).start()
        out_part(k, 2, hidden)
        copy(RS3_C0, k).wait_recv()
        g[k, 2] = (g[k, 2].astype(f32) + cr[k, 0].astype(f32)).astype(bf16)
        copy(RS3_X, k).start()

    tokens_all = 4 * pieces * n

    def tile(slot, left, right, cols, out, at):
        height = out.shape[1]
        target = out.at[pl.ds(pl.multiple_of(at * 256, 256), 256)]
        move = pltpu.make_async_copy(tile_stage.at[slot, :, pl.ds(0, height)], target, tile_sem.at[slot])
        part = left[:, :, :, pl.ds(pl.multiple_of(at * 256, 256), 256)].reshape(tokens_all, 256)
        tile_stage[slot, :, pl.ds(0, height)] = dot(part, right[...].reshape(tokens_all, cols), TN).astype(bf16)
        return move

    @pl.loop(0, 4)
    def _(k):
        down = tile(0, hid, cot, width, dwd_out, k)
        down.start()
        copy(RS3_C1, k).wait_recv()
        copy(RS3_X, k).wait_recv()
        copy(RS3_C0, k).wait_send()
        copy(RS3_C1, k).wait_send()
        credit(k, 1)
        copy(RS3_X, k).wait_send()
        credit(k, 2)
        grad = g[k, 0].astype(f32) + cr[k, 1].astype(f32) + xr[k].astype(f32)
        hidden = hid1[k]
        inverse = lax.rsqrt(jnp.mean(hidden * hidden, axis=-1, keepdims=True) + epsilon)
        unit = hidden * inverse
        scaled = grad * gain[...]
        result = cot[k, 0].astype(f32) + inverse * (scaled - unit * jnp.mean(scaled * unit, axis=-1, keepdims=True))
        g[k, 0] = result.astype(bf16)
        pl.semaphore_wait(free_sem.at[0, k], 1)
        pl.semaphore_wait(free_sem.at[1, k], 1)
        copy(AG3_X, k).start()
        copy(AG3_C, k).start()
        grad_stage[...] = result
        stored = pltpu.make_async_copy(grad_stage, grad_one_out.at[k], grad_sem.at[0])
        stored.start()
        sums = jnp.sum((grad * unit).reshape(-1, 8, width), axis=0)

        @pl.when(k == 0)
        def _():
            gain_grad[...] = sums

        @pl.when(k > 0)
        def _():
            gain_grad[...] += sums

        down.wait()
        gate = tile(0, xs, gg, units, dwg_out, k)
        gate.start()
        up = tile(1, xs, gu, units, dwu_out, k)
        up.start()
        gate.wait()
        up.wait()
        stored.wait()

    @pl.loop(0, pieces)
    def _(k):
        copy(AG3_X, k).wait_recv()
        copy(AG3_F, k).start()

        @pl.when(k < 2)
        def _():
            gate = tile(0, xs, gg, units, dwg_out, 4 + k)
            gate.start()
            up = tile(1, xs, gu, units, dwu_out, 4 + k)
            up.start()
            gate.wait()
            up.wait()

        copy(AG3_C, k).wait_recv()
        copy(AG3_F, k).wait_recv()
        datt_stage[...] = dot(g[k].reshape(4 * n, width), wo[...], NT).astype(bf16).reshape(4, n, heads)
        moved = pltpu.make_async_copy(datt_stage, datt_out.at[:, k], datt_sem.at[0])
        moved.start()
        moved.wait()

    for u in range(heads // 256):
        total = None
        for p in range(4):
            left = att[p, :, :, u * 256 : (u + 1) * 256].reshape(pieces * n, 256)
            term = dot(left, g[:, p].reshape(pieces * n, width), TN)
            total = term if total is None else total + term
        tile_stage[u] = total.astype(bf16)
        pltpu.make_async_copy(tile_stage.at[u], dwo_out.at[pl.ds(u * 256, 256)], tile_sem.at[u]).start()
    for u in range(heads // 256):
        pltpu.make_async_copy(tile_stage.at[u], dwo_out.at[pl.ds(u * 256, 256)], tile_sem.at[u]).wait()

    @pl.loop(0, pieces)
    def _(k):
        part_copy(k, 2).wait()
        for kind in (AG2_X, AG2_C, AG2_F, AG3_X, AG3_C, AG3_F):
            copy(kind, k).wait_send()


def middle(attended, wo, tokens, gain, cot_own, cots, wg, wu, wd):
    width, units, heads = wg.shape[0], wg.shape[1], wo.shape[0]
    pieces = CHUNKS
    n = tokens.shape[0] // pieces
    sds = jax.ShapeDtypeStruct
    own = (pieces, n, width)
    all_rows = (pieces, 4, n, width)
    all_units = (pieces, 4, n, units)
    return pl.pallas_call(
        middle_kernel,
        in_specs=[VMEM] * 4 + [ANY] * 2 + [VMEM] * 3,
        out_specs=[VMEM] + [ANY] * 7 + [VMEM],
        out_shape=[
            sds(own, f32),
            sds((4, pieces, n, heads), bf16),
            sds(all_rows, bf16),
            sds(own, f32),
            sds((units, width), bf16),
            sds((width, units), bf16),
            sds((width, units), bf16),
            sds((heads, width), bf16),
            sds((8, width), f32),
        ],
        scratch_shapes=[
            pltpu.VMEM(all_rows, bf16),
            pltpu.VMEM(all_rows, bf16),
            pltpu.VMEM(all_units, bf16),
            pltpu.VMEM(all_units, bf16),
            pltpu.VMEM(all_units, bf16),
            pltpu.VMEM(all_rows, bf16),
            pltpu.VMEM((pieces, 2, n, width), bf16),
            pltpu.VMEM(own, bf16),
            pltpu.VMEM((pieces, 2, n, width), bf16),
            pltpu.VMEM((n, width), f32),
            pltpu.VMEM((4, n, heads), bf16),
            pltpu.VMEM((2, 256, width), bf16),
            *dma_sems(12, pieces),
            pltpu.SemaphoreType.DMA((4,)),
            pltpu.SemaphoreType.DMA((pieces,)),
            pltpu.SemaphoreType.DMA((1,)),
            pltpu.SemaphoreType.DMA((1,)),
            pltpu.SemaphoreType.DMA((2,)),
            pltpu.SemaphoreType.REGULAR((2, pieces)),
        ],
        compiler_params=comm_params(2),
        cost_estimate=cost(150e-6 * 1e15, 80e6),
        name="middle",
    )(
        attended.reshape(4, pieces, n, heads), wo, tokens.reshape(own), gain,
        cot_own.reshape(own), cots, wg, wu, wd,
    )


def end_kernel(
    dq, dk, dv, wq, wk, wv, tokens, grad_one, gain, grad_ref, gain_grad, parts, cr, xr, send_sem, recv_sem
):
    own, width = tokens.shape
    rows = own // CHUNKS
    sems = (send_sem, recv_sem)

    def at(base, k):
        return pl.ds(pl.multiple_of(base + k * rows, rows), rows)

    def term(p, k):
        here = at(p * own, k)
        return dot(dq[here], wq[...], NT) + dot(dk[here], wk[...], NT) + dot(dv[here], wv[...], NT)

    side0 = lambda k: send(parts.at[at(0, k)], cr.at[0, at(0, k)], sems, (0, k), 1)
    side1 = lambda k: send(parts.at[at(own, k)], cr.at[1, at(0, k)], sems, (1, k), 1)
    across = lambda k: send(parts.at[at(2 * own, k)], xr.at[at(0, k)], sems, (2, k), 2)

    meet()

    @pl.loop(0, CHUNKS)
    def _(k):
        parts[at(0, k)] = term(3, k).astype(bf16)
        side0(k).start()
        mine = term(2, k)
        side0(k).wait_recv()
        parts[at(2 * own, k)] = (mine + cr[0, at(0, k)].astype(f32)).astype(bf16)
        across(k).start()

    @pl.loop(0, CHUNKS)
    def _(k):
        parts[at(own, k)] = term(1, k).astype(bf16)
        side1(k).start()
        grad_ref[at(0, k)] = term(0, k)

    @pl.loop(0, CHUNKS)
    def _(k):
        side1(k).wait_recv()
        across(k).wait_recv()
        here = at(0, k)
        grad = grad_ref[here] + cr[1, here].astype(f32) + xr[here].astype(f32)
        inputs = tokens[here].astype(f32)
        inverse = lax.rsqrt(jnp.mean(inputs * inputs, axis=-1, keepdims=True) + epsilon)
        unit = inputs * inverse
        scaled = grad * gain[...]
        grad_ref[here] = grad_one[here] + inverse * (scaled - unit * jnp.mean(scaled * unit, axis=-1, keepdims=True))
        sums = jnp.sum((grad * unit).reshape(-1, 8, width), axis=0)

        @pl.when(k == 0)
        def _():
            gain_grad[...] = sums

        @pl.when(k > 0)
        def _():
            gain_grad[...] += sums

    @pl.loop(0, CHUNKS)
    def _(k):
        side0(k).wait_send()
        side1(k).wait_send()
        across(k).wait_send()


def end(dq, dk, dv, wq, wk, wv, tokens, grad_one, gain):
    own, width = tokens.shape
    return pl.pallas_call(
        end_kernel,
        in_specs=[VMEM] * 9,
        out_specs=[VMEM] * 2,
        out_shape=[jax.ShapeDtypeStruct((own, width), f32), jax.ShapeDtypeStruct((8, width), f32)],
        scratch_shapes=[
            pltpu.VMEM((3 * own, width), bf16),
            pltpu.VMEM((2, own, width), bf16),
            pltpu.VMEM((own, width), bf16),
            *dma_sems(3, CHUNKS),
        ],
        compiler_params=comm_params(3),
        cost_estimate=cost(50e-6 * 1e15, 30e6),
        name="end",
    )(dq, dk, dv, wq, wk, wv, tokens, grad_one, gain)


def spread(heads):
    col = lax.broadcasted_iota(jnp.int32, (heads * HEAD_SIZE, heads * LANES), 1)
    row = lax.broadcasted_iota(jnp.int32, (heads * HEAD_SIZE, heads * LANES), 0)
    half, feature = row // HALF, row % HALF
    return (col == half * (LANES // 2) + feature).astype(bf16)


def body(
    tokens, segments, positions, norm_attn, w_query, key_weight, value_weight, w_out,
    norm_mlp, w_gate, w_up, w_down, cotangent,
):
    seq = segments.shape[0]
    own, width = tokens.shape
    me = lax.axis_index("tensor")
    order = me ^ jnp.arange(4, dtype=jnp.int32)
    blocks = 4

    starts = jnp.zeros_like(segments)
    for document in (1, 2, 3):
        first = jnp.sum((segments < document).astype(jnp.int32))
        starts = jnp.where(segments >= document, first, starts)
    start = jnp.take(starts.reshape(4, own), order, axis=0).reshape(1, seq)
    places = jnp.take(positions.reshape(4, own), order, axis=0).reshape(seq)
    lane = jnp.arange(LANES // 2)
    inverse = jnp.exp(lane.astype(f32) * (-2.0 * math.log(rope_base) / HEAD_SIZE))
    angles = places.astype(f32)[:, None] * jnp.where(lane < HALF, inverse, 0.0)[None, :]
    cos, sin = jnp.cos(angles), jnp.sin(angles)
    cos = jnp.concatenate([cos, cos], 1)
    sin = jnp.concatenate([-sin, sin], 1)

    spread_q, spread_k = spread(w_query.shape[1] // HEAD_SIZE), spread(key_weight.shape[1] // HEAD_SIZE)
    wq = dot(w_query, spread_q).astype(bf16)
    wk = dot(key_weight, spread_k).astype(bf16)
    wv = dot(value_weight, spread_k).astype(bf16)
    wo = dot(spread_q, w_out, TN).astype(bf16)
    gain_attn, gain_mlp = norm_attn.reshape(1, width), norm_mlp.reshape(1, width)

    inputs = tokens.astype(f32)
    inverse_one = lax.rsqrt(jnp.mean(inputs * inputs, axis=-1, keepdims=True) + epsilon)
    normed_one = (inputs * inverse_one * norm_attn).astype(bf16)

    qkv, attn_in = project_qkv(normed_one, wq, wk, wv, cos, sin)
    attended, lse, cots = attend(qkv, start, cotangent, blocks)
    hid1, grad_attended, parts, grad_one, dwd, dwg, dwu, dwo, gain_two_grad = middle(
        attended, wo, tokens, gain_mlp, cotangent, cots, w_gate, w_up, w_down
    )
    grad_attended = grad_attended.reshape(seq, -1)
    dq, dk, dv, output = attend_back(
        qkv, attended, grad_attended, lse, start, cos, sin, parts, hid1, blocks
    )
    output = output.reshape(own, width)
    attn_in = attn_in.reshape(seq, width)
    grad_w_down, grad_w_gate, grad_w_up = dp_sum(dwd), dp_sum(dwg), dp_sum(dwu)
    grad_w_out = dp_sum(dot(spread_q, dwo).astype(bf16))
    grad_w_query = dp_sum(dot(attn_in, dot(dq, spread_q, NT).astype(bf16), TN).astype(bf16))
    grad_w_key = dp_sum(dot(attn_in, dot(dk, spread_k, NT).astype(bf16), TN).astype(bf16))
    grad_w_value = dp_sum(dot(attn_in, dot(dv, spread_k, NT).astype(bf16), TN).astype(bf16))
    grad_tokens, gain_one_grad = end(dq, dk, dv, wq, wk, wv, tokens, grad_one.reshape(own, width), gain_attn)

    gains = jnp.stack([jnp.sum(gain_one_grad, 0), jnp.sum(gain_two_grad, 0)])
    gains = all_sum(gains)
    return (
        output, grad_tokens, gains[0], grad_w_query, grad_w_key, grad_w_value, grad_w_out,
        gains[1], grad_w_gate, grad_w_up, grad_w_down,
    )


def solution(mesh):
    rows, cols, both = P("tensor", None), P(None, "tensor"), P(("dp", "tensor"), None)
    in_specs = (both, P("dp"), P("dp"), P(), cols, cols, cols, rows, P(), cols, cols, rows, both)
    out_specs = (both, both, P(), cols, cols, cols, rows, P(), cols, cols, rows)
    return jax.shard_map(body, mesh=mesh, in_specs=in_specs, out_specs=out_specs, check_vma=False)
```

```python
import functools
import math

import jax
import jax.numpy as jnp
from jax import lax
from jax.experimental import pallas as pl
from jax.experimental.pallas import tpu as pltpu
from jax.sharding import PartitionSpec as P

HEAD_SIZE = 96
HALF = HEAD_SIZE // 2
LANES = 128
epsilon = 1e-05
rope_base = 100000.0
masked_value = -1e30
score_scale = 1.0 / math.sqrt(HEAD_SIZE)
log2_e = math.log2(math.e)
bf16, f32 = jnp.bfloat16, jnp.float32
NN = (((1,), (0,)), ((), ()))
NT = (((1,), (1,)), ((), ()))
TN = (((0,), (0,)), ((), ()))
VMEM_LIMIT = 67043328
CHUNKS = 4


def dot(left, right, dims=NN):
    return lax.dot_general(left, right, dims, preferred_element_type=f32)


def params():
    return pltpu.CompilerParams(vmem_limit_bytes=VMEM_LIMIT)


def cost(flops, nbytes):
    return pl.CostEstimate(flops=int(flops), bytes_accessed=int(nbytes), transcendentals=0)


def whole(shape):
    return pl.BlockSpec(shape, lambda *_: (0,) * len(shape), pipeline_mode=pl.Buffered(1))


ANY = pl.BlockSpec(memory_space=pl.ANY)
VMEM = pl.BlockSpec(memory_space=pltpu.VMEM)


def peer(bits):
    me = lax.axis_index("tensor")
    low, high = lax.rem(me, 2), lax.div(me, 2)
    if bits % 2:
        low = 1 - low
    if bits // 2:
        high = 1 - high
    return 2 * high + low


def partner(bits):
    return {"tensor": peer(bits)}


def send(source, target, sems, at, bits):
    return pltpu.make_async_remote_copy(
        src_ref=source,
        dst_ref=target,
        send_sem=sems[0].at[at],
        recv_sem=sems[1].at[at],
        device_id=partner(bits),
        device_id_type=pl.DeviceIdType.MESH,
    )


def meet(*others):
    barrier = pltpu.get_barrier_semaphore()
    for other in others:
        pl.semaphore_signal(barrier, inc=1, device_id=other, device_id_type=pl.DeviceIdType.MESH)
    pl.semaphore_wait(barrier, len(others))


RING = 8
EARLY = 4


def ring_place():
    index = lax.axis_index("dp")
    deep, wide = lax.div(index, 2), lax.rem(index, 2)
    return deep + wide * (RING - 1 - 2 * deep)


def ring_peer(way):
    place = lax.rem(ring_place() + (1, RING - 1)[way], RING)
    wide = lax.div(place, RING // 2)
    return {"dp": 2 * (place + wide * (RING - 1 - 2 * place)) + wide}


def ring_chunk(way, step):
    return lax.rem(ring_place() + (2 * RING - step if way == 0 else step), RING)


def ring_send(source, target, sems, at, way):
    return pltpu.make_async_remote_copy(
        src_ref=source,
        dst_ref=target,
        send_sem=sems[0].at[at],
        recv_sem=sems[1].at[at],
        device_id=ring_peer(way),
        device_id_type=pl.DeviceIdType.MESH,
    )


class Reduce:
    def __init__(self, parts, state, land, mine, first, last, send_sem, recv_sem, load_sem):
        self.parts, self.state, self.land, self.mine = parts, state, land, mine
        self.first, self.last, self.sems, self.load_sem = first, last, (send_sem, recv_sem), load_sem

    def begin(self, way):
        source = self.parts.at[way, ring_chunk(way, 0)] if self.state is None else self.state.at[way]
        return ring_send(source, self.land.at[way, 0], self.sems, (way, 0), way)

    def copy(self, way, k):
        return ring_send(self.land.at[way, k - 1], self.land.at[way, k], self.sems, (way, k), way)

    def load(self, way, k):
        source = self.parts.at[way, ring_chunk(way, self.first + k + 1)]
        return pltpu.make_async_copy(source, self.mine.at[way, k], self.load_sem.at[way, k])

    def start(self):
        for way in range(2):
            self.begin(way).start()

    def prefetch(self):
        for k in range(self.last - self.first):
            for way in range(2):
                self.load(way, k).start()

    def step(self, k):
        for way in range(2):
            self.landed(way, k)
            if self.mine is None:
                own = self.parts[way, ring_chunk(way, self.first + k + 1)]
            else:
                self.load(way, k).wait()
                own = self.mine[way, k]
            self.land[way, k] = (self.land[way, k].astype(f32) + own.astype(f32)).astype(bf16)
            if isinstance(k, int):
                if k + 1 < self.last - self.first:
                    self.copy(way, k + 1).start()
            else:

                @pl.when(k + 1 < self.last - self.first)
                def _():
                    self.copy(way, k + 1).start()

    def landed(self, way, k):
        ring_send(self.land.at[way, k], self.land.at[way, k], self.sems, (way, k), way).wait_recv()

    def finish(self):
        for way in range(2):
            self.begin(way).wait_send()
            for k in range(1, self.last - self.first):
                self.copy(way, k).wait_send()


class Spread:
    def __init__(self, reduced, full, send_sem, recv_sem, own_sem):
        self.reduced, self.full, self.sems, self.own_sem = reduced, full, (send_sem, recv_sem), own_sem

    def slot(self, way, step):
        return self.full.at[way, ring_chunk(way, step + RING - 1)]

    def begin(self, way):
        last = self.reduced.last - self.reduced.first - 1
        return ring_send(self.reduced.land.at[way, last], self.slot(way, 0), self.sems, (way, 0), way)

    def keep(self, way):
        last = self.reduced.last - self.reduced.first - 1
        return pltpu.make_async_copy(self.reduced.land.at[way, last], self.slot(way, 0), self.own_sem.at[way])

    def start(self):
        for way in range(2):
            self.begin(way).start()
            self.keep(way).start()

    def copy(self, way, k):
        return ring_send(self.slot(way, k), self.slot(way, k), self.sems, (way, k), way)

    def step(self, k):
        for way in range(2):
            ring_send(self.slot(way, k + 1), self.slot(way, k + 1), self.sems, (way, k), way).wait_recv()

            @pl.when(k < RING - 2)
            def _():
                self.copy(way, k + 1).start()

    def finish(self):
        for way in range(2):
            self.begin(way).wait_send()
            self.keep(way).wait()
            for k in range(1, RING - 1):
                self.copy(way, k).wait_send()


def ring_scratch(shape, steps, loads):
    rows, cols = shape[2:]
    land = pltpu.VMEM((2, steps, rows, cols), bf16)
    sems = [pltpu.SemaphoreType.DMA((2, steps))] * (3 if loads else 2)
    return [land] * (2 if loads else 1) + sems


def comm_params(number):
    return pltpu.CompilerParams(vmem_limit_bytes=VMEM_LIMIT, collective_id=number, has_side_effects=True)


def dma_sems(*shape):
    return [pltpu.SemaphoreType.DMA(shape)] * 2


def qkv_kernel(x_ref, wq, wk, wv, cos_ref, sin_ref, qkv_ref, stack_ref, land, send_sem, recv_sem, out_sem):
    sems = (send_sem, recv_sem)
    own = x_ref.shape[0]
    rows = own // CHUNKS
    lane = lax.broadcasted_iota(jnp.int32, (rows, LANES), 1)

    def project(ref, base):
        x = ref[...]
        cos, sin = cos_ref[pl.ds(base, rows), :], sin_ref[pl.ds(base, rows), :]
        for w, first, turn in ((wq, 0, True), (wk, 4, True), (wv, 6, False)):
            y = dot(x, w[...])
            for h in range(w.shape[1] // LANES):
                v = y[:, h * LANES : (h + 1) * LANES]
                if turn:
                    v = v * cos + pltpu.roll(v, LANES // 2, 1) * sin
                else:
                    v = jnp.where(lane == HALF, 1.0, v)
                at = (first + h) * LANES
                qkv_ref[pl.ds(base, rows), at : at + LANES] = v.astype(bf16)

    def piece(k):
        return pl.ds(pl.multiple_of(k * rows, rows), rows)

    side = send(x_ref, land.at[0], sems, 2 * CHUNKS, 1)
    across = lambda k: send(x_ref.at[piece(k)], land.at[1, piece(k)], sems, k, 2)
    onward = lambda k: send(land.at[1, piece(k)], land.at[2, piece(k)], sems, CHUNKS + k, 1)
    store = lambda p: pltpu.make_async_copy(x_ref if p == 0 else land.at[p - 1], stack_ref.at[p], out_sem.at[p])

    meet(partner(1), partner(2))
    side.start()
    for k in range(CHUNKS):
        across(k).start()
    store(0).start()

    @pl.loop(0, CHUNKS)
    def _(k):
        project(x_ref.at[piece(k)], pl.multiple_of(k * rows, rows))

    side.wait_recv()
    store(1).start()

    @pl.loop(0, CHUNKS)
    def _(k):
        project(land.at[0, piece(k)], pl.multiple_of(own + k * rows, rows))

    @pl.loop(0, CHUNKS)
    def _(k):
        across(k).wait_recv()
        onward(k).start()
        project(land.at[1, piece(k)], pl.multiple_of(2 * own + k * rows, rows))
        onward(k).wait_recv()
        project(land.at[2, piece(k)], pl.multiple_of(3 * own + k * rows, rows))

    store(2).start()
    store(3).start()
    side.wait_send()
    for k in range(CHUNKS):
        across(k).wait_send()
        onward(k).wait_send()
    for p in range(4):
        store(p).wait()


def project_qkv(x, wq, wk, wv, cos, sin):
    own, width = x.shape
    return pl.pallas_call(
        qkv_kernel,
        in_specs=[VMEM] * 6,
        out_specs=[VMEM, ANY],
        out_shape=[jax.ShapeDtypeStruct((4 * own, 8 * LANES), bf16), jax.ShapeDtypeStruct((4, own, width), bf16)],
        scratch_shapes=[pltpu.VMEM((3, own, width), bf16), *dma_sems(2 * CHUNKS + 1), pltpu.SemaphoreType.DMA((4,))],
        compiler_params=comm_params(1),
        cost_estimate=cost(40e-6 * 1e15, 20e6),
        name="gather_project_qkv",
    )(x, wq, wk, wv, cos, sin)


def attend_kernel(
    q_ref, k_ref, v_ref, start_ref, cot_ref, o_ref, lse_ref, cots_ref, send_sem, recv_sem, *, blocks, size
):
    sems = (send_sem, recv_sem)
    side = send(cot_ref, cots_ref.at[0], sems, 2 * CHUNKS, 1)
    across = lambda k: send(cot_ref.at[k], cots_ref.at[1, k], sems, k, 2)
    onward = lambda k: send(cots_ref.at[1, k], cots_ref.at[2, k], sems, CHUNKS + k, 1)

    @pl.when(pl.program_id(0) == 0)
    def _():
        meet(partner(1), partner(2))
        side.start()
        for k in range(CHUNKS):
            across(k).start()

    for i in range(blocks):
        at = pl.multiple_of(peer(i) * size, size)
        queries = [q_ref[pl.ds(at, size), r * LANES : (r + 1) * LANES] for r in range(2)]
        start = start_ref[:, pl.ds(at, size)]
        state = [None, None]
        for j in [i, *range(i)]:
            key_at = pl.multiple_of(peer(j) * size, size)
            keys = k_ref[pl.ds(key_at, size), :]
            values = v_ref[pl.ds(key_at, size), :]
            key_rows = lax.broadcasted_iota(jnp.int32, (size, size), 0)
            allowed = key_rows >= start - j * size
            if j == i:
                allowed &= key_rows <= lax.broadcasted_iota(jnp.int32, (size, size), 1)
            for r in range(2):
                scores = jnp.where(allowed, dot(keys, queries[r], NT) * (score_scale * log2_e), masked_value)
                peak = jnp.max(scores, axis=0, keepdims=True)
                if state[r] is not None:
                    peak = jnp.maximum(state[r][0], peak)
                weights = jnp.exp2(scores - peak)
                mixed = dot(values, weights.astype(bf16), TN)
                if state[r] is not None:
                    mixed += state[r][1] * jnp.exp2(state[r][0] - peak)
                state[r] = (peak, mixed)
        for r, (peak, mixed) in enumerate(state):
            total = mixed[HALF : HALF + 1, :]
            o_ref[pl.ds(at, size), r * LANES : (r + 1) * LANES] = (mixed / total).T.astype(bf16)
            lse_ref[0, r : r + 1, pl.ds(at, size)] = peak + jnp.log2(total)

    @pl.when(pl.program_id(0) == 1)
    def _():
        for k in range(CHUNKS):
            across(k).wait_recv()
            onward(k).start()
        side.wait()
        for k in range(CHUNKS):
            across(k).wait_send()
            onward(k).wait()


def attend(qkv, start, cot, blocks):
    seq = qkv.shape[0]
    own, width = cot.shape
    pieces = (CHUNKS, own // CHUNKS, width)
    flops = 2 * 2 * 4 * LANES * seq * seq
    return pl.pallas_call(
        functools.partial(attend_kernel, blocks=blocks, size=seq // blocks),
        grid=(2,),
        in_specs=[
            pl.BlockSpec((seq, 2 * LANES), lambda g: (0, g)),
            pl.BlockSpec((seq, LANES), lambda g: (0, 4 + g)),
            pl.BlockSpec((seq, LANES), lambda g: (0, 6 + g)),
            pl.BlockSpec((1, seq), lambda g: (0, 0)),
            ANY,
        ],
        out_specs=[
            pl.BlockSpec((seq, 2 * LANES), lambda g: (0, g)),
            pl.BlockSpec((1, 2, seq), lambda g: (g, 0, 0)),
            ANY,
        ],
        scratch_shapes=dma_sems(2 * CHUNKS + 1),
        out_shape=[
            jax.ShapeDtypeStruct((seq, 4 * LANES), bf16),
            jax.ShapeDtypeStruct((2, 2, seq), f32),
            jax.ShapeDtypeStruct((3, *pieces), bf16),
        ],
        compiler_params=comm_params(4),
        cost_estimate=cost(flops, 6 * seq * 8 * LANES),
        name="attention",
    )(qkv, qkv, qkv, start, cot.reshape(pieces))


def attend_back_kernel(count, *refs, blocks, size):
    q_ref, k_ref, v_ref, o_ref, do_ref, lse_ref, start_ref, cos_ref, sin_ref, *rest = refs
    parts, rest = rest[:count], rest[count:]
    dq_ref, dk_ref, dv_ref, *rest = rest
    states, rest = rest[:count], rest[count:]
    dq_sum, dk_sum, dv_sum, inner, *rest = rest
    rings = [Reduce(p, None, *rest[5 * a : 5 * a + 2], 0, EARLY, *rest[5 * a + 2 : 5 * a + 5]) for a, p in enumerate(parts)]
    keep_sem = rest[-1] if count else None

    def keep(a, way):
        return pltpu.make_async_copy(rings[a].land.at[way, EARLY - 1], states[a].at[way], keep_sem.at[a, way])

    if count:

        @pl.when(pl.program_id(0) == 0)
        def _():
            meet(ring_peer(0), ring_peer(1))
            for ring in rings:
                ring.start()
            for ring in rings:
                ring.prefetch()

    pairs = blocks * (blocks + 1) // 2
    hooks = {}
    for number in range(count * EARLY):
        hooks[min(round((number + 1) * 2.2) + 1, 2 * pairs - 1)] = hooks.get(min(round((number + 1) * 2.2) + 1, 2 * pairs - 1), []) + [
            (number % count, number // count)
        ]

    def hook(pair):
        for half in range(2):
            todo = hooks.get(half * pairs + pair, [])
            if todo:

                @pl.when(pl.program_id(0) == half)
                def _():
                    for a, k in todo:
                        rings[a].step(k)
                        if k == EARLY - 1:
                            keep(a, 0).start()
                            keep(a, 1).start()

    for c in range(blocks):
        rows = slice(c * size, (c + 1) * size)
        for r in range(2):
            cols = slice(r * LANES, (r + 1) * LANES)
            product = do_ref[rows, cols].astype(f32) * o_ref[rows, cols].astype(f32)
            inner[r : r + 1, rows] = jnp.sum(product.T, axis=0, keepdims=True)
    for i in reversed(range(blocks)):
        for j in [i, *range(i)]:
            at = pl.multiple_of(peer(i) * size, size)
            key_at = pl.multiple_of(peer(j) * size, size)
            keys = k_ref[pl.ds(key_at, size), :]
            values = v_ref[pl.ds(key_at, size), :]
            start = start_ref[:, pl.ds(at, size)]
            key_rows = lax.broadcasted_iota(jnp.int32, (size, size), 0)
            allowed = key_rows >= start - j * size
            if j == i:
                allowed &= key_rows <= lax.broadcasted_iota(jnp.int32, (size, size), 1)
            dk = dv = None
            for r in range(2):
                cols = slice(r * LANES, (r + 1) * LANES)
                queries = q_ref[pl.ds(at, size), cols]
                grads = do_ref[pl.ds(at, size), cols]
                scores = jnp.where(allowed, dot(keys, queries, NT) * (score_scale * log2_e), masked_value)
                weights = jnp.exp2(scores - lse_ref[0, r : r + 1, pl.ds(at, size)])
                grad_weights = dot(values, grads, NT)
                grad_scores = (weights * (grad_weights - inner[r : r + 1, pl.ds(at, size)])).astype(bf16)
                dv_term = dot(weights.astype(bf16), grads)
                dk_term = dot(grad_scores, queries)
                dv = dv_term if dv is None else dv + dv_term
                dk = dk_term if dk is None else dk + dk_term
                dq = dot(grad_scores, keys, TN)
                if j == i:
                    dq_sum[pl.ds(at, size), cols] = dq
                else:
                    dq_sum[pl.ds(at, size), cols] += dq
            if i == blocks - 1:
                dk_sum[pl.ds(key_at, size), :] = dk
                dv_sum[pl.ds(key_at, size), :] = dv
            else:
                dk_sum[pl.ds(key_at, size), :] += dk
                dv_sum[pl.ds(key_at, size), :] += dv
            hook(sum(range(blocks, i + 1, -1)) + (0 if j == i else j + 1))
    for c in range(blocks):
        rows = slice(c * size, (c + 1) * size)
        cos, sin = cos_ref[rows, :], sin_ref[rows, :]

        def back(grads):
            return ((grads * cos - pltpu.roll(grads, LANES // 2, 1) * sin) * score_scale).astype(bf16)

        for r in range(2):
            cols = slice(r * LANES, (r + 1) * LANES)
            dq_ref[rows, cols] = back(dq_sum[rows, cols])
        dk_ref[rows, :] = back(dk_sum[rows, :])
        dv_ref[rows, :] = dv_sum[rows, :].astype(bf16)

    if count:

        @pl.when(pl.program_id(0) == 1)
        def _():
            for a, ring in enumerate(rings):
                ring.finish()
                keep(a, 0).wait()
                keep(a, 1).wait()


def attend_back(qkv, attended, grads, lse, start, cos, sin, parts, blocks):
    seq = qkv.shape[0]
    pair = pl.BlockSpec((seq, 2 * LANES), lambda g: (0, g))
    single = pl.BlockSpec((seq, LANES), lambda g: (0, g))
    table = pl.BlockSpec((seq, LANES), lambda g: (0, 0))
    count = len(parts)
    outs = pl.pallas_call(
        functools.partial(attend_back_kernel, count, blocks=blocks, size=seq // blocks),
        grid=(2,),
        in_specs=[
            pair,
            pl.BlockSpec((seq, LANES), lambda g: (0, 4 + g)),
            pl.BlockSpec((seq, LANES), lambda g: (0, 6 + g)),
            pair,
            pair,
            pl.BlockSpec((1, 2, seq), lambda g: (g, 0, 0)),
            pl.BlockSpec((1, seq), lambda g: (0, 0)),
            table,
            table,
            *[ANY] * count,
        ],
        out_specs=[pair, single, single, *[ANY] * count],
        scratch_shapes=[
            pltpu.VMEM((seq, 2 * LANES), f32),
            pltpu.VMEM((seq, LANES), f32),
            pltpu.VMEM((seq, LANES), f32),
            pltpu.VMEM((2, seq), f32),
            *[x for p in parts for x in ring_scratch(p.shape, EARLY, True)],
            *[pltpu.SemaphoreType.DMA((count, 2))] * bool(count),
        ],
        out_shape=[
            jax.ShapeDtypeStruct((seq, 4 * LANES), bf16),
            jax.ShapeDtypeStruct((seq, 2 * LANES), bf16),
            jax.ShapeDtypeStruct((seq, 2 * LANES), bf16),
            *[jax.ShapeDtypeStruct((2, *p.shape[2:]), bf16) for p in parts],
        ],
        compiler_params=comm_params(5) if count else params(),
        cost_estimate=cost(5 * 2 * 4 * LANES * seq * seq, 10 * seq * 8 * LANES),
        name="attention_back",
    )(qkv, qkv, qkv, attended, grads, lse, start, cos, sin, *parts)
    return outs[:3], outs[3:]


RS1_C0, RS1_C1, RS1_X, AG2_X, AG2_C, AG2_F, RS3_C0, RS3_C1, RS3_X, AG3_X, AG3_C, AG3_F = range(12)


def middle_kernel(
    att, wo, tokens, gain, cot_own, cots, wg, wu, wd,
    hid1, datt_out, parts_out, grad_one_out, dwd_out, dwg_out, dwu_out, dwo_out, gain_grad,
    xs, cot, hid, gg, gu, g, cr, xr, part_stage, grad_stage, datt_stage, tile_stage,
    send_sem, recv_sem, cot_sem, part_sem, grad_sem, datt_sem, tile_sem, free_sem,
):
    pieces, _, n, width = xs.shape
    units = wg.shape[1]
    heads = wo.shape[0]
    sems = (send_sem, recv_sem)
    two = (2 * n, width)

    def copy(kind, k):
        source, target, bits = {
            RS1_C0: (g.at[k, 3], cr.at[k, 0], 1),
            RS1_C1: (g.at[k, 1], cr.at[k, 1], 1),
            RS1_X: (g.at[k, 2], xr.at[k], 2),
            AG2_X: (xs.at[k, 0], xs.at[k, 2], 2),
            AG2_C: (xs.at[k, 0], xs.at[k, 1], 1),
            AG2_F: (xs.at[k, 2], xs.at[k, 3], 1),
            RS3_C0: (g.at[k, 3], cr.at[k, 0], 1),
            RS3_C1: (g.at[k, 1], cr.at[k, 1], 1),
            RS3_X: (g.at[k, 2], xr.at[k], 2),
            AG3_X: (g.at[k, 0], g.at[k, 2], 2),
            AG3_C: (g.at[k, 0], g.at[k, 1], 1),
            AG3_F: (g.at[k, 2], g.at[k, 3], 1),
        }[kind]
        return send(source, target, sems, (kind, k), bits)

    def credit(k, bits):
        pl.semaphore_signal(
            free_sem.at[bits - 1, k], inc=1, device_id=partner(bits), device_id_type=pl.DeviceIdType.MESH
        )

    def cot_copy(p):
        source = cot_own if p == 0 else cots.at[p - 1]
        return pltpu.make_async_copy(source, cot.at[:, p], cot_sem.at[p])

    def part_copy(k, low):
        return pltpu.make_async_copy(part_stage.at[k], parts_out.at[k, pl.ds(low, 2)], part_sem.at[k])

    for p in range(4):
        cot_copy(p).start()
    meet(partner(1), partner(2))

    @pl.loop(0, pieces)
    def _(k):
        for p, kind in ((3, RS1_C0), (1, RS1_C1)):
            g[k, p] = dot(att[p, k], wo[...]).astype(bf16)
            copy(kind, k).start()

    @pl.loop(0, pieces)
    def _(k):
        term = dot(att[2, k], wo[...])
        copy(RS1_C0, k).wait_recv()
        g[k, 2] = (term + cr[k, 0].astype(f32)).astype(bf16)
        copy(RS1_X, k).start()

    def feed_forward(k, low):
        x = xs[k, pl.ds(low, 2)].reshape(two)
        gate = dot(x, wg[...])
        up = dot(x, wu[...])
        grad_hidden = dot(cot[k, pl.ds(low, 2)].reshape(two), wd[...], NT)
        sig = jax.nn.sigmoid(gate)
        act = gate * sig
        hidden = (act * up).astype(bf16)
        grad_gate = (grad_hidden * up * sig * (1.0 + gate * (1.0 - sig))).astype(bf16)
        grad_up = (grad_hidden * act).astype(bf16)
        hid[k, pl.ds(low, 2)] = hidden.reshape(2, n, units)
        gg[k, pl.ds(low, 2)] = grad_gate.reshape(2, n, units)
        gu[k, pl.ds(low, 2)] = grad_up.reshape(2, n, units)
        back = dot(grad_gate, wg[...], NT) + dot(grad_up, wu[...], NT)
        g[k, pl.ds(low, 2)] = back.astype(bf16).reshape(2, n, width)
        return hidden

    def out_part(k, low, hidden):
        part_stage[k] = dot(hidden, wd[...]).astype(bf16).reshape(2, n, width)
        part_copy(k, low).start()

    for p in range(4):
        cot_copy(p).wait()

    @pl.loop(0, pieces)
    def _(k):
        term = dot(att[0, k], wo[...])
        copy(RS1_C1, k).wait_recv()
        copy(RS1_X, k).wait_recv()
        hidden = tokens[k].astype(f32) + (term + cr[k, 1].astype(f32) + xr[k].astype(f32))
        hid1[k] = hidden
        inverse = lax.rsqrt(jnp.mean(hidden * hidden, axis=-1, keepdims=True) + epsilon)
        xs[k, 0] = (hidden * inverse * gain[...]).astype(bf16)
        copy(AG2_X, k).start()
        copy(AG2_C, k).start()
        copy(AG2_C, k).wait_recv()
        copy(RS1_C1, k).wait_send()
        out_part(k, 0, feed_forward(k, 0))

    @pl.loop(0, pieces)
    def _(k):
        copy(AG2_X, k).wait_recv()
        copy(AG2_F, k).start()
        part_copy(k, 0).wait()
        copy(AG2_F, k).wait_recv()
        copy(RS1_C0, k).wait_send()
        copy(RS1_X, k).wait_send()
        hidden = feed_forward(k, 2)
        copy(RS3_C0, k).start()
        copy(RS3_C1, k).start()
        out_part(k, 2, hidden)
        copy(RS3_C0, k).wait_recv()
        g[k, 2] = (g[k, 2].astype(f32) + cr[k, 0].astype(f32)).astype(bf16)
        copy(RS3_X, k).start()

    tokens_all = 4 * pieces * n

    def tile(slot, left, right, cols, out, at):
        height = out.shape[1]
        target = out.at[pl.ds(pl.multiple_of(at * 256, 256), 256)]
        move = pltpu.make_async_copy(tile_stage.at[slot, :, pl.ds(0, height)], target, tile_sem.at[slot])
        part = left[:, :, :, pl.ds(pl.multiple_of(at * 256, 256), 256)].reshape(tokens_all, 256)
        tile_stage[slot, :, pl.ds(0, height)] = dot(part, right[...].reshape(tokens_all, cols), TN).astype(bf16)
        return move

    @pl.loop(0, 4)
    def _(k):
        down = tile(0, hid, cot, width, dwd_out, k)
        down.start()
        copy(RS3_C1, k).wait_recv()
        copy(RS3_X, k).wait_recv()
        copy(RS3_C0, k).wait_send()
        copy(RS3_C1, k).wait_send()
        credit(k, 1)
        copy(RS3_X, k).wait_send()
        credit(k, 2)
        grad = g[k, 0].astype(f32) + cr[k, 1].astype(f32) + xr[k].astype(f32)
        hidden = hid1[k]
        inverse = lax.rsqrt(jnp.mean(hidden * hidden, axis=-1, keepdims=True) + epsilon)
        unit = hidden * inverse
        scaled = grad * gain[...]
        result = cot[k, 0].astype(f32) + inverse * (scaled - unit * jnp.mean(scaled * unit, axis=-1, keepdims=True))
        g[k, 0] = result.astype(bf16)
        pl.semaphore_wait(free_sem.at[0, k], 1)
        pl.semaphore_wait(free_sem.at[1, k], 1)
        copy(AG3_X, k).start()
        copy(AG3_C, k).start()
        grad_stage[...] = result
        stored = pltpu.make_async_copy(grad_stage, grad_one_out.at[k], grad_sem.at[0])
        stored.start()
        sums = jnp.sum((grad * unit).reshape(-1, 8, width), axis=0)

        @pl.when(k == 0)
        def _():
            gain_grad[...] = sums

        @pl.when(k > 0)
        def _():
            gain_grad[...] += sums

        down.wait()
        gate = tile(0, xs, gg, units, dwg_out, k)
        gate.start()
        up = tile(1, xs, gu, units, dwu_out, k)
        up.start()
        gate.wait()
        up.wait()
        stored.wait()

    @pl.loop(0, pieces)
    def _(k):
        copy(AG3_X, k).wait_recv()
        copy(AG3_F, k).start()

        @pl.when(k < 2)
        def _():
            gate = tile(0, xs, gg, units, dwg_out, 4 + k)
            gate.start()
            up = tile(1, xs, gu, units, dwu_out, 4 + k)
            up.start()
            gate.wait()
            up.wait()

        copy(AG3_C, k).wait_recv()
        copy(AG3_F, k).wait_recv()
        datt_stage[...] = dot(g[k].reshape(4 * n, width), wo[...], NT).astype(bf16).reshape(4, n, heads)
        moved = pltpu.make_async_copy(datt_stage, datt_out.at[:, k], datt_sem.at[0])
        moved.start()
        moved.wait()

    for u in range(heads // 256):
        total = None
        for p in range(4):
            left = att[p, :, :, u * 256 : (u + 1) * 256].reshape(pieces * n, 256)
            term = dot(left, g[:, p].reshape(pieces * n, width), TN)
            total = term if total is None else total + term
        tile_stage[u] = total.astype(bf16)
        pltpu.make_async_copy(tile_stage.at[u], dwo_out.at[pl.ds(u * 256, 256)], tile_sem.at[u]).start()
    for u in range(heads // 256):
        pltpu.make_async_copy(tile_stage.at[u], dwo_out.at[pl.ds(u * 256, 256)], tile_sem.at[u]).wait()

    @pl.loop(0, pieces)
    def _(k):
        part_copy(k, 2).wait()
        for kind in (AG2_X, AG2_C, AG2_F, AG3_X, AG3_C, AG3_F):
            copy(kind, k).wait_send()


def middle(attended, wo, tokens, gain, cot_own, cots, wg, wu, wd):
    width, units, heads = wg.shape[0], wg.shape[1], wo.shape[0]
    pieces = CHUNKS
    n = tokens.shape[0] // pieces
    sds = jax.ShapeDtypeStruct
    own = (pieces, n, width)
    all_rows = (pieces, 4, n, width)
    all_units = (pieces, 4, n, units)
    return pl.pallas_call(
        middle_kernel,
        in_specs=[VMEM] * 4 + [ANY] * 2 + [VMEM] * 3,
        out_specs=[VMEM] + [ANY] * 7 + [VMEM],
        out_shape=[
            sds(own, f32),
            sds((4, pieces, n, heads), bf16),
            sds(all_rows, bf16),
            sds(own, f32),
            sds((units, width), bf16),
            sds((width, units), bf16),
            sds((width, units), bf16),
            sds((heads, width), bf16),
            sds((8, width), f32),
        ],
        scratch_shapes=[
            pltpu.VMEM(all_rows, bf16),
            pltpu.VMEM(all_rows, bf16),
            pltpu.VMEM(all_units, bf16),
            pltpu.VMEM(all_units, bf16),
            pltpu.VMEM(all_units, bf16),
            pltpu.VMEM(all_rows, bf16),
            pltpu.VMEM((pieces, 2, n, width), bf16),
            pltpu.VMEM(own, bf16),
            pltpu.VMEM((pieces, 2, n, width), bf16),
            pltpu.VMEM((n, width), f32),
            pltpu.VMEM((4, n, heads), bf16),
            pltpu.VMEM((2, 256, width), bf16),
            *dma_sems(12, pieces),
            pltpu.SemaphoreType.DMA((4,)),
            pltpu.SemaphoreType.DMA((pieces,)),
            pltpu.SemaphoreType.DMA((1,)),
            pltpu.SemaphoreType.DMA((1,)),
            pltpu.SemaphoreType.DMA((2,)),
            pltpu.SemaphoreType.REGULAR((2, pieces)),
        ],
        compiler_params=comm_params(2),
        cost_estimate=cost(150e-6 * 1e15, 80e6),
        name="middle",
    )(
        attended.reshape(4, pieces, n, heads), wo, tokens.reshape(own), gain,
        cot_own.reshape(own), cots, wg, wu, wd,
    )


def rows_back(grad, inputs, gain):
    inverse = lax.rsqrt(jnp.mean(inputs * inputs, axis=-1, keepdims=True) + epsilon)
    unit = inputs * inverse
    scaled = grad * gain
    back = inverse * (scaled - unit * jnp.mean(scaled * unit, axis=-1, keepdims=True))
    return back, jnp.sum((grad * unit).reshape(-1, 8, grad.shape[-1]), axis=0)


def end_kernel(count, *refs):
    refs = list(refs)
    take = lambda n: [refs.pop(0) for _ in range(n)]
    dq, dk, dv, wq, wk, wv, tokens, grad_one, gain, attn_in, merge, gain_two, hid1, parts_in = take(14)
    parts, states, dwo = take(count), take(count), take(1 if count else 0)
    grad_ref, gains_ref, out_ref = take(3)
    fulls = take(count + 2 if count else 0)
    dwqkv_out = take(0 if count else 1)
    terms, cr, xr, out_mine, out_side, out_across, gain_sum, gain_land, dwqkv = take(9)
    send_sem, recv_sem, load_sem, gain_send, gain_recv = take(5)
    own, width = tokens.shape
    rows = own // CHUNKS
    sems = (send_sem, recv_sem)
    gain_sems = (gain_send, gain_recv)

    def at(base, k):
        return pl.ds(pl.multiple_of(base + k * rows, rows), rows)

    def term(p, k):
        here = at(p * own, k)
        return dot(dq[here], wq[...], NT) + dot(dk[here], wk[...], NT) + dot(dv[here], wv[...], NT)

    side0 = lambda k: send(terms.at[at(0, k)], cr.at[0, at(0, k)], sems, (0, k), 1)
    side1 = lambda k: send(terms.at[at(own, k)], cr.at[1, at(0, k)], sems, (1, k), 1)
    across = lambda k: send(terms.at[at(2 * own, k)], xr.at[at(0, k)], sems, (2, k), 2)
    out_load = [pltpu.make_async_copy(parts_in.at[:, 2 - 2 * k], out_mine.at[k], load_sem.at[k]) for k in range(2)]
    out_from_side = [send(parts_in.at[:, 3 - 2 * k], out_side.at[k], sems, (3, k), 1) for k in range(2)]
    out_from_across = send(out_mine.at[0], out_across, sems, (3, 2), 2)

    if count:
        reduces, rest = [], take(5 * count)
        for a in range(count):
            land, mine, *own_sems = rest[5 * a : 5 * a + 5]
            reduces.append(Reduce(parts[a], states[a], land, mine, EARLY, RING - 1, *own_sems))
        land, mine, *own_sems = take(5)
        late = [Reduce(dwo[0], None, land, mine, 0, RING - 1, *own_sems)]
        land, *own_sems = take(3)
        late.append(Reduce(dwqkv, None, land, None, 0, RING - 1, *own_sems, None))
        spreads = [Spread(r, full, *take(3)) for r, full in zip([*reduces, *late], fulls)]
        early_spreads, late_spreads = spreads[:count], spreads[count:]
        dp = lax.axis_index("dp")
        flip = lambda bit: {"dp": dp + bit - 2 * bit * lax.rem(lax.div(dp, bit), 2)}
        meet(partner(1), partner(2), ring_peer(0), ring_peer(1), flip(1), flip(2), flip(4))
        for ring in (*reduces, late[0]):
            ring.start()
        for ring in (*reduces, late[0]):
            ring.prefetch()
    else:
        meet(partner(1), partner(2))
    for k in range(2):
        out_load[k].start()
        out_from_side[k].start()

    @pl.loop(0, CHUNKS)
    def _(k):
        terms[at(0, k)] = term(3, k).astype(bf16)
        side0(k).start()
        mine = term(2, k)
        side0(k).wait_recv()
        terms[at(2 * own, k)] = (mine + cr[0, at(0, k)].astype(f32)).astype(bf16)
        across(k).start()

    chunk = dwqkv.shape[2]

    def weight_rows(k, size):
        part = attn_in[:, pl.ds(pl.multiple_of(k * size, size), size)]
        padded = jnp.concatenate([dot(part, d[...], TN).astype(bf16) for d in (dq, dk, dv)], axis=1)
        return dot(padded, merge[...], NT).astype(bf16)

    @pl.loop(0, width // 384)
    def _(k):
        block = weight_rows(k, 384)
        for i in range(384 // chunk):
            number = k * (384 // chunk) + i
            dwqkv[lax.div(number, RING), lax.rem(number, RING)] = block[i * chunk : (i + 1) * chunk]

    if count:
        late[1].start()
    else:
        stored = pltpu.make_async_copy(dwqkv, dwqkv_out[0], load_sem.at[2])
        stored.start()
        stored.wait()

    @pl.loop(0, CHUNKS)
    def _(k):
        terms[at(own, k)] = term(1, k).astype(bf16)
        side1(k).start()
        grad_ref[at(0, k)] = term(0, k)

    out_load[0].wait()
    out_from_side[0].wait_recv()

    @pl.loop(0, CHUNKS)
    def _(k):
        out_mine[0, k] = (out_mine[0, k].astype(f32) + out_side[0, k].astype(f32)).astype(bf16)

    out_from_across.start()

    if count:

        @pl.loop(0, RING - 1 - EARLY)
        def _(k):
            for ring in reduces:
                ring.step(k)
            for ring in late:
                ring.step(k)

        for ring in early_spreads:
            ring.start()

    gain_sum[...] = jnp.zeros_like(gain_sum)
    gain_sum[1:2] = jnp.sum(gain_two[...], axis=0, keepdims=True)

    @pl.loop(0, CHUNKS)
    def _(k):
        side1(k).wait_recv()
        across(k).wait_recv()
        here = at(0, k)
        grad = grad_ref[here] + cr[1, here].astype(f32) + xr[here].astype(f32)
        back, sums = rows_back(grad, tokens[here].astype(f32), gain[...])
        grad_ref[here] = grad_one[here] + back
        gain_sum[0:1] += jnp.sum(sums, axis=0, keepdims=True)

    def gain_copy(stage):
        to = [partner(1), partner(2)] + ([flip(1), flip(2), flip(4)] if count else [])
        return pltpu.make_async_remote_copy(
            src_ref=gain_sum,
            dst_ref=gain_land.at[stage],
            send_sem=gain_send.at[stage],
            recv_sem=gain_recv.at[stage],
            device_id=to[stage],
            device_id_type=pl.DeviceIdType.MESH,
        )

    def gain_add(stage):
        gain_copy(stage).wait()
        gain_sum[...] += gain_land[stage]

    gain_copy(0).start()
    if count:

        @pl.loop(0, EARLY)
        def _(k):
            for ring in early_spreads:
                ring.step(k)
            for ring in late:
                ring.step(RING - 1 - EARLY + k)

        for ring in late_spreads:
            ring.start()
    gain_add(0)
    gain_copy(1).start()
    out_load[1].wait()
    out_from_side[1].wait_recv()
    out_from_across.wait_recv()

    @pl.loop(0, CHUNKS)
    def _(k):
        total = out_mine[1, k].astype(f32) + out_side[1, k].astype(f32) + out_across[k].astype(f32)
        out_ref[k] = (hid1[k] + total).astype(bf16)

    gain_add(1)
    if count:
        gain_copy(2).start()

        @pl.loop(0, RING - 1 - EARLY)
        def _(k):
            for ring in early_spreads:
                ring.step(EARLY + k)
            for ring in late_spreads:
                ring.step(k)

        gain_add(2)
        gain_copy(3).start()
        gain_add(3)
        gain_copy(4).start()

        @pl.loop(RING - 1 - EARLY, RING - 1)
        def _(k):
            for ring in late_spreads:
                ring.step(k)

        gain_add(4)
        for ring in (*reduces, *late, *spreads):
            ring.finish()
    gains_ref[...] = gain_sum[...]

    @pl.loop(0, CHUNKS)
    def _(k):
        side0(k).wait_send()
        side1(k).wait_send()
        across(k).wait_send()

    for k in range(2):
        out_from_side[k].wait_send()
    out_from_across.wait_send()


def end(dq, dk, dv, wq, wk, wv, tokens, grad_one, gain, attn_in, merge, gain_two, hid1, parts_in, parts, states, dwo):
    own, width = tokens.shape
    heads = merge.shape[0]
    count = len(parts)
    sds = jax.ShapeDtypeStruct
    pieces = hid1.shape
    qkv_shape = (2, RING, width // (2 * RING), heads)
    late = [dwo] if count else []
    ring_shapes = [*[p.shape for p in parts], dwo.shape, qkv_shape] if count else []
    ring_buffers = []
    for p in parts:
        ring_buffers += ring_scratch(p.shape, RING - 1 - EARLY, True)
    if count:
        ring_buffers += ring_scratch(dwo.shape, RING - 1, True) + ring_scratch(qkv_shape, RING - 1, False)
        for _ in ring_shapes:
            ring_buffers += [pltpu.SemaphoreType.DMA((2, RING - 1))] * 2 + [pltpu.SemaphoreType.DMA((2,))]
    stages = 5 if count else 2
    outs = pl.pallas_call(
        functools.partial(end_kernel, count),
        in_specs=[VMEM] * 13 + [ANY] * (1 + 2 * count + len(late)),
        out_specs=[VMEM] * 3 + [ANY] * (len(ring_shapes) or 1),
        out_shape=[
            sds((own, width), f32),
            sds((8, width), f32),
            sds(pieces, bf16),
            *[sds(shape, bf16) for shape in (ring_shapes or [qkv_shape])],
        ],
        scratch_shapes=[
            pltpu.VMEM((3 * own, width), bf16),
            pltpu.VMEM((2, own, width), bf16),
            pltpu.VMEM((own, width), bf16),
            pltpu.VMEM((2, *pieces), bf16),
            pltpu.VMEM((2, *pieces), bf16),
            pltpu.VMEM(pieces, bf16),
            pltpu.VMEM((8, width), f32),
            pltpu.VMEM((stages, 8, width), f32),
            pltpu.VMEM(qkv_shape, bf16),
            *dma_sems(4, max(CHUNKS, 3)),
            pltpu.SemaphoreType.DMA((3,)),
            *dma_sems(stages),
            *ring_buffers,
        ],
        compiler_params=comm_params(3),
        cost_estimate=cost(150e-6 * 1e15, 60e6),
        name="end",
    )(dq, dk, dv, wq, wk, wv, tokens, grad_one, gain, attn_in, merge, gain_two, hid1, parts_in, *parts, *states, *late)
    return outs[:3], outs[3:]


def spread(heads):
    col = lax.broadcasted_iota(jnp.int32, (heads * HEAD_SIZE, heads * LANES), 1)
    row = lax.broadcasted_iota(jnp.int32, (heads * HEAD_SIZE, heads * LANES), 0)
    half, feature = row // HALF, row % HALF
    return (col == half * (LANES // 2) + feature).astype(bf16)


def body(
    tokens, segments, positions, norm_attn, w_query, key_weight, value_weight, w_out,
    norm_mlp, w_gate, w_up, w_down, cotangent,
):
    seq = segments.shape[0]
    own, width = tokens.shape
    me = lax.axis_index("tensor")
    order = me ^ jnp.arange(4, dtype=jnp.int32)
    blocks = 4

    starts = jnp.zeros_like(segments)
    for document in (1, 2, 3):
        first = jnp.sum((segments < document).astype(jnp.int32))
        starts = jnp.where(segments >= document, first, starts)
    start = jnp.take(starts.reshape(4, own), order, axis=0).reshape(1, seq)
    places = jnp.take(positions.reshape(4, own), order, axis=0).reshape(seq)
    lane = jnp.arange(LANES // 2)
    inverse = jnp.exp(lane.astype(f32) * (-2.0 * math.log(rope_base) / HEAD_SIZE))
    angles = places.astype(f32)[:, None] * jnp.where(lane < HALF, inverse, 0.0)[None, :]
    cos, sin = jnp.cos(angles), jnp.sin(angles)
    cos = jnp.concatenate([cos, cos], 1)
    sin = jnp.concatenate([-sin, sin], 1)

    spread_q, spread_k = spread(w_query.shape[1] // HEAD_SIZE), spread(key_weight.shape[1] // HEAD_SIZE)
    wq = dot(w_query, spread_q).astype(bf16)
    wk = dot(key_weight, spread_k).astype(bf16)
    wv = dot(value_weight, spread_k).astype(bf16)
    wo = dot(spread_q, w_out, TN).astype(bf16)
    gain_attn, gain_mlp = norm_attn.reshape(1, width), norm_mlp.reshape(1, width)

    inputs = tokens.astype(f32)
    inverse_one = lax.rsqrt(jnp.mean(inputs * inputs, axis=-1, keepdims=True) + epsilon)
    normed_one = (inputs * inverse_one * norm_attn).astype(bf16)

    qkv, attn_in = project_qkv(normed_one, wq, wk, wv, cos, sin)
    attended, lse, cots = attend(qkv, start, cotangent, blocks)
    hid1, grad_attended, parts, grad_one, dwd, dwg, dwu, dwo, gain_two = middle(
        attended, wo, tokens, gain_mlp, cotangent, cots, w_gate, w_up, w_down
    )
    grad_attended = grad_attended.reshape(seq, -1)
    dwo = dot(spread_q, dwo).astype(bf16)
    ringed = lax.axis_size("dp") == RING
    chunks = lambda t: t.reshape(2, RING, t.shape[0] // (2 * RING), t.shape[1])
    early = [chunks(t) for t in (dwd, dwg, dwu)] if ringed else []
    (dq, dk, dv), states = attend_back(qkv, attended, grad_attended, lse, start, cos, sin, early, blocks)
    (grad_tokens, gains, output), sums = end(
        dq, dk, dv, wq, wk, wv, tokens, grad_one.reshape(own, width), gain_attn, attn_in.reshape(seq, width),
        spread(8), gain_two, hid1, parts, early, states, chunks(dwo) if ringed else None,
    )
    output = output.reshape(own, width)
    if not ringed:
        gains = lax.psum(gains, "dp")
        sums = [lax.psum(t, "dp") for t in (dwd, dwg, dwu, dwo, sums[0])]
    sums = [t.reshape(shape).astype(f32) for t, shape in zip(sums, (
        w_down.shape, w_gate.shape, w_up.shape, w_out.shape, (width, spread(8).shape[0])
    ))]
    grad_w_down, grad_w_gate, grad_w_up, grad_w_out, grad_w_qkv = sums
    heads_q, heads_k = w_query.shape[1], key_weight.shape[1]
    grad_w_query = grad_w_qkv[:, :heads_q]
    grad_w_key = grad_w_qkv[:, heads_q : heads_q + heads_k]
    grad_w_value = grad_w_qkv[:, heads_q + heads_k :]
    return (
        output, grad_tokens, gains[0], grad_w_query, grad_w_key, grad_w_value, grad_w_out,
        gains[1], grad_w_gate, grad_w_up, grad_w_down,
    )


def solution(mesh):
    rows, cols, both = P("tensor", None), P(None, "tensor"), P(("dp", "tensor"), None)
    in_specs = (both, P("dp"), P("dp"), P(), cols, cols, cols, rows, P(), cols, cols, rows, both)
    out_specs = (both, both, P(), cols, cols, cols, rows, P(), cols, cols, rows)
    return jax.shard_map(body, mesh=mesh, in_specs=in_specs, out_specs=out_specs, check_vma=False)
```

```python
import functools
import math

import jax
import jax.numpy as jnp
from jax import lax
from jax.experimental import pallas as pl
from jax.experimental.pallas import tpu as pltpu
from jax.sharding import PartitionSpec as P

HEAD_SIZE = 96
HALF = HEAD_SIZE // 2
LANES = 128
epsilon = 1e-05
rope_base = 100000.0
masked_value = -1e30
score_scale = 1.0 / math.sqrt(HEAD_SIZE)
log2_e = math.log2(math.e)
bf16, f32 = jnp.bfloat16, jnp.float32
NN = (((1,), (0,)), ((), ()))
NT = (((1,), (1,)), ((), ()))
TN = (((0,), (0,)), ((), ()))
VMEM_LIMIT = 67043328
CHUNKS = 4


def dot(left, right, dims=NN):
    return lax.dot_general(left, right, dims, preferred_element_type=f32)


def params():
    return pltpu.CompilerParams(vmem_limit_bytes=VMEM_LIMIT)


def cost(flops, nbytes):
    return pl.CostEstimate(flops=int(flops), bytes_accessed=int(nbytes), transcendentals=0)


def whole(shape):
    return pl.BlockSpec(shape, lambda *_: (0,) * len(shape), pipeline_mode=pl.Buffered(1))


ANY = pl.BlockSpec(memory_space=pl.ANY)
VMEM = pl.BlockSpec(memory_space=pltpu.VMEM)


def peer(bits):
    me = lax.axis_index("tensor")
    low, high = lax.rem(me, 2), lax.div(me, 2)
    if bits % 2:
        low = 1 - low
    if bits // 2:
        high = 1 - high
    return 2 * high + low


def partner(bits):
    return {"tensor": peer(bits)}


def send(source, target, sems, at, bits):
    return pltpu.make_async_remote_copy(
        src_ref=source,
        dst_ref=target,
        send_sem=sems[0].at[at],
        recv_sem=sems[1].at[at],
        device_id=partner(bits),
        device_id_type=pl.DeviceIdType.MESH,
    )


def meet(*others):
    barrier = pltpu.get_barrier_semaphore()
    for other in others:
        pl.semaphore_signal(barrier, inc=1, device_id=other, device_id_type=pl.DeviceIdType.MESH)
    pl.semaphore_wait(barrier, len(others))


RING = 8
IN_MIDDLE = 3
IN_BACK = 6


def ring_place():
    index = lax.axis_index("dp")
    deep, wide = lax.div(index, 2), lax.rem(index, 2)
    return deep + wide * (RING - 1 - 2 * deep)


def ring_peer(way):
    place = lax.rem(ring_place() + (1, RING - 1)[way], RING)
    wide = lax.div(place, RING // 2)
    return {"dp": 2 * (place + wide * (RING - 1 - 2 * place)) + wide}


def ring_chunk(way, step):
    return lax.rem(ring_place() + (2 * RING - step if way == 0 else step), RING)


def ring_send(source, target, sems, at, way):
    return pltpu.make_async_remote_copy(
        src_ref=source,
        dst_ref=target,
        send_sem=sems[0].at[at],
        recv_sem=sems[1].at[at],
        device_id=ring_peer(way),
        device_id_type=pl.DeviceIdType.MESH,
    )


class Reduce:
    def __init__(self, parts, state, land, mine, first, last, send_sem, recv_sem, load_sem=None):
        self.parts, self.state, self.land, self.mine = parts, state, land, mine
        self.first, self.count, self.sems, self.load_sem = first, last - first, (send_sem, recv_sem), load_sem

    def begin(self, way):
        source = self.parts.at[way, ring_chunk(way, 0)] if self.state is None else self.state.at[way]
        return ring_send(source, self.land(way, 0), self.sems, (way, 0), way)

    def copy(self, way, k):
        return ring_send(self.land(way, k - 1), self.land(way, k), self.sems, (way, k), way)

    def load(self, way, k):
        source = self.parts.at[way, ring_chunk(way, self.first + k + 1)]
        return pltpu.make_async_copy(source, self.mine(way, k), self.load_sem.at[way, k])

    def start(self):
        for way in range(2):
            self.begin(way).start()

    def prefetch(self):
        for k in range(self.count):
            for way in range(2):
                self.load(way, k).start()

    def step(self, k):
        for way in range(2):
            (self.copy(way, k) if k else self.begin(way)).wait_recv()
            if self.mine is None:
                own = self.parts[way, ring_chunk(way, self.first + k + 1)]
            else:
                self.load(way, k).wait()
                own = self.mine(way, k)[...]
            here = self.land(way, k)
            here[...] = (here[...].astype(f32) + own.astype(f32)).astype(bf16)
            if k + 1 < self.count:
                self.copy(way, k + 1).start()

    def result(self, way):
        return self.land(way, self.count - 1)

    def finish(self):
        for way in range(2):
            self.begin(way).wait_send()
            for k in range(1, self.count):
                self.copy(way, k).wait_send()


class Spread:
    def __init__(self, reduced, full, send_sem, recv_sem, own_sem):
        self.reduced, self.full, self.sems, self.own_sem = reduced, full, (send_sem, recv_sem), own_sem

    def slot(self, way, step):
        return self.full.at[way, ring_chunk(way, step + RING - 1)]

    def keep(self, way):
        return pltpu.make_async_copy(self.reduced.result(way), self.slot(way, 0), self.own_sem.at[way])

    def copy(self, way, k):
        source = self.slot(way, k) if k else self.reduced.result(way)
        return ring_send(source, self.slot(way, k), self.sems, (way, k), way)

    def start(self):
        for way in range(2):
            self.copy(way, 0).start()
            self.keep(way).start()

    def step(self, k):
        for way in range(2):
            ring_send(self.slot(way, k + 1), self.slot(way, k + 1), self.sems, (way, k), way).wait_recv()
            if k < RING - 2:
                self.copy(way, k + 1).start()

    def finish(self):
        for way in range(2):
            self.keep(way).wait()
            for k in range(RING - 1):
                self.copy(way, k).wait_send()


def slots(ref):
    return lambda way, k: ref.at[way, k]


def ring_scratch(shape, steps, loads):
    rows, cols = shape[2:]
    land = pltpu.VMEM((2, steps, rows, cols), bf16)
    sems = [pltpu.SemaphoreType.DMA((2, steps))] * (3 if loads else 2)
    return [land] * (2 if loads else 1) + sems


def comm_params(number):
    return pltpu.CompilerParams(vmem_limit_bytes=VMEM_LIMIT, collective_id=number, has_side_effects=True)


def dma_sems(*shape):
    return [pltpu.SemaphoreType.DMA(shape)] * 2


def spread(heads, turned=False):
    shape = (heads * HEAD_SIZE, heads * LANES)
    feature = lax.broadcasted_iota(jnp.int32, shape[::-1] if turned else shape, int(turned))
    lane = lax.broadcasted_iota(jnp.int32, shape[::-1] if turned else shape, 1 - int(turned))
    target = feature
    for half in range(1, 2 * heads):
        target += jnp.where(feature >= half * HALF, LANES // 2 - HALF, 0)
    return jnp.where(lane == target, 1.0, 0.0).astype(bf16)


def front_kernel(
    tokens, gains, w_query, key_weight, value_weight, w_out, segments, positions, cot,
    qkv_out, stack_out, att_out, lse_out, cots, wq_out, wk_out, wv_out, wo_out, cos_out, sin_out, start_out,
    x, land, qkv, att, wq, wk, wv, wo, cos_v, sin_v, send_sem, recv_sem, store_sem,
    *, blocks,
):
    sems = (send_sem, recv_sem)
    own, width = tokens.shape
    rows = own // CHUNKS
    seq = qkv.shape[0]
    size = seq // blocks

    def piece(k):
        return pl.ds(pl.multiple_of(k * rows, rows), rows)

    side = send(x, land.at[0], sems, (0, 0), 1)
    across = lambda k: send(x.at[piece(k)], land.at[1, piece(k)], sems, (1, k), 2)
    onward = lambda k: send(land.at[1, piece(k)], land.at[2, piece(k)], sems, (2, k), 1)
    cot_side = send(cot, cots.at[0], sems, (3, 0), 1)
    cot_across = lambda k: send(cot.at[k], cots.at[1, k], sems, (4, k), 2)
    cot_onward = lambda k: send(cots.at[1, k], cots.at[2, k], sems, (5, k), 1)
    stores = []

    def store(source, target):
        copy = pltpu.make_async_copy(source, target, store_sem.at[len(stores)])
        copy.start()
        stores.append(copy)

    meet(partner(1), partner(2))

    @pl.loop(0, CHUNKS)
    def _(k):
        inputs = tokens[piece(k)].astype(f32)
        inverse = lax.rsqrt(jnp.mean(inputs * inputs, axis=-1, keepdims=True) + epsilon)
        x[piece(k)] = (inputs * inverse * gains[0:1, :]).astype(bf16)
        across(k).start()

    side.start()
    store(x, stack_out.at[0])

    spread_q, spread_k = spread(w_query.shape[1] // HEAD_SIZE), spread(key_weight.shape[1] // HEAD_SIZE)
    for source, matrix, target, out in (
        (w_query, spread_q, wq, wq_out),
        (key_weight, spread_k, wk, wk_out),
        (value_weight, spread_k, wv, wv_out),
    ):
        target[...] = dot(source[...], matrix).astype(bf16)
        store(target, out)
    wo[...] = dot(spread(w_query.shape[1] // HEAD_SIZE, True), w_out[...]).astype(bf16)
    store(wo, wo_out)

    lane = lax.broadcasted_iota(jnp.int32, (1, LANES), 1)
    feature = jnp.where(lane < LANES // 2, lane, lane - LANES // 2)
    frequency = jnp.exp(feature.astype(f32) * (-2.0 * math.log(rope_base) / HEAD_SIZE))
    frequency = jnp.where(feature < HALF, frequency, 0.0)
    sign = jnp.where(lane < LANES // 2, -1.0, 1.0)
    for p in range(4):

        @pl.loop(0, CHUNKS)
        def _(k):
            base = pl.multiple_of(peer(p) * own + k * rows, rows)
            angles = positions[pl.ds(base, rows), :].astype(f32) * frequency
            here = pl.ds(pl.multiple_of(p * own + k * rows, rows), rows)
            cos_v[here] = jnp.cos(angles)
            sin_v[here] = jnp.sin(angles) * sign

    store(cos_v, cos_out)
    store(sin_v, sin_out)
    documents = segments[...].astype(f32)
    starts = jnp.zeros_like(documents)
    for document in (1, 2, 3):
        first = jnp.sum(jnp.where(documents < document, 1.0, 0.0), axis=1, keepdims=True)
        starts = jnp.where(documents >= document, first, starts)
    start_out[...] = starts.astype(jnp.int32)

    head_lane = lax.broadcasted_iota(jnp.int32, (rows, LANES), 1)

    def project(ref, base):
        values = ref[...]
        here = pl.ds(pl.multiple_of(base, rows), rows)
        cos, sin = cos_v[here], sin_v[here]
        for w, first, turn in ((wq, 0, True), (wk, 4, True), (wv, 6, False)):
            y = dot(values, w[...])
            for h in range(w.shape[1] // LANES):
                v = y[:, h * LANES : (h + 1) * LANES]
                if turn:
                    v = v * cos + pltpu.roll(v, LANES // 2, 1) * sin
                else:
                    v = jnp.where(head_lane == HALF, 1.0, v)
                at = (first + h) * LANES
                qkv[here, at : at + LANES] = v.astype(bf16)

    @pl.loop(0, CHUNKS)
    def _(k):
        project(x.at[piece(k)], k * rows)

    side.wait_recv()
    store(land.at[0], stack_out.at[1])
    cot_side.start()

    @pl.loop(0, CHUNKS)
    def _(k):
        project(land.at[0, piece(k)], own + k * rows)

    @pl.loop(0, CHUNKS)
    def _(k):
        across(k).wait_recv()
        onward(k).start()
        cot_across(k).start()
        project(land.at[1, piece(k)], 2 * own + k * rows)
        onward(k).wait_recv()
        project(land.at[2, piece(k)], 3 * own + k * rows)

    store(land.at[1], stack_out.at[2])
    store(land.at[2], stack_out.at[3])
    store(qkv, qkv_out)

    @pl.loop(0, 2)
    def _(g):
        for i in range(blocks):
            at = pl.ds(pl.multiple_of(peer(i) * size, size), size)
            cols = [pl.ds(pl.multiple_of((2 * g + r) * LANES, LANES), LANES) for r in range(2)]
            queries = [qkv[at, cols[r]] for r in range(2)]
            start = start_out[:, i * size : (i + 1) * size]
            state = [None, None]
            for j in [i, *range(i)]:
                key_at = pl.ds(pl.multiple_of(peer(j) * size, size), size)
                keys = qkv[key_at, pl.ds(pl.multiple_of((4 + g) * LANES, LANES), LANES)]
                values = qkv[key_at, pl.ds(pl.multiple_of((6 + g) * LANES, LANES), LANES)]
                key_rows = lax.broadcasted_iota(jnp.int32, (size, size), 0)
                allowed = key_rows >= start - j * size
                if j == i:
                    allowed &= key_rows <= lax.broadcasted_iota(jnp.int32, (size, size), 1)
                for r in range(2):
                    scores = jnp.where(allowed, dot(keys, queries[r], NT) * (score_scale * log2_e), masked_value)
                    peak = jnp.max(scores, axis=0, keepdims=True)
                    if state[r] is not None:
                        peak = jnp.maximum(state[r][0], peak)
                    weights = jnp.exp2(scores - peak)
                    mixed = dot(values, weights.astype(bf16), TN)
                    if state[r] is not None:
                        mixed += state[r][1] * jnp.exp2(state[r][0] - peak)
                    state[r] = (peak, mixed)
            for r, (peak, mixed) in enumerate(state):
                total = mixed[HALF : HALF + 1, :]
                att[at, cols[r]] = (mixed / total).T.astype(bf16)
                lse_out[g, r : r + 1, at] = peak + jnp.log2(total)

    store(att, att_out)
    for k in range(CHUNKS):
        cot_across(k).wait_recv()
        cot_onward(k).start()
    side.wait_send()
    cot_side.wait()
    for k in range(CHUNKS):
        across(k).wait_send()
        onward(k).wait_send()
        cot_across(k).wait_send()
        cot_onward(k).wait()
    for copy in stores:
        copy.wait()


def front(tokens, gains, w_query, key_weight, value_weight, w_out, segments, positions, cot, blocks):
    own, width = tokens.shape
    seq = segments.shape[1]
    pieces = (CHUNKS, own // CHUNKS, width)
    sds = jax.ShapeDtypeStruct
    heads = 4 * LANES
    arrays = dict(
        qkv=(seq, 8 * LANES), att=(seq, heads), wq=(width, heads), wk=(width, heads // 2), wv=(width, heads // 2),
        wo=(heads, width),
    )
    low = lambda name: sds(arrays[name], bf16)
    scratch = lambda name: pltpu.VMEM(arrays[name], bf16)
    table = sds((seq, LANES), f32)
    return pl.pallas_call(
        functools.partial(front_kernel, blocks=blocks),
        in_specs=[VMEM] * 8 + [ANY],
        out_specs=[ANY] * 3 + [VMEM] + [ANY] * 7 + [VMEM],
        out_shape=[
            low("qkv"), sds((4, own, width), bf16), low("att"), sds((2, 2, seq), f32), sds((3, *pieces), bf16),
            low("wq"), low("wk"), low("wv"), low("wo"), table, table, sds((1, seq), jnp.int32),
        ],
        scratch_shapes=[
            pltpu.VMEM((own, width), bf16),
            pltpu.VMEM((3, own, width), bf16),
            *[scratch(name) for name in arrays],
            pltpu.VMEM((seq, LANES), f32),
            pltpu.VMEM((seq, LANES), f32),
            *dma_sems(6, CHUNKS),
            pltpu.SemaphoreType.DMA((12,)),
        ],
        compiler_params=comm_params(1),
        cost_estimate=cost(80e-6 * 1e15, 40e6),
        name="front",
    )(tokens, gains, w_query, key_weight, value_weight, w_out, segments, positions, cot.reshape(pieces))


def attend_back_kernel(count, *refs, blocks, size):
    q_ref, k_ref, v_ref, o_ref, do_ref, lse_ref, start_ref, cos_ref, sin_ref, *rest = refs
    parts, befores, rest = rest[:count], rest[count : 2 * count], rest[2 * count :]
    dq_ref, dk_ref, dv_ref, *rest = rest
    states, rest = rest[:count], rest[count:]
    dq_sum, dk_sum, dv_sum, inner, *rest = rest
    rings = []
    for a in range(count):
        land, mine, *own_sems = rest[5 * a : 5 * a + 5]
        rings.append(Reduce(parts[a], befores[a], slots(land), slots(mine), IN_MIDDLE, IN_BACK, *own_sems))
    steps = IN_BACK - IN_MIDDLE
    keep_sem = rest[-1] if count else None

    def keep(a, way):
        return pltpu.make_async_copy(rings[a].result(way), states[a].at[way], keep_sem.at[a, way])

    if count:

        @pl.when(pl.program_id(0) == 0)
        def _():
            meet(ring_peer(0), ring_peer(1))
            for ring in rings:
                ring.start()
            for ring in rings:
                ring.prefetch()

    pairs = blocks * (blocks + 1) // 2
    hooks = {}
    for number in range(count * steps):
        due = min(round((number + 1) * 2.25) + 1, 2 * pairs - 1)
        hooks.setdefault(due, []).append((number % count, number // count))

    def hook(pair):
        for half in range(2):
            todo = hooks.get(half * pairs + pair, [])
            if todo:

                @pl.when(pl.program_id(0) == half)
                def _():
                    for a, k in todo:
                        rings[a].step(k)
                        if k == steps - 1:
                            keep(a, 0).start()
                            keep(a, 1).start()

    for c in range(blocks):
        rows = slice(c * size, (c + 1) * size)
        for r in range(2):
            cols = slice(r * LANES, (r + 1) * LANES)
            product = do_ref[rows, cols].astype(f32) * o_ref[rows, cols].astype(f32)
            inner[r : r + 1, rows] = jnp.sum(product.T, axis=0, keepdims=True)
    for i in reversed(range(blocks)):
        for j in [i, *range(i)]:
            at = pl.multiple_of(peer(i) * size, size)
            key_at = pl.multiple_of(peer(j) * size, size)
            keys = k_ref[pl.ds(key_at, size), :]
            values = v_ref[pl.ds(key_at, size), :]
            start = start_ref[:, i * size : (i + 1) * size]
            key_rows = lax.broadcasted_iota(jnp.int32, (size, size), 0)
            allowed = key_rows >= start - j * size
            if j == i:
                allowed &= key_rows <= lax.broadcasted_iota(jnp.int32, (size, size), 1)
            dk = dv = None
            for r in range(2):
                cols = slice(r * LANES, (r + 1) * LANES)
                queries = q_ref[pl.ds(at, size), cols]
                grads = do_ref[pl.ds(at, size), cols]
                scores = jnp.where(allowed, dot(keys, queries, NT) * (score_scale * log2_e), masked_value)
                weights = jnp.exp2(scores - lse_ref[0, r : r + 1, pl.ds(at, size)])
                grad_weights = dot(values, grads, NT)
                grad_scores = (weights * (grad_weights - inner[r : r + 1, pl.ds(at, size)])).astype(bf16)
                dv_term = dot(weights.astype(bf16), grads)
                dk_term = dot(grad_scores, queries)
                dv = dv_term if dv is None else dv + dv_term
                dk = dk_term if dk is None else dk + dk_term
                dq = dot(grad_scores, keys, TN)
                if j == i:
                    dq_sum[pl.ds(at, size), cols] = dq
                else:
                    dq_sum[pl.ds(at, size), cols] += dq
            if i == blocks - 1:
                dk_sum[pl.ds(key_at, size), :] = dk
                dv_sum[pl.ds(key_at, size), :] = dv
            else:
                dk_sum[pl.ds(key_at, size), :] += dk
                dv_sum[pl.ds(key_at, size), :] += dv
            hook(sum(range(blocks, i + 1, -1)) + (0 if j == i else j + 1))
    for c in range(blocks):
        rows = slice(c * size, (c + 1) * size)
        cos, sin = cos_ref[rows, :], sin_ref[rows, :]

        def back(grads):
            return ((grads * cos - pltpu.roll(grads, LANES // 2, 1) * sin) * score_scale).astype(bf16)

        for r in range(2):
            cols = slice(r * LANES, (r + 1) * LANES)
            dq_ref[rows, cols] = back(dq_sum[rows, cols])
        dk_ref[rows, :] = back(dk_sum[rows, :])
        dv_ref[rows, :] = dv_sum[rows, :].astype(bf16)

    if count:

        @pl.when(pl.program_id(0) == 1)
        def _():
            for a, ring in enumerate(rings):
                ring.finish()
                keep(a, 0).wait()
                keep(a, 1).wait()


def attend_back(qkv, attended, grads, lse, start, cos, sin, parts, befores, blocks):
    seq = qkv.shape[0]
    pair = pl.BlockSpec((seq, 2 * LANES), lambda g: (0, g))
    single = pl.BlockSpec((seq, LANES), lambda g: (0, g))
    table = pl.BlockSpec((seq, LANES), lambda g: (0, 0))
    count = len(parts)
    outs = pl.pallas_call(
        functools.partial(attend_back_kernel, count, blocks=blocks, size=seq // blocks),
        grid=(2,),
        in_specs=[
            pair,
            pl.BlockSpec((seq, LANES), lambda g: (0, 4 + g)),
            pl.BlockSpec((seq, LANES), lambda g: (0, 6 + g)),
            pair,
            pair,
            pl.BlockSpec((1, 2, seq), lambda g: (g, 0, 0)),
            pl.BlockSpec((1, seq), lambda g: (0, 0)),
            table,
            table,
            *[ANY] * (2 * count),
        ],
        out_specs=[pair, single, single, *[ANY] * count],
        scratch_shapes=[
            pltpu.VMEM((seq, 2 * LANES), f32),
            pltpu.VMEM((seq, LANES), f32),
            pltpu.VMEM((seq, LANES), f32),
            pltpu.VMEM((2, seq), f32),
            *[x for p in parts for x in ring_scratch(p.shape, IN_BACK - IN_MIDDLE, True)],
            *[pltpu.SemaphoreType.DMA((count, 2))] * bool(count),
        ],
        out_shape=[
            jax.ShapeDtypeStruct((seq, 4 * LANES), bf16),
            jax.ShapeDtypeStruct((seq, 2 * LANES), bf16),
            jax.ShapeDtypeStruct((seq, 2 * LANES), bf16),
            *[jax.ShapeDtypeStruct((2, *p.shape[2:]), bf16) for p in parts],
        ],
        compiler_params=comm_params(5) if count else params(),
        cost_estimate=cost(5 * 2 * 4 * LANES * seq * seq, 10 * seq * 8 * LANES),
        name="attention_back",
    )(qkv, qkv, qkv, attended, grads, lse, start, cos, sin, *parts, *befores)
    return outs[:3], outs[3:]


def rows_back(grad, inputs, gain):
    inverse = lax.rsqrt(jnp.mean(inputs * inputs, axis=-1, keepdims=True) + epsilon)
    unit = inputs * inverse
    scaled = grad * gain
    back = inverse * (scaled - unit * jnp.mean(scaled * unit, axis=-1, keepdims=True))
    return back, jnp.sum((grad * unit).reshape(-1, 8, grad.shape[-1]), axis=0)

RS1_C0, RS1_C1, RS1_X, AG2_X, AG2_C, AG2_F, RS3_C0, RS3_C1, RS3_X, AG3_X, AG3_C, AG3_F = range(12)


class _Chunks:
    def __init__(self, ref):
        self.ref, self.rows = ref, ref.shape[0] // (2 * RING)

    @property
    def at(self):
        return self

    def __getitem__(self, index):
        way, chunk = index
        return self.ref.at[pl.ds(pl.multiple_of((way * RING + chunk) * self.rows, self.rows), self.rows)]


def middle_kernel(
    ringed, att, wo, tokens, gains, cot_own, cots, wg_in, wu_in, wd_in,
    hid1, datt_out, parts_out, grad_one_out, dwd_out, dwg_out, dwu_out, dwo_out, gain_grad, *refs,
):
    states, refs = (refs[:3], refs[3:]) if ringed else ([], refs)
    (
        xs, cot, hid, gg, gu, g, cr, xr, part_stage, grad_stage, datt_stage, tile_stage, wg, wu, wd,
        send_sem, recv_sem, cot_sem, part_sem, grad_sem, datt_sem, tile_sem, free_sem, *ring_sems,
    ) = refs
    gain = gains.at[1:2]
    pieces, _, n, width = xs.shape
    units = wg.shape[1]
    heads = wo.shape[0]
    sems = (send_sem, recv_sem)
    two = (2 * n, width)

    def copy(kind, k):
        source, target, bits = {
            RS1_C0: (g.at[k, 3], cr.at[k, 0], 1),
            RS1_C1: (g.at[k, 1], cr.at[k, 1], 1),
            RS1_X: (g.at[k, 2], xr.at[k], 2),
            AG2_X: (xs.at[k, 0], xs.at[k, 2], 2),
            AG2_C: (xs.at[k, 0], xs.at[k, 1], 1),
            AG2_F: (xs.at[k, 2], xs.at[k, 3], 1),
            RS3_C0: (g.at[k, 3], cr.at[k, 0], 1),
            RS3_C1: (g.at[k, 1], cr.at[k, 1], 1),
            RS3_X: (g.at[k, 2], xr.at[k], 2),
            AG3_X: (g.at[k, 0], g.at[k, 2], 2),
            AG3_C: (g.at[k, 0], g.at[k, 1], 1),
            AG3_F: (g.at[k, 2], g.at[k, 3], 1),
        }[kind]
        return send(source, target, sems, (kind, k), bits)

    def credit(k, bits):
        pl.semaphore_signal(
            free_sem.at[bits - 1, k], inc=1, device_id=partner(bits), device_id_type=pl.DeviceIdType.MESH
        )

    def cot_copy(p):
        if p >= 4:
            source, target = ((wg_in, wg), (wu_in, wu), (wd_in, wd))[p - 4]
            return pltpu.make_async_copy(source, target, cot_sem.at[p])
        source = cot_own if p == 0 else cots.at[p - 1]
        return pltpu.make_async_copy(source, cot.at[:, p], cot_sem.at[p])

    def part_copy(k, low):
        return pltpu.make_async_copy(part_stage.at[k], parts_out.at[k, pl.ds(low, 2)], part_sem.at[k])

    for p in (4, 5, 6, 0, 1, 2, 3):
        cot_copy(p).start()
    meet(partner(1), partner(2), *([ring_peer(0), ring_peer(1)] if ringed else []))

    @pl.loop(0, pieces)
    def _(k):
        for p, kind in ((3, RS1_C0), (1, RS1_C1)):
            g[k, p] = dot(att[p, k], wo[...]).astype(bf16)
            copy(kind, k).start()

    @pl.loop(0, pieces)
    def _(k):
        term = dot(att[2, k], wo[...])
        copy(RS1_C0, k).wait_recv()
        g[k, 2] = (term + cr[k, 0].astype(f32)).astype(bf16)
        copy(RS1_X, k).start()

    def feed_forward(k, low):
        x = xs[k, pl.ds(low, 2)].reshape(two)
        gate = dot(x, wg[...])
        up = dot(x, wu[...])
        grad_hidden = dot(cot[k, pl.ds(low, 2)].reshape(two), wd[...], NT)
        sig = jax.nn.sigmoid(gate)
        act = gate * sig
        hidden = (act * up).astype(bf16)
        grad_gate = (grad_hidden * up * sig * (1.0 + gate * (1.0 - sig))).astype(bf16)
        grad_up = (grad_hidden * act).astype(bf16)
        hid[k, pl.ds(low, 2)] = hidden.reshape(2, n, units)
        gg[k, pl.ds(low, 2)] = grad_gate.reshape(2, n, units)
        gu[k, pl.ds(low, 2)] = grad_up.reshape(2, n, units)
        back = dot(grad_gate, wg[...], NT) + dot(grad_up, wu[...], NT)
        g[k, pl.ds(low, 2)] = back.astype(bf16).reshape(2, n, width)
        return hidden

    def out_part(k, low, hidden):
        part_stage[k] = dot(hidden, wd[...]).astype(bf16).reshape(2, n, width)
        part_copy(k, low).start()

    for p in range(7):
        cot_copy(p).wait()

    @pl.loop(0, pieces)
    def _(k):
        term = dot(att[0, k], wo[...])
        copy(RS1_C1, k).wait_recv()
        copy(RS1_X, k).wait_recv()
        hidden = tokens[k].astype(f32) + (term + cr[k, 1].astype(f32) + xr[k].astype(f32))
        hid1[k] = hidden
        inverse = lax.rsqrt(jnp.mean(hidden * hidden, axis=-1, keepdims=True) + epsilon)
        xs[k, 0] = (hidden * inverse * gain[...]).astype(bf16)
        copy(AG2_X, k).start()
        copy(AG2_C, k).start()
        copy(AG2_C, k).wait_recv()
        copy(RS1_C1, k).wait_send()
        out_part(k, 0, feed_forward(k, 0))

    @pl.loop(0, pieces)
    def _(k):
        copy(AG2_X, k).wait_recv()
        copy(AG2_F, k).start()
        part_copy(k, 0).wait()
        copy(AG2_F, k).wait_recv()
        copy(RS1_C0, k).wait_send()
        copy(RS1_X, k).wait_send()
        hidden = feed_forward(k, 2)
        copy(RS3_C0, k).start()
        copy(RS3_C1, k).start()
        out_part(k, 2, hidden)
        copy(RS3_C0, k).wait_recv()
        g[k, 2] = (g[k, 2].astype(f32) + cr[k, 0].astype(f32)).astype(bf16)
        copy(RS3_X, k).start()

    tokens_all = 4 * pieces * n

    def tile(slot, left, right, cols, out, at):
        height = out.shape[1]
        target = out.at[pl.ds(pl.multiple_of(at * 256, 256), 256)]
        move = pltpu.make_async_copy(tile_stage.at[slot, :, pl.ds(0, height)], target, tile_sem.at[slot])
        part = left[:, :, :, pl.ds(pl.multiple_of(at * 256, 256), 256)].reshape(tokens_all, 256)
        tile_stage[slot, :, pl.ds(0, height)] = dot(part, right[...].reshape(tokens_all, cols), TN).astype(bf16)
        return move

    def norm_back(k):
        copy(RS3_C1, k).wait_recv()
        copy(RS3_X, k).wait_recv()
        copy(RS3_C0, k).wait_send()
        copy(RS3_C1, k).wait_send()
        credit(k, 1)
        copy(RS3_X, k).wait_send()
        credit(k, 2)
        grad = g[k, 0].astype(f32) + cr[k, 1].astype(f32) + xr[k].astype(f32)
        back, sums = rows_back(grad, hid1[k], gain[...])
        result = cot[k, 0].astype(f32) + back
        g[k, 0] = result.astype(bf16)
        pl.semaphore_wait(free_sem.at[0, k], 1)
        pl.semaphore_wait(free_sem.at[1, k], 1)
        copy(AG3_X, k).start()
        copy(AG3_C, k).start()
        grad_stage[...] = result
        stored = pltpu.make_async_copy(grad_stage, grad_one_out.at[k], grad_sem.at[0])
        stored.start()

        @pl.when(k == 0)
        def _():
            gain_grad[...] = sums

        @pl.when(k > 0)
        def _():
            gain_grad[...] += sums

        return stored

    @pl.loop(0, 2)
    def _(k):
        first = tile(0, hid, cot, width, dwd_out, 2 * k)
        first.start()
        second = tile(1, hid, cot, width, dwd_out, 2 * k + 1)
        second.start()
        stored = norm_back(k)
        first.wait()
        second.wait()
        stored.wait()

    rings = []
    if ringed:
        n_down = dwd_out.shape[0] // (2 * RING)
        n_up = dwg_out.shape[0] // (2 * RING)
        places = (
            (lambda way, k: cot.at[k, 1 + way, pl.ds(0, n_down)], lambda way, k: cot.at[k, 3, pl.ds(way * n_down, n_down)]),
            (lambda way, k: hid.at[k, way, pl.ds(0, n_up)], lambda way, k: gg.at[k, way, pl.ds(0, n_up)]),
            (lambda way, k: hid.at[k, 2 + way, pl.ds(0, n_up)], lambda way, k: gu.at[k, way, pl.ds(0, n_up)]),
        )
        for a, (part, (land, mine)) in enumerate(zip((dwd_out, dwg_out, dwu_out), places)):
            rings.append(Reduce(_Chunks(part), None, land, mine, 0, IN_MIDDLE, *ring_sems[3 * a : 3 * a + 3]))
        for way in range(2):
            pl.semaphore_signal(
                free_sem.at[2, way], inc=1, device_id=ring_peer(1 - way), device_id_type=pl.DeviceIdType.MESH
            )

    @pl.loop(2, 4)
    def _(k):
        stored = norm_back(k)
        for i in range(3):
            at = 3 * (k - 2) + i
            gate = tile(0, xs, gg, units, dwg_out, at)
            gate.start()
            up = tile(1, xs, gu, units, dwu_out, at)
            up.start()
            gate.wait()
            up.wait()
        stored.wait()

    if ringed:
        for way in range(2):
            pl.semaphore_wait(free_sem.at[2, way], 1)
        for ring in rings:
            ring.start()
        for ring in rings:
            ring.prefetch()

    for k in range(pieces):
        copy(AG3_X, k).wait_recv()
        copy(AG3_F, k).start()
        copy(AG3_C, k).wait_recv()
        copy(AG3_F, k).wait_recv()
        datt_stage[...] = dot(g[k].reshape(4 * n, width), wo[...], NT).astype(bf16).reshape(4, n, heads)
        moved = pltpu.make_async_copy(datt_stage, datt_out.at[:, k], datt_sem.at[0])
        moved.start()
        moved.wait()
        if ringed and k > 0:
            for ring in rings:
                if k - 1 < IN_MIDDLE - 1:
                    ring.step(k - 1)

    for u in range(heads // 256):
        total = None
        for p in range(4):
            left = att[p, :, :, u * 256 : (u + 1) * 256].reshape(pieces * n, 256)
            term = dot(left, g[:, p].reshape(pieces * n, width), TN)
            total = term if total is None else total + term
        tile_stage[u] = total.astype(bf16)
        pltpu.make_async_copy(tile_stage.at[u], dwo_out.at[pl.ds(u * 256, 256)], tile_sem.at[u]).start()
    for u in range(heads // 256):
        pltpu.make_async_copy(tile_stage.at[u], dwo_out.at[pl.ds(u * 256, 256)], tile_sem.at[u]).wait()

    if ringed:
        for a, ring in enumerate(rings):
            ring.step(IN_MIDDLE - 1)
            for way in range(2):
                pltpu.make_async_copy(ring.result(way), states[a].at[way], ring_sems[-1].at[a, way]).start()
        for a, ring in enumerate(rings):
            ring.finish()
            for way in range(2):
                pltpu.make_async_copy(ring.result(way), states[a].at[way], ring_sems[-1].at[a, way]).wait()

    @pl.loop(0, pieces)
    def _(k):
        part_copy(k, 2).wait()
        for kind in (AG2_X, AG2_C, AG2_F, AG3_X, AG3_C, AG3_F):
            copy(kind, k).wait_send()


def middle(attended, wo, tokens, gains, cot_own, cots, wg, wu, wd, ringed):
    width, units, heads = wg.shape[0], wg.shape[1], wo.shape[0]
    pieces = CHUNKS
    n = tokens.shape[0] // pieces
    sds = jax.ShapeDtypeStruct
    own = (pieces, n, width)
    all_rows = (pieces, 4, n, width)
    all_units = (pieces, 4, n, units)
    chunk_down, chunk_up = (units // (2 * RING), width), (width // (2 * RING), units)
    states = [sds((2, *chunk), bf16) for chunk in (chunk_down, chunk_up, chunk_up)] if ringed else []
    return pl.pallas_call(
        functools.partial(middle_kernel, ringed),
        in_specs=[VMEM] * 4 + [ANY] * 5,
        out_specs=[VMEM] + [ANY] * 7 + [VMEM] + [ANY] * len(states),
        out_shape=[
            sds(own, f32),
            sds((4, pieces, n, heads), bf16),
            sds(all_rows, bf16),
            sds(own, f32),
            sds((units, width), bf16),
            sds((width, units), bf16),
            sds((width, units), bf16),
            sds((heads, width), bf16),
            sds((8, width), f32),
            *states,
        ],
        scratch_shapes=[
            pltpu.VMEM(all_rows, bf16),
            pltpu.VMEM(all_rows, bf16),
            pltpu.VMEM(all_units, bf16),
            pltpu.VMEM(all_units, bf16),
            pltpu.VMEM(all_units, bf16),
            pltpu.VMEM(all_rows, bf16),
            pltpu.VMEM((pieces, 2, n, width), bf16),
            pltpu.VMEM(own, bf16),
            pltpu.VMEM((pieces, 2, n, width), bf16),
            pltpu.VMEM((n, width), f32),
            pltpu.VMEM((4, n, heads), bf16),
            pltpu.VMEM((2, 256, width), bf16),
            *[pltpu.VMEM(w.shape, bf16) for w in (wg, wu, wd)],
            *dma_sems(12, pieces),
            pltpu.SemaphoreType.DMA((7,)),
            pltpu.SemaphoreType.DMA((pieces,)),
            pltpu.SemaphoreType.DMA((1,)),
            pltpu.SemaphoreType.DMA((1,)),
            pltpu.SemaphoreType.DMA((2,)),
            pltpu.SemaphoreType.REGULAR((3, pieces)),
            *([pltpu.SemaphoreType.DMA((2, IN_MIDDLE))] * 9 + [pltpu.SemaphoreType.DMA((3, 2))]) * ringed,
        ],
        compiler_params=comm_params(2),
        cost_estimate=cost(150e-6 * 1e15, 80e6),
        name="middle",
    )(
        attended.reshape(4, pieces, n, heads), wo, tokens.reshape(own), gains,
        cot_own.reshape(own), cots, wg, wu, wd,
    )


def end_kernel(count, *refs):
    refs = list(refs)
    take = lambda n: [refs.pop(0) for _ in range(n)]
    loaded, gains, gain_two, parts_in = take(10), *take(3)
    parts, states, dwo = take(count), take(count), take(1 if count else 0)
    grad_ref, gains_ref, out_ref = take(3)
    fulls = take(count + 3 if count else 0)
    dw_out = take(0 if count else 2)
    inputs = take(10)
    dq, dk, dv, wq, wk, wv, attn_in, tokens, grad_one, hid1 = inputs
    terms, cr, xr, out_mine, out_side, out_across, gain_sum, gain_land, dwq, dwkv = take(10)
    send_sem, recv_sem, load_sem, gain_send, gain_recv, in_sem = take(6)
    own, width = tokens.shape
    rows = own // CHUNKS
    sems = (send_sem, recv_sem)
    gain = gains.at[0:1]
    fetch = [pltpu.make_async_copy(source, target, in_sem.at[i]) for i, (source, target) in enumerate(zip(loaded, inputs))]

    def at(base, k):
        return pl.ds(pl.multiple_of(base + k * rows, rows), rows)

    def term(p, k):
        here = at(p * own, k)
        return dot(dq[here], wq[...], NT) + dot(dk[here], wk[...], NT) + dot(dv[here], wv[...], NT)

    side0 = lambda k: send(terms.at[at(0, k)], cr.at[0, at(0, k)], sems, (0, k), 1)
    side1 = lambda k: send(terms.at[at(own, k)], cr.at[1, at(0, k)], sems, (1, k), 1)
    across = lambda k: send(terms.at[at(2 * own, k)], xr.at[at(0, k)], sems, (2, k), 2)
    out_load = [pltpu.make_async_copy(parts_in.at[:, 2 - 2 * k], out_mine.at[k], load_sem.at[k]) for k in range(2)]
    out_from_side = [send(parts_in.at[:, 3 - 2 * k], out_side.at[k], sems, (3, k), 1) for k in range(2)]
    out_from_across = send(out_mine.at[0], out_across, sems, (3, 2), 2)

    reduces, late, early_spreads, late_spreads = [], [], [], []
    if count:
        for a in range(count):
            land, mine, *own_sems = take(5)
            reduces.append(Reduce(parts[a], states[a], slots(land), slots(mine), IN_BACK, RING - 1, *own_sems))
        land, mine, *own_sems = take(5)
        late.append(Reduce(dwo[0], None, slots(land), slots(mine), 0, RING - 1, *own_sems))
        for part in (dwq, dwkv):
            land, *own_sems = take(3)
            late.append(Reduce(part, None, slots(land), None, 0, RING - 1, *own_sems))
        spreads = [Spread(r, full, *take(3)) for r, full in zip([*reduces, *late], fulls)]
        early_spreads, late_spreads = spreads[:count], spreads[count:]

    for copy in fetch:
        copy.start()
    if count:
        dp = lax.axis_index("dp")
        flip = lambda bit: {"dp": dp + bit - 2 * bit * lax.rem(lax.div(dp, bit), 2)}
        meet(partner(1), partner(2), ring_peer(0), ring_peer(1), flip(1), flip(2), flip(4))
        for ring in (*reduces, late[0]):
            ring.start()
        for ring in (*reduces, late[0]):
            ring.prefetch()
    else:
        meet(partner(1), partner(2))
    for copy in fetch[:6]:
        copy.wait()

    @pl.loop(0, CHUNKS)
    def _(k):
        terms[at(0, k)] = term(3, k).astype(bf16)
        side0(k).start()

    for k in range(2):
        out_load[k].start()
        out_from_side[k].start()

    @pl.loop(0, CHUNKS)
    def _(k):
        mine = term(2, k)
        side0(k).wait_recv()
        terms[at(2 * own, k)] = (mine + cr[0, at(0, k)].astype(f32)).astype(bf16)
        across(k).start()

    for ring, following in zip(reduces, early_spreads):
        ring.step(0)
        following.start()

    chunk = dwq.shape[2]
    tall = 4 * chunk
    fetch[6].wait()
    merge_q, merge_kv = spread(dwq.shape[3] // HEAD_SIZE), spread(dwkv.shape[3] // HEAD_SIZE)

    @pl.loop(0, width // tall)
    def _(k):
        part = attn_in[:, pl.ds(pl.multiple_of(k * tall, LANES), tall)]
        block_q = dot(dot(part, dq[...], TN).astype(bf16), merge_q, NT).astype(bf16)
        padded = jnp.concatenate([dot(part, d[...], TN).astype(bf16) for d in (dk, dv)], axis=1)
        block_kv = dot(padded, merge_kv, NT).astype(bf16)
        for i in range(4):
            number = k * 4 + i
            here = (lax.div(number, RING), lax.rem(number, RING))
            dwq[here] = block_q[i * chunk : (i + 1) * chunk]
            dwkv[here] = block_kv[i * chunk : (i + 1) * chunk]

    if count:
        late[0].step(0)
        for ring in late[1:]:
            ring.start()
        late[0].step(1)
    else:
        stored = [pltpu.make_async_copy(s, t, load_sem.at[2 + i]) for i, (s, t) in enumerate(zip((dwq, dwkv), dw_out))]
        for copy in stored:
            copy.start()
        for copy in stored:
            copy.wait()

    out_load[0].wait()
    out_from_side[0].wait_recv()

    @pl.loop(0, CHUNKS)
    def _(k):
        out_mine[0, k] = (out_mine[0, k].astype(f32) + out_side[0, k].astype(f32)).astype(bf16)

    out_from_across.start()

    def early(numbers, k):
        for a in numbers:
            if a < count:
                early_spreads[a].step(k)

    def onward(turn):
        for a, ring in enumerate(late):
            ahead = 2 if a == 0 else 0
            if turn < RING - 1:
                if turn + ahead < RING - 1:
                    ring.step(turn + ahead)
                if turn == RING - 2:
                    late_spreads[a].start()
            else:
                late_spreads[a].step(turn - (RING - 1))

    early((0,), 0)

    @pl.loop(0, CHUNKS)
    def _(k):
        terms[at(own, k)] = term(1, k).astype(bf16)
        side1(k).start()
        grad_ref[at(0, k)] = term(0, k)

    onward(0)
    early((1, 2), 0)
    onward(1)

    def tokens_back():
        for copy in fetch[7:9]:
            copy.wait()
        gain_sum[...] = jnp.zeros_like(gain_sum)
        gain_sum[1:2] = jnp.sum(gain_two[...], axis=0, keepdims=True)

        @pl.loop(0, CHUNKS)
        def _(k):
            side1(k).wait_recv()
            across(k).wait_recv()
            here = at(0, k)
            grad = grad_ref[here] + cr[1, here].astype(f32) + xr[here].astype(f32)
            back, sums = rows_back(grad, tokens[here].astype(f32), gain[...])
            grad_ref[here] = grad_one[here] + back
            gain_sum[0:1] += jnp.sum(sums, axis=0, keepdims=True)

        gain_copy(0).start()

    def gain_copy(stage):
        to = [partner(1), partner(2)] + ([flip(1), flip(2), flip(4)] if count else [])
        return pltpu.make_async_remote_copy(
            src_ref=gain_sum,
            dst_ref=gain_land.at[stage],
            send_sem=gain_send.at[stage],
            recv_sem=gain_recv.at[stage],
            device_id=to[stage],
            device_id_type=pl.DeviceIdType.MESH,
        )

    def gain_add(stage):
        gain_copy(stage).wait()
        gain_sum[...] += gain_land[stage]

    def output():
        fetch[9].wait()
        out_load[1].wait()
        out_from_side[1].wait_recv()
        out_from_across.wait_recv()

        @pl.loop(0, CHUNKS)
        def _(k):
            total = out_mine[1, k].astype(f32) + out_side[1, k].astype(f32) + out_across[k].astype(f32)
            out_ref[k] = (hid1[k] + total).astype(bf16)

    for turn in range(1, RING - 1):
        if turn == 2:
            tokens_back()
        if turn == 3:
            gain_add(0)
            gain_copy(1).start()
        if turn == 4:
            gain_add(1)
            if count:
                gain_copy(2).start()
            output()
        if turn == 5 and count:
            gain_add(2)
            gain_copy(3).start()
        if turn == 6 and count:
            gain_add(3)
            gain_copy(4).start()
        early((0,), turn)
        if count:
            onward(2 * turn)
        early((1, 2), turn)
        if count:
            onward(2 * turn + 1)
    if count:
        gain_add(4)
    for ring in (*reduces, *late, *early_spreads, *late_spreads):
        ring.finish()
    gains_ref[...] = gain_sum[...]

    @pl.loop(0, CHUNKS)
    def _(k):
        side0(k).wait_send()
        side1(k).wait_send()
        across(k).wait_send()

    for k in range(2):
        out_from_side[k].wait_send()
    out_from_across.wait_send()


def end(dq, dk, dv, wq, wk, wv, attn_in, tokens, grad_one, hid1, gains, gain_two, parts_in, parts, states, dwo, cuts):
    own, width = tokens.shape
    count = len(parts)
    sds = jax.ShapeDtypeStruct
    pieces = hid1.shape
    loaded = (dq, dk, dv, wq, wk, wv, attn_in, tokens, grad_one, hid1)
    qkv_shapes = [(2, RING, width // (2 * RING), c) for c in cuts]
    late = [dwo] if count else []
    ring_shapes = [*[p.shape for p in parts], dwo.shape, *qkv_shapes] if count else qkv_shapes
    ring_buffers = []
    for p in parts:
        ring_buffers += ring_scratch(p.shape, RING - 1 - IN_BACK, True)
    if count:
        ring_buffers += ring_scratch(dwo.shape, RING - 1, True)
        for shape in qkv_shapes:
            ring_buffers += ring_scratch(shape, RING - 1, False)
        for _ in ring_shapes:
            ring_buffers += [pltpu.SemaphoreType.DMA((2, RING - 1))] * 2 + [pltpu.SemaphoreType.DMA((2,))]
    stages = 5 if count else 2
    outs = pl.pallas_call(
        functools.partial(end_kernel, count),
        in_specs=[ANY] * 10 + [VMEM] * 2 + [ANY] * (1 + 2 * count + len(late)),
        out_specs=[VMEM] * 3 + [ANY] * len(ring_shapes),
        out_shape=[
            sds((own, width), f32),
            sds((8, width), f32),
            sds(pieces, bf16),
            *[sds(shape, bf16) for shape in ring_shapes],
        ],
        scratch_shapes=[
            *[pltpu.VMEM(t.shape, t.dtype) for t in loaded],
            pltpu.VMEM((3 * own, width), bf16),
            pltpu.VMEM((2, own, width), bf16),
            pltpu.VMEM((own, width), bf16),
            pltpu.VMEM((2, *pieces), bf16),
            pltpu.VMEM((2, *pieces), bf16),
            pltpu.VMEM(pieces, bf16),
            pltpu.VMEM((8, width), f32),
            pltpu.VMEM((stages, 8, width), f32),
            *[pltpu.VMEM(shape, bf16) for shape in qkv_shapes],
            *dma_sems(4, max(CHUNKS, 3)),
            pltpu.SemaphoreType.DMA((4,)),
            *dma_sems(stages),
            pltpu.SemaphoreType.DMA((10,)),
            *ring_buffers,
        ],
        compiler_params=comm_params(3),
        cost_estimate=cost(150e-6 * 1e15, 60e6),
        name="end",
    )(*loaded, gains, gain_two, parts_in, *parts, *states, *late)
    return outs[:3], outs[3:]


def body(
    tokens, segments, positions, norm_attn, w_query, key_weight, value_weight, w_out,
    norm_mlp, w_gate, w_up, w_down, cotangent,
):
    seq = segments.shape[0]
    own, width = tokens.shape
    blocks = 4
    heads_q, heads_k = w_query.shape[1], key_weight.shape[1]
    gains = jnp.stack([norm_attn, norm_mlp])

    qkv, attn_in, attended, lse, cots, wq, wk, wv, wo, cos, sin, start = front(
        tokens, gains, w_query, key_weight, value_weight, w_out, segments.reshape(1, seq), positions.reshape(seq, 1),
        cotangent, blocks,
    )
    ringed = lax.axis_size("dp") == RING
    hid1, grad_attended, parts, grad_one, dwd, dwg, dwu, dwo, gain_two, *states = middle(
        attended, wo, tokens, gains, cotangent, cots, w_gate, w_up, w_down, ringed
    )
    grad_attended = grad_attended.reshape(seq, -1)
    dwo = dot(spread(heads_q // HEAD_SIZE), dwo).astype(bf16)
    chunks = lambda t: t.reshape(2, RING, t.shape[0] // (2 * RING), t.shape[1])
    early = [chunks(t) for t in (dwd, dwg, dwu)] if ringed else []
    (dq, dk, dv), states = attend_back(
        qkv, attended, grad_attended, lse, start, cos, sin, early, states, blocks
    )
    (grad_tokens, gain_grads, output), sums = end(
        dq, dk, dv, wq, wk, wv, attn_in.reshape(seq, width), tokens, grad_one.reshape(own, width), hid1, gains,
        gain_two, parts, early, states, chunks(dwo) if ringed else None, (heads_q, 2 * heads_k),
    )
    output = output.reshape(own, width)
    if not ringed:
        gain_grads = lax.psum(gain_grads, "dp")
        sums = [lax.psum(t, "dp") for t in (dwd, dwg, dwu, dwo, *sums)]
    down, gate, up, out, query, both = [t.reshape(-1, t.shape[-1]) for t in sums]
    key, value = both[:, :heads_k], both[:, heads_k:]
    return (
        output, grad_tokens, gain_grads[0],
        *[t.astype(f32) for t in (query, key, value, out)],
        gain_grads[1], *[t.astype(f32) for t in (gate, up, down)],
    )


def solution(mesh):
    rows, cols, both = P("tensor", None), P(None, "tensor"), P(("dp", "tensor"), None)
    in_specs = (both, P("dp"), P("dp"), P(), cols, cols, cols, rows, P(), cols, cols, rows, both)
    out_specs = (both, both, P(), cols, cols, cols, rows, P(), cols, cols, rows)
    return jax.shard_map(body, mesh=mesh, in_specs=in_specs, out_specs=out_specs, check_vma=False)
```

```python
import functools
import math

import jax
import jax.numpy as jnp
from jax import lax
from jax.experimental import pallas as pl
from jax.experimental.pallas import tpu as pltpu
from jax.sharding import PartitionSpec as P

HEAD_SIZE = 96
HALF = HEAD_SIZE // 2
LANES = 128
epsilon = 1e-05
rope_base = 100000.0
masked_value = -1e30
score_scale = 1.0 / math.sqrt(HEAD_SIZE)
log2_e = math.log2(math.e)
bf16, f32 = jnp.bfloat16, jnp.float32
NN = (((1,), (0,)), ((), ()))
NT = (((1,), (1,)), ((), ()))
TN = (((0,), (0,)), ((), ()))
VMEM_LIMIT = 67043328
CHUNKS = 4


def dot(left, right, dims=NN):
    return lax.dot_general(left, right, dims, preferred_element_type=f32)


def params():
    return pltpu.CompilerParams(vmem_limit_bytes=VMEM_LIMIT)


def cost(flops, nbytes):
    return pl.CostEstimate(flops=int(flops), bytes_accessed=int(nbytes), transcendentals=0)


def whole(shape):
    return pl.BlockSpec(shape, lambda *_: (0,) * len(shape), pipeline_mode=pl.Buffered(1))


ANY = pl.BlockSpec(memory_space=pl.ANY)
VMEM = pl.BlockSpec(memory_space=pltpu.VMEM)


def peer(bits):
    me = lax.axis_index("tensor")
    low, high = lax.rem(me, 2), lax.div(me, 2)
    if bits % 2:
        low = 1 - low
    if bits // 2:
        high = 1 - high
    return 2 * high + low


def partner(bits):
    return {"tensor": peer(bits)}


def send(source, target, sems, at, bits):
    return pltpu.make_async_remote_copy(
        src_ref=source,
        dst_ref=target,
        send_sem=sems[0].at[at],
        recv_sem=sems[1].at[at],
        device_id=partner(bits),
        device_id_type=pl.DeviceIdType.MESH,
    )


def meet(*others):
    barrier = pltpu.get_barrier_semaphore()
    for other in others:
        pl.semaphore_signal(barrier, inc=1, device_id=other, device_id_type=pl.DeviceIdType.MESH)
    pl.semaphore_wait(barrier, len(others))


RING = 8
IN_MIDDLE = (6, 3, 3)


def ring_place():
    index = lax.axis_index("dp")
    deep, wide = lax.div(index, 2), lax.rem(index, 2)
    return deep + wide * (RING - 1 - 2 * deep)


def ring_peer(way):
    place = lax.rem(ring_place() + (1, RING - 1)[way], RING)
    wide = lax.div(place, RING // 2)
    return {"dp": 2 * (place + wide * (RING - 1 - 2 * place)) + wide}


def ring_chunk(way, step):
    return lax.rem(ring_place() + (2 * RING - step if way == 0 else step), RING)


def ring_send(source, target, sems, at, way):
    return pltpu.make_async_remote_copy(
        src_ref=source,
        dst_ref=target,
        send_sem=sems[0].at[at],
        recv_sem=sems[1].at[at],
        device_id=ring_peer(way),
        device_id_type=pl.DeviceIdType.MESH,
    )


class Reduce:
    def __init__(self, parts, state, land, mine, first, last, send_sem, recv_sem, load_sem=None):
        self.parts, self.state, self.land, self.mine = parts, state, land, mine
        self.first, self.count, self.sems, self.load_sem = first, last - first, (send_sem, recv_sem), load_sem

    def begin(self, way):
        source = self.parts.at[way, ring_chunk(way, 0)] if self.state is None else self.state.at[way]
        return ring_send(source, self.land(way, 0), self.sems, (way, 0), way)

    def copy(self, way, k):
        return ring_send(self.land(way, k - 1), self.land(way, k), self.sems, (way, k), way)

    def load(self, way, k):
        source = self.parts.at[way, ring_chunk(way, self.first + k + 1)]
        return pltpu.make_async_copy(source, self.mine(way, k), self.load_sem.at[way, k])

    def start(self):
        for way in range(2):
            self.begin(way).start()

    def prefetch(self, steps=None):
        for k in steps or range(self.count):
            for way in range(2):
                self.load(way, k).start()

    def step(self, k):
        for way in range(2):
            here = self.land(way, k)
            ring_send(here, here, self.sems, (way, k), way).wait_recv()
            if self.mine is None:
                own = self.parts[way, ring_chunk(way, self.first + k + 1)]
            else:
                self.load(way, k).wait()
                own = self.mine(way, k)[...]
            here[...] = (here[...].astype(f32) + own.astype(f32)).astype(bf16)
            if not isinstance(k, int) or k + 1 < self.count:
                self.copy(way, k + 1).start()

    def result(self, way):
        return self.land(way, self.count - 1)

    def finish(self):
        for way in range(2):
            self.begin(way).wait_send()
            for k in range(1, self.count):
                self.copy(way, k).wait_send()


class Spread:
    def __init__(self, reduced, full, send_sem, recv_sem, own_sem):
        self.reduced, self.full, self.sems, self.own_sem = reduced, full, (send_sem, recv_sem), own_sem

    def slot(self, way, step):
        return self.full.at[way, ring_chunk(way, step + RING - 1)]

    def keep(self, way):
        return pltpu.make_async_copy(self.reduced.result(way), self.slot(way, 0), self.own_sem.at[way])

    def copy(self, way, k):
        source = self.slot(way, k) if k else self.reduced.result(way)
        return ring_send(source, self.slot(way, k), self.sems, (way, k), way)

    def start(self):
        for way in range(2):
            self.copy(way, 0).start()
            self.keep(way).start()

    def step(self, k):
        for way in range(2):
            ring_send(self.slot(way, k + 1), self.slot(way, k + 1), self.sems, (way, k), way).wait_recv()
            if k < RING - 2:
                self.copy(way, k + 1).start()

    def finish(self):
        for way in range(2):
            self.keep(way).wait()
            for k in range(RING - 1):
                self.copy(way, k).wait_send()


class Reduced:
    def __init__(self, state):
        self.state = state

    def result(self, way):
        return self.state.at[way]


def slots(ref):
    return lambda way, k: ref.at[way, k]


def ring_scratch(shape, steps, loads):
    rows, cols = shape[2:]
    land = pltpu.VMEM((2, steps, rows, cols), bf16)
    sems = [pltpu.SemaphoreType.DMA((2, steps))] * (3 if loads else 2)
    return [land] * (2 if loads else 1) + sems


def as_row(ref):
    return jnp.concatenate([ref[i : i + 1, :] for i in range(ref.shape[0])], axis=1)


def comm_params(number):
    return pltpu.CompilerParams(vmem_limit_bytes=VMEM_LIMIT, collective_id=number, has_side_effects=True)


def dma_sems(*shape):
    return [pltpu.SemaphoreType.DMA(shape)] * 2


def spread(heads, turned=False):
    shape = (heads * HEAD_SIZE, heads * LANES)
    feature = lax.broadcasted_iota(jnp.int32, shape[::-1] if turned else shape, int(turned))
    lane = lax.broadcasted_iota(jnp.int32, shape[::-1] if turned else shape, 1 - int(turned))
    target = feature
    for half in range(1, 2 * heads):
        target += jnp.where(feature >= half * HALF, LANES // 2 - HALF, 0)
    return jnp.where(lane == target, 1.0, 0.0).astype(bf16)


def front_kernel(
    tokens, gain_ref, w_query, key_turned, value_turned, w_out, segments, positions, cot,
    qkv_out, stack_out, att_out, lse_out, cots, wq_out, wk_out, wv_out, wo_out, cos_out, sin_out, start_out,
    x, land, qkv, att, wq, wk, wv, wo, cos_v, sin_v, send_sem, recv_sem, store_sem,
    *, blocks,
):
    sems = (send_sem, recv_sem)
    own, width = tokens.shape
    rows = own // CHUNKS
    seq = qkv.shape[0]
    size = seq // blocks

    def piece(k):
        return pl.ds(pl.multiple_of(k * rows, rows), rows)

    side = send(x, land.at[0], sems, (0, 0), 1)
    across = lambda k: send(x.at[piece(k)], land.at[1, piece(k)], sems, (1, k), 2)
    onward = lambda k: send(land.at[1, piece(k)], land.at[2, piece(k)], sems, (2, k), 1)
    cot_side = send(cot, cots.at[0], sems, (3, 0), 1)
    cot_across = lambda k: send(cot.at[k], cots.at[1, k], sems, (4, k), 2)
    cot_onward = lambda k: send(cots.at[1, k], cots.at[2, k], sems, (5, k), 1)
    stores = []

    def store(source, target):
        copy = pltpu.make_async_copy(source, target, store_sem.at[len(stores)])
        copy.start()
        stores.append(copy)

    gain = as_row(gain_ref)
    meet(partner(1), partner(2))

    @pl.loop(0, CHUNKS)
    def _(k):
        inputs = tokens[piece(k)].astype(f32)
        inverse = lax.rsqrt(jnp.mean(inputs * inputs, axis=-1, keepdims=True) + epsilon)
        x[piece(k)] = (inputs * inverse * gain).astype(bf16)
        across(k).start()

    side.start()
    store(x, stack_out.at[0])

    spread_q, spread_k = spread(w_query.shape[1] // HEAD_SIZE), spread(key_turned.shape[0] // HEAD_SIZE)
    for source, matrix, dims, target, out in (
        (w_query, spread_q, NN, wq, wq_out),
        (key_turned, spread_k, TN, wk, wk_out),
        (value_turned, spread_k, TN, wv, wv_out),
    ):
        target[...] = dot(source[...], matrix, dims).astype(bf16)
        store(target, out)
    wo[...] = dot(spread(w_query.shape[1] // HEAD_SIZE, True), w_out[...]).astype(bf16)
    store(wo, wo_out)

    lane = lax.broadcasted_iota(jnp.int32, (1, LANES), 1)
    feature = jnp.where(lane < LANES // 2, lane, lane - LANES // 2)
    frequency = jnp.exp(feature.astype(f32) * (-2.0 * math.log(rope_base) / HEAD_SIZE))
    frequency = jnp.where(feature < HALF, frequency, 0.0)
    sign = jnp.where(lane < LANES // 2, -1.0, 1.0)
    per_own = own // LANES
    for p in range(4):

        @pl.loop(0, per_own)
        def _(k):
            row = positions[pl.ds(peer(p) * per_own + k, 1), :].astype(f32)
            angles = jnp.broadcast_to(row, (LANES, LANES)).T * frequency
            here = pl.ds(pl.multiple_of(p * own + k * LANES, LANES), LANES)
            cos_v[here] = jnp.cos(angles)
            sin_v[here] = jnp.sin(angles) * sign

    store(cos_v, cos_out)
    store(sin_v, sin_out)
    documents = segments[...].astype(f32)
    starts = jnp.zeros_like(documents)
    for document in (1, 2, 3):
        first = jnp.where(documents < document, 1.0, 0.0)
        first = jnp.sum(jnp.sum(first, axis=0, keepdims=True), axis=1, keepdims=True)
        starts = jnp.where(documents >= document, first, starts)
    starts = starts.astype(jnp.int32)
    for i in range(seq // LANES):
        start_out[:, i * LANES : (i + 1) * LANES] = starts[i : i + 1, :]

    head_lane = lax.broadcasted_iota(jnp.int32, (rows, LANES), 1)

    def project(ref, base):
        values = ref[...]
        here = pl.ds(pl.multiple_of(base, rows), rows)
        cos, sin = cos_v[here], sin_v[here]
        for w, first, turn in ((wq, 0, True), (wk, 4, True), (wv, 6, False)):
            y = dot(values, w[...])
            for h in range(w.shape[1] // LANES):
                v = y[:, h * LANES : (h + 1) * LANES]
                if turn:
                    v = v * cos + pltpu.roll(v, LANES // 2, 1) * sin
                else:
                    v = jnp.where(head_lane == HALF, 1.0, v)
                at = (first + h) * LANES
                qkv[here, at : at + LANES] = v.astype(bf16)

    @pl.loop(0, CHUNKS)
    def _(k):
        project(x.at[piece(k)], k * rows)

    side.wait_recv()
    store(land.at[0], stack_out.at[1])
    cot_side.start()

    @pl.loop(0, CHUNKS)
    def _(k):
        project(land.at[0, piece(k)], own + k * rows)

    @pl.loop(0, CHUNKS)
    def _(k):
        across(k).wait_recv()
        onward(k).start()
        cot_across(k).start()
        project(land.at[1, piece(k)], 2 * own + k * rows)
        onward(k).wait_recv()
        project(land.at[2, piece(k)], 3 * own + k * rows)

    store(land.at[1], stack_out.at[2])
    store(land.at[2], stack_out.at[3])
    store(qkv, qkv_out)

    @pl.loop(0, 2)
    def _(g):
        for i in range(blocks):
            at = pl.ds(pl.multiple_of(peer(i) * size, size), size)
            cols = [pl.ds(pl.multiple_of((2 * g + r) * LANES, LANES), LANES) for r in range(2)]
            queries = [qkv[at, cols[r]] for r in range(2)]
            start = start_out[:, i * size : (i + 1) * size]
            state = [None, None]
            for j in [i, *range(i)]:
                key_at = pl.ds(pl.multiple_of(peer(j) * size, size), size)
                keys = qkv[key_at, pl.ds(pl.multiple_of((4 + g) * LANES, LANES), LANES)]
                values = qkv[key_at, pl.ds(pl.multiple_of((6 + g) * LANES, LANES), LANES)]
                key_rows = lax.broadcasted_iota(jnp.int32, (size, size), 0)
                allowed = key_rows >= start - j * size
                if j == i:
                    allowed &= key_rows <= lax.broadcasted_iota(jnp.int32, (size, size), 1)
                for r in range(2):
                    scores = jnp.where(allowed, dot(keys, queries[r], NT) * (score_scale * log2_e), masked_value)
                    peak = jnp.max(scores, axis=0, keepdims=True)
                    if state[r] is not None:
                        peak = jnp.maximum(state[r][0], peak)
                    weights = jnp.exp2(scores - peak)
                    mixed = dot(values, weights.astype(bf16), TN)
                    if state[r] is not None:
                        mixed += state[r][1] * jnp.exp2(state[r][0] - peak)
                    state[r] = (peak, mixed)
            for r, (peak, mixed) in enumerate(state):
                total = mixed[HALF : HALF + 1, :]
                att[at, cols[r]] = (mixed / total).T.astype(bf16)
                lse_out[g, r : r + 1, at] = peak + jnp.log2(total)

    store(att, att_out)
    for k in range(CHUNKS):
        cot_across(k).wait_recv()
        cot_onward(k).start()
    side.wait_send()
    cot_side.wait()
    for k in range(CHUNKS):
        across(k).wait_send()
        onward(k).wait_send()
        cot_across(k).wait_send()
        cot_onward(k).wait()
    for copy in stores:
        copy.wait()


def front(tokens, gain, w_query, key_turned, value_turned, w_out, segments, positions, cot, blocks):
    own, width = tokens.shape
    seq = segments.shape[0] * LANES
    pieces = (CHUNKS, own // CHUNKS, width)
    sds = jax.ShapeDtypeStruct
    heads = 4 * LANES
    arrays = dict(
        qkv=(seq, 8 * LANES), att=(seq, heads), wq=(width, heads), wk=(width, heads // 2), wv=(width, heads // 2),
        wo=(heads, width),
    )
    low = lambda name: sds(arrays[name], bf16)
    scratch = lambda name: pltpu.VMEM(arrays[name], bf16)
    table = sds((seq, LANES), f32)
    return pl.pallas_call(
        functools.partial(front_kernel, blocks=blocks),
        in_specs=[VMEM] * 8 + [ANY],
        out_specs=[ANY] * 3 + [VMEM] + [ANY] * 7 + [VMEM],
        out_shape=[
            low("qkv"), sds((4, own, width), bf16), low("att"), sds((2, 2, seq), f32), sds((3, *pieces), bf16),
            low("wq"), low("wk"), low("wv"), low("wo"), table, table, sds((1, seq), jnp.int32),
        ],
        scratch_shapes=[
            pltpu.VMEM((own, width), bf16),
            pltpu.VMEM((3, own, width), bf16),
            *[scratch(name) for name in arrays],
            pltpu.VMEM((seq, LANES), f32),
            pltpu.VMEM((seq, LANES), f32),
            *dma_sems(6, CHUNKS),
            pltpu.SemaphoreType.DMA((12,)),
        ],
        compiler_params=comm_params(1),
        cost_estimate=cost(80e-6 * 1e15, 40e6),
        name="front",
    )(tokens, gain, w_query, key_turned, value_turned, w_out, segments, positions, cot.reshape(pieces))


def attend_back_kernel(count, *refs, blocks, size):
    q_ref, k_ref, v_ref, o_ref, do_ref, lse_ref, start_ref, cos_ref, sin_ref, *rest = refs
    parts, befores, rest = rest[:count], rest[count : 2 * count], rest[2 * count :]
    dq_ref, dk_ref, dv_ref, *rest = rest
    states, rest = rest[:count], rest[count:]
    dq_sum, dk_sum, dv_sum, inner, *rest = rest
    rings = []
    for a in range(count):
        land, mine, *own_sems = rest[5 * a : 5 * a + 5]
        rings.append(Reduce(parts[a], befores[a], slots(land), slots(mine), IN_MIDDLE[a], RING - 1, *own_sems))
    keep_sem = rest[-1] if count else None

    def keep(a, way):
        return pltpu.make_async_copy(rings[a].result(way), states[a].at[way], keep_sem.at[a, way])

    if count:

        @pl.when(pl.program_id(0) == 0)
        def _():
            meet(ring_peer(0), ring_peer(1))
            for ring in sorted(rings, key=lambda ring: -ring.count):
                ring.start()
            for ring in rings:
                ring.prefetch()

    pairs = blocks * (blocks + 1) // 2
    hooks = {}
    turns = sorted((k, -rings[a].count, a) for a in range(count) for k in range(rings[a].count))
    for number, (k, _, a) in enumerate(turns):
        hooks.setdefault(min(round((number + 1) * 2.1) + 1, 2 * pairs - 1), []).append((a, k))

    def hook(pair):
        for half in range(2):
            todo = hooks.get(half * pairs + pair, [])
            if todo:

                @pl.when(pl.program_id(0) == half)
                def _():
                    for a, k in todo:
                        rings[a].step(k)
                        if k == rings[a].count - 1:
                            keep(a, 0).start()
                            keep(a, 1).start()

    for c in range(blocks):
        rows = slice(c * size, (c + 1) * size)
        for r in range(2):
            cols = slice(r * LANES, (r + 1) * LANES)
            product = do_ref[rows, cols].astype(f32) * o_ref[rows, cols].astype(f32)
            inner[r : r + 1, rows] = jnp.sum(product.T, axis=0, keepdims=True)
    for i in reversed(range(blocks)):
        for j in [i, *range(i)]:
            at = pl.multiple_of(peer(i) * size, size)
            key_at = pl.multiple_of(peer(j) * size, size)
            keys = k_ref[pl.ds(key_at, size), :]
            values = v_ref[pl.ds(key_at, size), :]
            start = start_ref[:, i * size : (i + 1) * size]
            key_rows = lax.broadcasted_iota(jnp.int32, (size, size), 0)
            allowed = key_rows >= start - j * size
            if j == i:
                allowed &= key_rows <= lax.broadcasted_iota(jnp.int32, (size, size), 1)
            dk = dv = None
            for r in range(2):
                cols = slice(r * LANES, (r + 1) * LANES)
                queries = q_ref[pl.ds(at, size), cols]
                grads = do_ref[pl.ds(at, size), cols]
                scores = jnp.where(allowed, dot(keys, queries, NT) * (score_scale * log2_e), masked_value)
                weights = jnp.exp2(scores - lse_ref[0, r : r + 1, pl.ds(at, size)])
                grad_weights = dot(values, grads, NT)
                grad_scores = (weights * (grad_weights - inner[r : r + 1, pl.ds(at, size)])).astype(bf16)
                dv_term = dot(weights.astype(bf16), grads)
                dk_term = dot(grad_scores, queries)
                dv = dv_term if dv is None else dv + dv_term
                dk = dk_term if dk is None else dk + dk_term
                dq = dot(grad_scores, keys, TN)
                if j == i:
                    dq_sum[pl.ds(at, size), cols] = dq
                else:
                    dq_sum[pl.ds(at, size), cols] += dq
            if i == blocks - 1:
                dk_sum[pl.ds(key_at, size), :] = dk
                dv_sum[pl.ds(key_at, size), :] = dv
            else:
                dk_sum[pl.ds(key_at, size), :] += dk
                dv_sum[pl.ds(key_at, size), :] += dv
            hook(sum(range(blocks, i + 1, -1)) + (0 if j == i else j + 1))
    for c in range(blocks):
        rows = slice(c * size, (c + 1) * size)
        cos, sin = cos_ref[rows, :], sin_ref[rows, :]

        def back(grads):
            return ((grads * cos - pltpu.roll(grads, LANES // 2, 1) * sin) * score_scale).astype(bf16)

        for r in range(2):
            cols = slice(r * LANES, (r + 1) * LANES)
            dq_ref[rows, cols] = back(dq_sum[rows, cols])
        dk_ref[rows, :] = back(dk_sum[rows, :])
        dv_ref[rows, :] = dv_sum[rows, :].astype(bf16)

    if count:

        @pl.when(pl.program_id(0) == 1)
        def _():
            for a, ring in enumerate(rings):
                ring.finish()
                keep(a, 0).wait()
                keep(a, 1).wait()


def attend_back(qkv, attended, grads, lse, start, cos, sin, parts, befores, blocks):
    seq = qkv.shape[0]
    pair = pl.BlockSpec((seq, 2 * LANES), lambda g: (0, g))
    single = pl.BlockSpec((seq, LANES), lambda g: (0, g))
    table = pl.BlockSpec((seq, LANES), lambda g: (0, 0))
    count = len(parts)
    outs = pl.pallas_call(
        functools.partial(attend_back_kernel, count, blocks=blocks, size=seq // blocks),
        grid=(2,),
        in_specs=[
            pair,
            pl.BlockSpec((seq, LANES), lambda g: (0, 4 + g)),
            pl.BlockSpec((seq, LANES), lambda g: (0, 6 + g)),
            pair,
            pair,
            pl.BlockSpec((1, 2, seq), lambda g: (g, 0, 0)),
            pl.BlockSpec((1, seq), lambda g: (0, 0)),
            table,
            table,
            *[ANY] * (2 * count),
        ],
        out_specs=[pair, single, single, *[ANY] * count],
        scratch_shapes=[
            pltpu.VMEM((seq, 2 * LANES), f32),
            pltpu.VMEM((seq, LANES), f32),
            pltpu.VMEM((seq, LANES), f32),
            pltpu.VMEM((2, seq), f32),
            *[x for p, n in zip(parts, IN_MIDDLE) for x in ring_scratch(p.shape, RING - 1 - n, True)],
            *[pltpu.SemaphoreType.DMA((count, 2))] * bool(count),
        ],
        out_shape=[
            jax.ShapeDtypeStruct((seq, 4 * LANES), bf16),
            jax.ShapeDtypeStruct((seq, 2 * LANES), bf16),
            jax.ShapeDtypeStruct((seq, 2 * LANES), bf16),
            *[jax.ShapeDtypeStruct((2, *p.shape[2:]), bf16) for p in parts],
        ],
        compiler_params=comm_params(5) if count else params(),
        cost_estimate=cost(5 * 2 * 4 * LANES * seq * seq, 10 * seq * 8 * LANES),
        name="attention_back",
    )(qkv, qkv, qkv, attended, grads, lse, start, cos, sin, *parts, *befores)
    return outs[:3], outs[3:]


def rows_back(grad, inputs, gain):
    inverse = lax.rsqrt(jnp.mean(inputs * inputs, axis=-1, keepdims=True) + epsilon)
    unit = inputs * inverse
    scaled = grad * gain
    back = inverse * (scaled - unit * jnp.mean(scaled * unit, axis=-1, keepdims=True))
    return back, jnp.sum((grad * unit).reshape(-1, 8, grad.shape[-1]), axis=0)

RS1_C0, RS1_C1, RS1_X, AG2_X, AG2_C, AG2_F, RS3_C0, RS3_C1, RS3_X, AG3_X, AG3_C, AG3_F = range(12)


class _Chunks:
    def __init__(self, ref):
        self.ref, self.rows = ref, ref.shape[0] // (2 * RING)

    @property
    def at(self):
        return self

    def __getitem__(self, index):
        way, chunk = index
        return self.ref.at[pl.ds(pl.multiple_of((way * RING + chunk) * self.rows, self.rows), self.rows)]


def middle_kernel(
    ringed, att, wo, gain_ref, tokens, cot_own, cots, wg_in, wu_in, wd_in,
    hid1, datt_out, parts_out, grad_one_out, dwd_out, dwg_out, dwu_out, dwo_out, gain_grad, *refs,
):
    states, refs = (refs[:3], refs[3:]) if ringed else ([], refs)
    (
        xs, cot, hid, gg, gu, g, cr, xr, part_stage, grad_stage, datt_stage, tile_stage, wg, wu, wd,
        send_sem, recv_sem, cot_sem, part_sem, grad_sem, datt_sem, tile_sem, free_sem, *ring_sems,
    ) = refs
    gain = as_row(gain_ref)
    pieces, _, n, width = xs.shape
    units = wg.shape[1]
    heads = wo.shape[0]
    sems = (send_sem, recv_sem)
    two = (2 * n, width)

    def copy(kind, k):
        source, target, bits = {
            RS1_C0: (g.at[k, 3], cr.at[k, 0], 1),
            RS1_C1: (g.at[k, 1], cr.at[k, 1], 1),
            RS1_X: (g.at[k, 2], xr.at[k], 2),
            AG2_X: (xs.at[k, 0], xs.at[k, 2], 2),
            AG2_C: (xs.at[k, 0], xs.at[k, 1], 1),
            AG2_F: (xs.at[k, 2], xs.at[k, 3], 1),
            RS3_C0: (g.at[k, 3], cr.at[k, 0], 1),
            RS3_C1: (g.at[k, 1], cr.at[k, 1], 1),
            RS3_X: (g.at[k, 2], xr.at[k], 2),
            AG3_X: (g.at[k, 0], g.at[k, 2], 2),
            AG3_C: (g.at[k, 0], g.at[k, 1], 1),
            AG3_F: (g.at[k, 2], g.at[k, 3], 1),
        }[kind]
        return send(source, target, sems, (kind, k), bits)

    def credit(k, bits):
        pl.semaphore_signal(
            free_sem.at[bits - 1, k], inc=1, device_id=partner(bits), device_id_type=pl.DeviceIdType.MESH
        )

    def cot_copy(p):
        if p >= 4:
            source, target = ((wg_in, wg), (wu_in, wu), (wd_in, wd), (tokens, xs.at[:, 3]))[p - 4]
            return pltpu.make_async_copy(source, target, cot_sem.at[p])
        source = cot_own if p == 0 else cots.at[p - 1]
        return pltpu.make_async_copy(source, cot.at[:, p], cot_sem.at[p])

    def part_copy(k, low):
        return pltpu.make_async_copy(part_stage.at[low // 2], parts_out.at[k, pl.ds(low, 2)], part_sem.at[low // 2])

    for p in (7, 4, 5, 6, 0, 1, 2, 3):
        cot_copy(p).start()
    meet(partner(1), partner(2), *([ring_peer(0), ring_peer(1)] if ringed else []))

    @pl.loop(0, pieces)
    def _(k):
        for p, kind in ((3, RS1_C0), (1, RS1_C1)):
            g[k, p] = dot(att[p, k], wo[...]).astype(bf16)
            copy(kind, k).start()

    def send_across(k):
        term = dot(att[2, k], wo[...])
        copy(RS1_C0, k).wait_recv()
        g[k, 2] = (term + cr[k, 0].astype(f32)).astype(bf16)
        copy(RS1_X, k).start()

    @pl.loop(0, 2)
    def _(k):
        send_across(k)

    def feed_forward(k, low):
        x = xs[k, pl.ds(low, 2)].reshape(two)
        gate = dot(x, wg[...])
        up = dot(x, wu[...])
        grad_hidden = dot(cot[k, pl.ds(low, 2)].reshape(two), wd[...], NT)
        sig = jax.nn.sigmoid(gate)
        act = gate * sig
        hidden = (act * up).astype(bf16)
        grad_gate = (grad_hidden * up * sig * (1.0 + gate * (1.0 - sig))).astype(bf16)
        grad_up = (grad_hidden * act).astype(bf16)
        hid[k, pl.ds(low, 2)] = hidden.reshape(2, n, units)
        gg[k, pl.ds(low, 2)] = grad_gate.reshape(2, n, units)
        gu[k, pl.ds(low, 2)] = grad_up.reshape(2, n, units)
        back = dot(grad_gate, wg[...], NT) + dot(grad_up, wu[...], NT)
        g[k, pl.ds(low, 2)] = back.astype(bf16).reshape(2, n, width)
        return hidden

    def out_part(k, low, hidden):
        part = dot(hidden, wd[...]).astype(bf16).reshape(2, n, width)

        @pl.when(k > 0)
        def _():
            part_copy(k - 1, low).wait()

        part_stage[low // 2] = part
        part_copy(k, low).start()

    for p in range(8):
        cot_copy(p).wait()

    def low_rows(k):
        term = dot(att[0, k], wo[...])
        copy(RS1_C1, k).wait_recv()
        copy(RS1_X, k).wait_recv()
        hidden = xs[k, 3].astype(f32) + (term + cr[k, 1].astype(f32) + xr[k].astype(f32))
        hid1[k] = hidden
        inverse = lax.rsqrt(jnp.mean(hidden * hidden, axis=-1, keepdims=True) + epsilon)
        xs[k, 0] = (hidden * inverse * gain).astype(bf16)
        copy(AG2_X, k).start()
        copy(AG2_C, k).start()

        @pl.when(k + 2 < pieces)
        def _():
            send_across(k + 2)

        copy(AG2_C, k).wait_recv()
        copy(RS1_C1, k).wait_send()
        out_part(k, 0, feed_forward(k, 0))

    def add_side(k):
        copy(RS3_C0, k).wait_recv()
        g[k, 2] = (g[k, 2].astype(f32) + cr[k, 0].astype(f32)).astype(bf16)
        copy(RS3_X, k).start()

    def high_rows(k):
        copy(AG2_X, k).wait_recv()
        copy(AG2_F, k).start()

        @pl.when(k >= 2)
        def _():
            add_side(k - 2)

        copy(AG2_F, k).wait_recv()
        copy(RS1_C0, k).wait_send()
        copy(RS1_X, k).wait_send()
        hidden = feed_forward(k, 2)
        copy(RS3_C0, k).start()
        copy(RS3_C1, k).start()
        out_part(k, 2, hidden)

    @pl.loop(0, pieces + 1)
    def _(k):
        @pl.when(k < pieces)
        def _():
            low_rows(k)

        @pl.when(k > 0)
        def _():
            high_rows(k - 1)

    @pl.loop(pieces - 2, pieces)
    def _(k):
        add_side(k)

    tokens_all = 4 * pieces * n

    def tile(slot, left, right, cols, out, at):
        height = out.shape[1]
        target = out.at[pl.ds(pl.multiple_of(at * 256, 256), 256)]
        move = pltpu.make_async_copy(tile_stage.at[slot, :, pl.ds(0, height)], target, tile_sem.at[slot])
        part = left[:, :, :, pl.ds(pl.multiple_of(at * 256, 256), 256)].reshape(tokens_all, 256)
        tile_stage[slot, :, pl.ds(0, height)] = dot(part, right[...].reshape(tokens_all, cols), TN).astype(bf16)
        return move

    def norm_back(k):
        copy(RS3_C1, k).wait_recv()
        copy(RS3_X, k).wait_recv()
        copy(RS3_C0, k).wait_send()
        copy(RS3_C1, k).wait_send()
        credit(k, 1)
        copy(RS3_X, k).wait_send()
        credit(k, 2)
        grad = g[k, 0].astype(f32) + cr[k, 1].astype(f32) + xr[k].astype(f32)
        back, sums = rows_back(grad, hid1[k], gain)
        result = cot[k, 0].astype(f32) + back
        g[k, 0] = result.astype(bf16)
        pl.semaphore_wait(free_sem.at[0, k], 1)
        pl.semaphore_wait(free_sem.at[1, k], 1)
        copy(AG3_X, k).start()
        copy(AG3_C, k).start()
        grad_stage[...] = result
        stored = pltpu.make_async_copy(grad_stage, grad_one_out.at[k], grad_sem.at[0])
        stored.start()

        @pl.when(k == 0)
        def _():
            gain_grad[...] = sums

        @pl.when(k > 0)
        def _():
            gain_grad[...] += sums

        return stored

    @pl.loop(0, 2)
    def _(k):
        first = tile(0, hid, cot, width, dwd_out, 2 * k)
        first.start()
        second = tile(1, hid, cot, width, dwd_out, 2 * k + 1)
        second.start()
        stored = norm_back(k)
        first.wait()
        second.wait()
        stored.wait()

    rings = []
    if ringed:
        n_down = dwd_out.shape[0] // (2 * RING)
        n_up = dwg_out.shape[0] // (2 * RING)

        def down_own(way, k):
            if isinstance(k, int) and k >= 4:
                return cr.at[k - 4, way, pl.ds(0, n_down)]
            return cot.at[k, 3, pl.ds(way * n_down, n_down)]

        places = (
            (lambda way, k: cot.at[k % 4, 1 + way, pl.ds(k // 4 * n_down, n_down)], down_own),
            (lambda way, k: hid.at[k, way, pl.ds(0, n_up)], lambda way, k: gg.at[k, way, pl.ds(0, n_up)]),
            (lambda way, k: hid.at[k, 2 + way, pl.ds(0, n_up)], lambda way, k: gu.at[k, way, pl.ds(0, n_up)]),
        )
        for a, (part, (land, mine)) in enumerate(zip((dwd_out, dwg_out, dwu_out), places)):
            rings.append(Reduce(_Chunks(part), None, land, mine, 0, IN_MIDDLE[a], *ring_sems[3 * a : 3 * a + 3]))
        for way in range(2):
            pl.semaphore_signal(
                free_sem.at[2, way], inc=1, device_id=ring_peer(1 - way), device_id_type=pl.DeviceIdType.MESH
            )
        for way in range(2):
            pl.semaphore_wait(free_sem.at[2, way], 1)
        rings[0].start()
        rings[0].prefetch(range(4))

    @pl.loop(0, 3)
    def _(j):
        for i in range(2):
            gate = tile(0, xs, gg, units, dwg_out, 2 * j + i)
            gate.start()
            up = tile(1, xs, gu, units, dwu_out, 2 * j + i)
            up.start()
            gate.wait()
            up.wait()

        @pl.when(j == 0)
        def _():
            norm_back(2).wait()

        if ringed:
            rings[0].step(j)

    if ringed:
        for ring in rings[1:]:
            ring.start()
        for ring in rings[1:]:
            ring.prefetch()
    norm_back(3).wait()
    if ringed:
        rings[0].prefetch(range(4, IN_MIDDLE[0]))

    for k in range(pieces):
        copy(AG3_X, k).wait_recv()
        copy(AG3_F, k).start()
        copy(AG3_C, k).wait_recv()
        copy(AG3_F, k).wait_recv()
        datt_stage[...] = dot(g[k].reshape(4 * n, width), wo[...], NT).astype(bf16).reshape(4, n, heads)
        moved = pltpu.make_async_copy(datt_stage, datt_out.at[:, k], datt_sem.at[0])
        moved.start()
        moved.wait()
        if ringed and k < 3:
            rings[1].step(k)
            rings[2].step(k)
            rings[0].step(3 + k)

    if ringed:
        for a, ring in enumerate(rings):
            for way in range(2):
                pltpu.make_async_copy(ring.result(way), states[a].at[way], ring_sems[-1].at[a, way]).start()
    merge = spread(2)
    tall = merge.shape[0]

    def out_tile(u):
        target = dwo_out.at[pl.ds(u * tall, tall)]
        return pltpu.make_async_copy(tile_stage.at[u, pl.ds(0, tall)], target, tile_sem.at[u])

    for u in range(heads // 256):
        total = None
        for p in range(4):
            left = att[p, :, :, u * 256 : (u + 1) * 256].reshape(pieces * n, 256)
            term = dot(left, g[:, p].reshape(pieces * n, width), TN)
            total = term if total is None else total + term
        tile_stage[u, 0:tall] = dot(merge, total.astype(bf16)).astype(bf16)
        out_tile(u).start()
    for u in range(heads // 256):
        out_tile(u).wait()

    if ringed:
        for a, ring in enumerate(rings):
            ring.finish()
            for way in range(2):
                pltpu.make_async_copy(ring.result(way), states[a].at[way], ring_sems[-1].at[a, way]).wait()

    for low in (0, 2):
        part_copy(pieces - 1, low).wait()

    @pl.loop(0, pieces)
    def _(k):
        for kind in (AG2_X, AG2_C, AG2_F, AG3_X, AG3_C, AG3_F):
            copy(kind, k).wait_send()


def middle(attended, wo, tokens, gain, cot_own, cots, wg, wu, wd, ringed):
    width, units, heads = wg.shape[0], wg.shape[1], wo.shape[0]
    pieces = CHUNKS
    n = tokens.shape[0] // pieces
    sds = jax.ShapeDtypeStruct
    own = (pieces, n, width)
    all_rows = (pieces, 4, n, width)
    all_units = (pieces, 4, n, units)
    chunk_down, chunk_up = (units // (2 * RING), width), (width // (2 * RING), units)
    states = [sds((2, *chunk), bf16) for chunk in (chunk_down, chunk_up, chunk_up)] if ringed else []
    return pl.pallas_call(
        functools.partial(middle_kernel, ringed),
        in_specs=[VMEM] * 3 + [ANY] * 6,
        out_specs=[VMEM] + [ANY] * 7 + [VMEM] + [ANY] * len(states),
        out_shape=[
            sds(own, f32),
            sds((4, pieces, n, heads), bf16),
            sds(all_rows, bf16),
            sds(own, f32),
            sds((units, width), bf16),
            sds((width, units), bf16),
            sds((width, units), bf16),
            sds((heads * HEAD_SIZE // LANES, width), bf16),
            sds((8, width), f32),
            *states,
        ],
        scratch_shapes=[
            pltpu.VMEM(all_rows, bf16),
            pltpu.VMEM(all_rows, bf16),
            pltpu.VMEM(all_units, bf16),
            pltpu.VMEM(all_units, bf16),
            pltpu.VMEM(all_units, bf16),
            pltpu.VMEM(all_rows, bf16),
            pltpu.VMEM((pieces, 2, n, width), bf16),
            pltpu.VMEM(own, bf16),
            pltpu.VMEM((2, 2, n, width), bf16),
            pltpu.VMEM((n, width), f32),
            pltpu.VMEM((4, n, heads), bf16),
            pltpu.VMEM((2, 256, width), bf16),
            *[pltpu.VMEM(w.shape, bf16) for w in (wg, wu, wd)],
            *dma_sems(12, pieces),
            pltpu.SemaphoreType.DMA((8,)),
            pltpu.SemaphoreType.DMA((2,)),
            pltpu.SemaphoreType.DMA((1,)),
            pltpu.SemaphoreType.DMA((1,)),
            pltpu.SemaphoreType.DMA((2,)),
            pltpu.SemaphoreType.REGULAR((3, pieces)),
            *([pltpu.SemaphoreType.DMA((2, n)) for n in IN_MIDDLE for _ in range(3)] + [pltpu.SemaphoreType.DMA((3, 2))]) * ringed,
        ],
        compiler_params=comm_params(2),
        cost_estimate=cost(150e-6 * 1e15, 80e6),
        name="middle",
    )(
        attended.reshape(4, pieces, n, heads), wo, gain, tokens.reshape(own),
        cot_own.reshape(own), cots, wg, wu, wd,
    )


def end_kernel(count, *refs):
    refs = list(refs)
    take = lambda n: [refs.pop(0) for _ in range(n)]
    loaded, gain_ref, gain_two, parts_in = take(10), *take(3)
    states, dwo = take(count), take(1 if count else 0)
    grad_ref, gain_one_ref, gain_two_ref, out_ref = take(4)
    fulls = take(count + 3 if count else 0)
    dw_out = take(0 if count else 2)
    inputs = take(10)
    dq, dk, dv, wq, wk, wv, attn_in, tokens, grad_one, hid1 = inputs
    terms, cr, xr, out_mine, out_side, out_across, gain_sum, gain_land, dwq, dwkv = take(10)
    send_sem, recv_sem, load_sem, gain_send, gain_recv, in_sem = take(6)
    own, width = tokens.shape
    rows = own // CHUNKS
    sems = (send_sem, recv_sem)
    gain = as_row(gain_ref)
    fetch = [pltpu.make_async_copy(source, target, in_sem.at[i]) for i, (source, target) in enumerate(zip(loaded, inputs))]

    def at(base, k):
        return pl.ds(pl.multiple_of(base + k * rows, rows), rows)

    def term(p, k):
        here = at(p * own, k)
        return dot(dq[here], wq[...], NT) + dot(dk[here], wk[...], NT) + dot(dv[here], wv[...], NT)

    side0 = lambda k: send(terms.at[at(0, k)], cr.at[0, at(0, k)], sems, (0, k), 1)
    side1 = lambda k: send(terms.at[at(own, k)], cr.at[1, at(0, k)], sems, (1, k), 1)
    across = lambda k: send(terms.at[at(2 * own, k)], xr.at[at(0, k)], sems, (2, k), 2)
    out_load = [pltpu.make_async_copy(parts_in.at[:, 2 - 2 * k], out_mine.at[k], load_sem.at[k]) for k in range(2)]
    out_from_side = [send(parts_in.at[:, 3 - 2 * k], out_side.at[k], sems, (3, k), 1) for k in range(2)]
    out_from_across = send(out_mine.at[0], out_across, sems, (3, 2), 2)

    late, early_spreads, late_spreads = [], [], []
    if count:
        land, mine, *own_sems = take(5)
        late.append(Reduce(dwo[0], None, slots(land), slots(mine), 0, RING - 1, *own_sems))
        for part in (dwq, dwkv):
            land, *own_sems = take(3)
            late.append(Reduce(part, None, slots(land), None, 0, RING - 1, *own_sems))
        reduced = [Reduced(state) for state in states]
        spreads = [Spread(r, full, *take(3)) for r, full in zip([*reduced, *late], fulls)]
        early_spreads, late_spreads = spreads[:count], spreads[count:]

    for copy in fetch:
        copy.start()
    if count:
        dp = lax.axis_index("dp")
        flip = lambda bit: {"dp": dp + bit - 2 * bit * lax.rem(lax.div(dp, bit), 2)}
        meet(partner(1), partner(2), ring_peer(0), ring_peer(1), flip(1), flip(2), flip(4))
        for ring in (late[0], *early_spreads):
            ring.start()
        late[0].prefetch()
    else:
        meet(partner(1), partner(2))
    for copy in fetch[:6]:
        copy.wait()

    @pl.loop(0, CHUNKS)
    def _(k):
        terms[at(0, k)] = term(3, k).astype(bf16)
        side0(k).start()

    for k in range(2):
        out_load[k].start()
        out_from_side[k].start()

    @pl.loop(0, CHUNKS)
    def _(k):
        mine = term(2, k)
        side0(k).wait_recv()
        terms[at(2 * own, k)] = (mine + cr[0, at(0, k)].astype(f32)).astype(bf16)
        across(k).start()

    if count:
        late[0].step(0)
        early_spreads[0].step(0)
        early_spreads[1].step(0)

    chunk = dwq.shape[2]
    tall = 4 * chunk
    fetch[6].wait()
    merge_q, merge_k = spread(dwq.shape[3] // HEAD_SIZE), spread(dwkv.shape[1] * dwkv.shape[2] // HEAD_SIZE)

    @pl.loop(0, width // tall)
    def _(k):
        part = attn_in[:, pl.ds(pl.multiple_of(k * tall, LANES), tall)]
        block = dot(dot(part, dq[...], TN).astype(bf16), merge_q, NT).astype(bf16)
        for i in range(4):
            number = k * 4 + i
            dwq[lax.div(number, RING), lax.rem(number, RING)] = block[i * chunk : (i + 1) * chunk]

    short = dwkv.shape[2]
    for half, grads in enumerate((dk, dv)):
        block = dot(merge_k, dot(grads[...], attn_in[...], TN).astype(bf16)).astype(bf16)
        for i in range(RING):
            dwkv[half, i] = block[i * short : (i + 1) * short]

    if count:
        for ring in late[1:]:
            ring.start()
        late[0].step(1)
        early_spreads[2].step(0)
    else:
        stored = [pltpu.make_async_copy(s, t, load_sem.at[2 + i]) for i, (s, t) in enumerate(zip((dwq, dwkv), dw_out))]
        for copy in stored:
            copy.start()
        for copy in stored:
            copy.wait()

    out_load[0].wait()
    out_from_side[0].wait_recv()

    @pl.loop(0, CHUNKS)
    def _(k):
        out_mine[0, k] = (out_mine[0, k].astype(f32) + out_side[0, k].astype(f32)).astype(bf16)

    out_from_across.start()

    def early(numbers, k):
        for a in numbers:
            if a < count:
                early_spreads[a].step(k)

    def onward(turn):
        for a, ring in enumerate(late):
            ahead = 2 if a == 0 else 0
            if turn < RING - 1:
                if turn + ahead < RING - 1:
                    ring.step(turn + ahead)
                if turn == RING - 2:
                    late_spreads[a].start()
            else:
                late_spreads[a].step(turn - (RING - 1))

    @pl.loop(0, CHUNKS)
    def _(k):
        terms[at(own, k)] = term(1, k).astype(bf16)
        side1(k).start()
        grad_ref[at(0, k)] = term(0, k)

    onward(0)
    onward(1)

    def tokens_back():
        for copy in fetch[7:9]:
            copy.wait()
        gain_sum[...] = jnp.zeros_like(gain_sum)
        gain_sum[1:2] = jnp.sum(gain_two[...], axis=0, keepdims=True)

        @pl.loop(0, CHUNKS)
        def _(k):
            side1(k).wait_recv()
            across(k).wait_recv()
            here = at(0, k)
            grad = grad_ref[here] + cr[1, here].astype(f32) + xr[here].astype(f32)
            back, sums = rows_back(grad, tokens[here].astype(f32), gain)
            grad_ref[here] = grad_one[here] + back
            gain_sum[0:1] += jnp.sum(sums, axis=0, keepdims=True)

        gain_copy(0).start()

    def gain_copy(stage):
        to = [partner(1), partner(2)] + ([flip(1), flip(2), flip(4)] if count else [])
        return pltpu.make_async_remote_copy(
            src_ref=gain_sum,
            dst_ref=gain_land.at[stage],
            send_sem=gain_send.at[stage],
            recv_sem=gain_recv.at[stage],
            device_id=to[stage],
            device_id_type=pl.DeviceIdType.MESH,
        )

    def gain_add(stage):
        gain_copy(stage).wait()
        gain_sum[...] += gain_land[stage]

    def output():
        fetch[9].wait()
        out_load[1].wait()
        out_from_side[1].wait_recv()
        out_from_across.wait_recv()

        @pl.loop(0, CHUNKS)
        def _(k):
            total = out_mine[1, k].astype(f32) + out_side[1, k].astype(f32) + out_across[k].astype(f32)
            out_ref[k] = (hid1[k] + total).astype(bf16)

    for turn in range(1, RING - 1):
        if turn == 2:
            tokens_back()
        if turn == 3:
            gain_add(0)
            gain_copy(1).start()
        if turn == 4:
            gain_add(1)
            if count:
                gain_copy(2).start()
            output()
        if turn == 5 and count:
            gain_add(2)
            gain_copy(3).start()
        if turn == 6 and count:
            gain_add(3)
            gain_copy(4).start()
        early((0,), turn)
        if count:
            onward(2 * turn)
        early((1, 2), turn)
        if count:
            onward(2 * turn + 1)
    if count:
        gain_add(4)
    for ring in (*late, *early_spreads, *late_spreads):
        ring.finish()
    for row, ref in enumerate((gain_one_ref, gain_two_ref)):
        for i in range(ref.shape[0]):
            ref[i : i + 1, :] = gain_sum[row : row + 1, i * LANES : (i + 1) * LANES]

    @pl.loop(0, CHUNKS)
    def _(k):
        side0(k).wait_send()
        side1(k).wait_send()
        across(k).wait_send()

    for k in range(2):
        out_from_side[k].wait_send()
    out_from_across.wait_send()


def end(dq, dk, dv, wq, wk, wv, attn_in, tokens, grad_one, hid1, gain, gain_two, parts_in, states, dwo, heads):
    own, width = tokens.shape
    count = len(states)
    sds = jax.ShapeDtypeStruct
    pieces = hid1.shape
    loaded = (dq, dk, dv, wq, wk, wv, attn_in, tokens, grad_one, hid1)
    qkv_shapes = [(2, RING, width // (2 * RING), heads), (2, RING, heads // (2 * RING), width)]
    late = [dwo] if count else []
    ring_shapes = [*[(2, RING, *t.shape[1:]) for t in states], dwo.shape, *qkv_shapes] if count else qkv_shapes
    ring_buffers = []
    if count:
        ring_buffers += ring_scratch(dwo.shape, RING - 1, True)
        for shape in qkv_shapes:
            ring_buffers += ring_scratch(shape, RING - 1, False)
        for _ in ring_shapes:
            ring_buffers += [pltpu.SemaphoreType.DMA((2, RING - 1))] * 2 + [pltpu.SemaphoreType.DMA((2,))]
    stages = 5 if count else 2
    outs = pl.pallas_call(
        functools.partial(end_kernel, count),
        in_specs=[ANY] * 10 + [VMEM] * 2 + [ANY] * (1 + count + len(late)),
        out_specs=[VMEM] * 4 + [ANY] * len(ring_shapes),
        out_shape=[
            sds((own, width), f32),
            sds(gain.shape, f32),
            sds(gain.shape, f32),
            sds(pieces, bf16),
            *[sds(shape, bf16) for shape in ring_shapes],
        ],
        scratch_shapes=[
            *[pltpu.VMEM(t.shape, t.dtype) for t in loaded],
            pltpu.VMEM((3 * own, width), bf16),
            pltpu.VMEM((2, own, width), bf16),
            pltpu.VMEM((own, width), bf16),
            pltpu.VMEM((2, *pieces), bf16),
            pltpu.VMEM((2, *pieces), bf16),
            pltpu.VMEM(pieces, bf16),
            pltpu.VMEM((8, width), f32),
            pltpu.VMEM((stages, 8, width), f32),
            *[pltpu.VMEM(shape, bf16) for shape in qkv_shapes],
            *dma_sems(4, max(CHUNKS, 3)),
            pltpu.SemaphoreType.DMA((4,)),
            *dma_sems(stages),
            pltpu.SemaphoreType.DMA((10,)),
            *ring_buffers,
        ],
        compiler_params=comm_params(3),
        cost_estimate=cost(150e-6 * 1e15, 60e6),
        name="end",
    )(*loaded, gain, gain_two, parts_in, *states, *late)
    return outs[:4], outs[4:]


def body(
    tokens, segments, positions, norm_attn, w_query, key_weight, value_weight, w_out,
    norm_mlp, w_gate, w_up, w_down, cotangent,
):
    seq = segments.shape[0]
    own, width = tokens.shape
    blocks = 4
    heads_q, heads_k = w_query.shape[1], key_weight.shape[1]
    rows_of = lambda t: t.reshape(-1, LANES)
    gain_attn, gain_mlp = rows_of(norm_attn), rows_of(norm_mlp)

    qkv, attn_in, attended, lse, cots, wq, wk, wv, wo, cos, sin, start = front(
        tokens, gain_attn, w_query, key_weight.T, value_weight.T, w_out, rows_of(segments), rows_of(positions),
        cotangent, blocks,
    )
    ringed = lax.axis_size("dp") == RING
    hid1, grad_attended, parts, grad_one, dwd, dwg, dwu, dwo, gain_two, *states = middle(
        attended, wo, tokens, gain_mlp, cotangent, cots, w_gate, w_up, w_down, ringed
    )
    grad_attended = grad_attended.reshape(seq, -1)
    chunks = lambda t: t.reshape(2, RING, t.shape[0] // (2 * RING), t.shape[1])
    early = [chunks(t) for t in (dwd, dwg, dwu)] if ringed else []
    (dq, dk, dv), states = attend_back(
        qkv, attended, grad_attended, lse, start, cos, sin, early, states, blocks
    )
    (grad_tokens, gain_one, gain_two, output), sums = end(
        dq, dk, dv, wq, wk, wv, attn_in.reshape(seq, width), tokens, grad_one.reshape(own, width), hid1, gain_attn,
        gain_two, parts, states, chunks(dwo) if ringed else None, heads_q,
    )
    if not ringed:
        gain_one, gain_two = lax.psum((gain_one, gain_two), "dp")
        sums = [lax.psum(t, "dp") for t in (dwd, dwg, dwu, dwo, *sums)]
    down, gate, up, out, query, both = [t.reshape(-1, t.shape[-1]) for t in sums]
    key, value = both[:heads_k].astype(f32).T, both[heads_k:].astype(f32).T
    query, out, gate, up, down = [t.astype(f32) for t in (query, out, gate, up, down)]
    return (
        output.reshape(own, width), grad_tokens, gain_one.reshape(width), query, key, value, out,
        gain_two.reshape(width), gate, up, down,
    )


def solution(mesh):
    rows, cols, both = P("tensor", None), P(None, "tensor"), P(("dp", "tensor"), None)
    in_specs = (both, P("dp"), P("dp"), P(), cols, cols, cols, rows, P(), cols, cols, rows, both)
    out_specs = (both, both, P(), cols, cols, cols, rows, P(), cols, cols, rows)
    return jax.shard_map(body, mesh=mesh, in_specs=in_specs, out_specs=out_specs, check_vma=False)
```
